32 devices in a mesh: row: 8 (over y, x, core), col: 4 (over z).
Axes of the slice: x: 2, y: 2, z: 4, core: 2. Of those that a mesh axis runs over, the one named last changes fastest.
Arguments:
- layer_input: bfloat16 [8192, 1536], P('row', 'col'), may hold values from -6 to 6
- cotangent: bfloat16 [8192, 1536], P('row', 'col'), may hold values from -8 to 8
- gain_attention: float32 [1536], P('col'), may hold values from 0.5 to 1.5
- gain_mixture: float32 [1536], P('col'), may hold values from 0.5 to 1.5
- w_query: bfloat16 [1536, 1536], P('row', 'col'), may hold values from -0.625 to 0.625
- w_key: bfloat16 [1536, 512], P('row', 'col'), may hold values from -0.625 to 0.625
- w_value: bfloat16 [1536, 512], P('row', 'col'), may hold values from -0.15625 to 0.15625
- w_out: bfloat16 [1536, 1536], P('row', 'col'), may hold values from -1.5 to 1.5
- w_router: bfloat16 [1536, 40], P('row'), may hold values from -0.078125 to 0.078125
- w_gate: bfloat16 [1536, 40, 512], P('row', 'col'), may hold values from -0.15625 to 0.15625
- w_up: bfloat16 [1536, 40, 512], P('row', 'col'), may hold values from -0.15625 to 0.15625
- w_down: bfloat16 [1536, 40, 512], P('row', 'col'), may hold values from -6 to 6
- routes: int32 [8192, 8], P('row'), may hold values from 0 to 39, all different within a row
- priority: int32 [8192, 8], P('row'), may hold values from 0 to 8191, as said below
- ancestry: int32 [8192, 3], P('row'), may hold values from 0 to 12, as said below
Outputs:
- layer_output: bfloat16 [8192, 1536], P('row', 'col')
- input_grad: float32 [8192, 1536], P('row', 'col')
- gain_attention_grad: float32 [1536], P('col')
- gain_mixture_grad: float32 [1536], P('col')
- w_query_grad: float32 [1536, 1536], P('row', 'col')
- w_key_grad: float32 [1536, 512], P('row', 'col')
- w_value_grad: float32 [1536, 512], P('row', 'col')
- w_out_grad: float32 [1536, 1536], P('row', 'col')
- w_router_grad: float32 [1536, 40], P('row')
- w_gate_grad: float32 [1536, 40, 512], P('row', 'col')
- w_up_grad: float32 [1536, 40, 512], P('row', 'col')
- w_down_grad: float32 [1536, 40, 512], P('row', 'col')
The draws below stay inside these ranges and needn't reach their ends.
Inputs may be any that keep to these rules, and one draw needn't show every extreme that they name: `routes`: each token names 8 different experts. `priority`: within each aligned block of 1024 tokens the 8192 entries hold each of 0 to 8191 once. `ancestry`: the 13 segments are contiguous runs of tokens in depth-first order: the trunk (segment 0, its own parent), 4 branches, and 2 leaves under each branch; the trunk holds 3276 tokens. Columns 1 and 2 give the parent's and grandparent's segment.
All inputs are finite; a program needn't handle non-finite values.
Results may differ from the reference program's by a relative error of at most 0.02.
Values may be sent and summed in bfloat16 or wider, within the bound.
No kernel may reach another device: no remote copies, remote signals or barrier semaphores. Data moves between devices by JAX's collectives and lax.ppermute only.
A program may use at most 256 MiB of HBM per device.

```python
import math
import jax
import jax.numpy as jnp
from jax import lax

D = 1536
QH = 24
KVH = 8
HD = 64
H = 512
EXPERTS = 40
TOPK = 8
SEGS = 13
TOK_DEV = 1024
TOKENS = 8192
CAP = 230


branch_order = [0, 1, 5, 6, 2, 7, 8, 3, 9, 10, 4, 11, 12]


parent_table = [0, 0, 0, 0, 0, 1, 1, 2, 2, 3, 3, 4, 4]


def draw_priority(key, part):
    groups = TOKENS // TOK_DEV
    pairs = TOK_DEV * TOPK
    keys_all = jax.random.split(key, groups)

    def one_order(single_key):
        return jax.random.permutation(single_key, pairs).astype(jnp.int32)
    orders = jax.vmap(one_order)(keys_all)
    return orders.reshape(TOKENS, TOPK).astype(jnp.int32)


def draw_ancestry(key, part):
    trunk = 2 * TOKENS // 5
    remainder = TOKENS - trunk
    shares = jax.random.randint(key, (12,), 2, 7).astype(jnp.int32)
    running = jnp.cumsum(shares, dtype=jnp.int32)
    bounds = trunk + running * remainder // running[11]
    index = jnp.arange(TOKENS, dtype=jnp.int32)
    order = (index >= trunk).astype(jnp.int32) + jnp.sum((index[:, None] >= bounds[None, :]).astype(jnp.int32), axis=1, dtype=jnp.int32)
    order = jnp.minimum(order, 12)
    own_segment = jnp.array(branch_order, dtype=jnp.int32)[order]
    parents = jnp.array(parent_table, dtype=jnp.int32)
    parent = parents[own_segment]
    grandparent = parents[parent]
    return jnp.stack([own_segment, parent, grandparent], axis=1).astype(jnp.int32)


def raised(values, own_key, source, target, shards_of, factor):
    owner, partner = [(jnp.arange(values.shape[dim]) // (values.shape[dim] // shards_of)).reshape([-1 if axis == dim else 1 for axis in range(values.ndim)]) for dim in (source, target)]
    chosen = jax.random.permutation(own_key, shards_of)[partner]
    strong = (owner == chosen) | (owner == (partner + shards_of // 2) % shards_of)
    return jnp.where(strong, factor * values, values)


def block_scale(stream_key, shape, pieces, smallest, high):
    def one(dim, shards_of):
        draws = jax.random.uniform(jax.random.fold_in(jax.random.fold_in(stream_key, 6), dim), (shards_of,), jnp.float32, smallest / len(pieces), high / len(pieces))
        return jnp.repeat(jnp.exp(draws), shape[dim] // shards_of).reshape((-1,) + (1,) * (len(shape) - dim - 1))

    factor_of = one(*pieces[0])
    for cut in pieces[1:]:
        factor_of = factor_of * one(*cut)
    return factor_of


def picks_of(stream_key, rows, amount, top, lift):
    ranking = jax.random.permutation(jax.random.fold_in(stream_key, 1), amount)
    pull = ranking
    for power in range(3):
        pull = pull * pull // amount
    pull = pull * lift // amount
    lots = jax.random.randint(jax.random.fold_in(stream_key, 2), (rows, amount), 0, 4096) + pull
    holders = jax.random.permutation(jax.random.fold_in(stream_key, 3), rows)[jnp.arange(amount) % rows]
    lots = jnp.where(jnp.arange(rows)[:, None] == holders[None, :], 1 << 14, lots)
    score = lots * amount + jnp.arange(amount)
    return lax.top_k(score.astype(jnp.int32), top)[1].astype(jnp.int32)


def gaussian(rng, dims, spread, reach, pieces=(), held_as=jnp.bfloat16):
    factor_of = block_scale(rng, dims, pieces, -0.22, 0.18) if pieces else 1.0
    entries = jax.random.normal(rng, dims, jnp.float32) * spread * factor_of
    return jnp.minimum(jnp.maximum(entries, -reach), reach).astype(held_as)


def gaussian_with(own_key, extent, scale, reach, cuts, heavy, held_as=jnp.bfloat16):
    values = scale * jax.random.normal(own_key, extent, jnp.float32)
    if cuts:
        values = values * block_scale(own_key, extent, cuts, -0.22, 0.18)
    return jnp.clip(raised(values, jax.random.fold_in(own_key, 3), *heavy), -reach, reach).astype(held_as)


def setup_inputs(seed: int = 0) -> dict:
    key_list = jax.random.split(jax.random.key(seed), 16)
    return {
        "layer_input": gaussian(key_list[0], (TOKENS, D), 1.0, 6.0, ((0, 8), (1, 4))),
        "cotangent": gaussian_with(key_list[1], (TOKENS, D), 1.0, 8.0, ((0, 8), (1, 4)), (0, 1, 8, 2.0)),
        "gain_attention": jnp.clip(1.0 + 0.1 * jax.random.normal(key_list[2], (D,), jnp.float32), 0.5, 1.5),
        "gain_mixture": jnp.clip(1.0 + 0.1 * jax.random.normal(key_list[3], (D,), jnp.float32), 0.5, 1.5),
        "w_query": gaussian(key_list[4], (D, QH * HD), (D // 16) ** -0.5, 0.625, ((0, 8), (1, 4))),
        "w_key": gaussian(key_list[5], (D, KVH * HD), (D // 16) ** -0.5, 0.625, ((0, 8), (1, 4))),
        "w_value": gaussian(key_list[6], (D, KVH * HD), D ** -0.5, 0.15625, ((0, 8), (1, 4))),
        "w_out": gaussian(key_list[7], (D, QH * HD), 0.25, 1.5, ((0, 8), (1, 4))),
        "w_router": gaussian(key_list[8], (D, EXPERTS), (4 * D) ** -0.5, 0.078125, ((0, 8),)),
        "w_gate": gaussian(key_list[9], (D, EXPERTS, H), D ** -0.5, 0.15625, ((0, 8), (1, 4))),
        "w_up": gaussian(key_list[10], (D, EXPERTS, H), D ** -0.5, 0.15625, ((0, 8), (1, 4))),
        "w_down": gaussian(key_list[11], (D, EXPERTS, H), 1.0, 6.0, ((0, 8), (1, 4))),
        "routes": picks_of(key_list[12], TOKENS, EXPERTS, TOPK, 1638),
        "priority": draw_priority(jax.random.fold_in(key_list[15], 71), 0),
        "ancestry": draw_ancestry(jax.random.fold_in(key_list[15], 71), 0),
    }


@jax.custom_vjp
def low(v):
    return lax.optimization_barrier(v.astype(jnp.bfloat16)).astype(jnp.float32)

@jax.custom_vjp
def low_back(v):
    return v

def low_keep(v):
    return (low(v), None)

def low_pass(kept, grad):
    return (grad,)

def back_keep(v):
    return (v, None)

def back_low(kept, grad):
    return (low(grad),)
low.defvjp(low_keep, low_pass)
low_back.defvjp(back_keep, back_low)
epsilon = 1e-06
branch_scale = 0.22
score_scale = 0.015625
rope_base = 10000.0
masked_score = -1e+30
highest = lax.Precision.HIGHEST

def product(left, right):
    return jnp.dot(left, right, precision=highest, preferred_element_type=jnp.float32)

def inverse_scale(values):
    return lax.rsqrt(lax.optimization_barrier(jnp.mean(values * values, axis=-1, keepdims=True)) + epsilon)

def tree_positions(ancestry):
    segment_ids = jnp.arange(SEGS, dtype=jnp.int32)
    member = (ancestry[:, 0:1] == segment_ids[None, :]).astype(jnp.int32)
    before = jnp.cumsum(member, axis=0, dtype=jnp.int32) - member
    on_path = ((ancestry[:, 0:1] == segment_ids[None, :]) | (ancestry[:, 1:2] == segment_ids[None, :]) | (ancestry[:, 2:3] == segment_ids[None, :])).astype(jnp.int32)
    return lax.optimization_barrier(jnp.sum(on_path * before, axis=1, dtype=jnp.int32))

def rope_tables(position):
    half = HD // 2
    freq = rope_base ** (-(jnp.arange(half, dtype=jnp.float32) * 2.0) / HD)
    angle = position.astype(jnp.float32)[:, None] * freq[None, :]
    return (jnp.cos(angle), jnp.sin(angle))

def rotate(values, cosine, sine):
    half = HD // 2
    first_half = values[..., :half]
    second_half = values[..., half:]
    cos_b = cosine[:, None, :]
    sin_b = sine[:, None, :]
    return jnp.concatenate([first_half * cos_b - second_half * sin_b, second_half * cos_b + first_half * sin_b], axis=-1)

def slot_tables(group_routes, group_priority, first_expert, expert_count):
    pairs = group_routes.shape[0] * TOPK
    flat_routes = group_routes.reshape(pairs)
    flat_priority = group_priority.reshape(pairs)
    numbers = jnp.arange(pairs, dtype=jnp.int32)
    order = jnp.zeros((pairs,), jnp.int32).at[flat_priority].set(numbers)
    ordered = flat_routes[order]
    member = (ordered[:, None] == jnp.arange(EXPERTS, dtype=jnp.int32)[None, :]).astype(jnp.int32)
    running = jnp.cumsum(member, axis=0, dtype=jnp.int32)
    rank_ordered = lax.optimization_barrier(jnp.sum(running * member, axis=1, dtype=jnp.int32)) - 1
    rank = rank_ordered[flat_priority]
    local = flat_routes - first_expert
    inside = (local >= 0) & (local < expert_count) & (rank < CAP)
    target = jnp.where(inside, local * CAP + rank, expert_count * CAP).astype(jnp.int32)
    slot_pair = jnp.zeros((expert_count * CAP + 1,), jnp.int32).at[target].set(numbers)[:expert_count * CAP]
    slot_live = jnp.zeros((expert_count * CAP + 1,), jnp.float32).at[target].set(1.0)[:expert_count * CAP]
    return (slot_pair, slot_live)

def attention(query, keys, value, ancestry):
    count = query.shape[0]
    group = QH // KVH
    query_block = math.gcd(count, 1024)
    blocks = count // query_block
    own_segment = ancestry[:, 0]
    index = jnp.arange(count, dtype=jnp.int32)

    def per_head(head_args):
        head_query, head_key, head_value = head_args

        @jax.checkpoint
        def per_block(block_args):
            block_query, block_ancestry, block_index = block_args
            scores = score_scale * jnp.einsum('qgd,kd->gqk', block_query, head_key, precision=highest)
            scores = low_back(scores)
            on_path = (own_segment[None, :] == block_ancestry[:, 0:1]) | (own_segment[None, :] == block_ancestry[:, 1:2]) | (own_segment[None, :] == block_ancestry[:, 2:3])
            allowed = on_path & (block_index[:, None] >= index[None, :])
            scores = jnp.where(allowed[None], scores, masked_score)
            weights = jax.nn.softmax(scores, axis=-1)
            return jnp.einsum('gqk,kd->qgd', weights, head_value, precision=highest)
        result = lax.map(per_block, (head_query.reshape(blocks, query_block, group, HD), ancestry.reshape(blocks, query_block, 3), index.reshape(blocks, query_block)))
        return result.reshape(count, group, HD)
    heads = lax.map(per_head, (query.reshape(count, KVH, group, HD).transpose(1, 0, 2, 3), keys.transpose(1, 0, 2), value.transpose(1, 0, 2)))
    return heads.transpose(1, 0, 2, 3).reshape(count, QH * HD)

def reference(layer_input, cotangent, gain_attention, gain_mixture, w_query, w_key, w_value, w_out, w_router, w_gate, w_up, w_down, routes, priority, ancestry):
    count = layer_input.shape[0]
    groups = count // TOK_DEV
    position = tree_positions(ancestry)
    cosine, sine = rope_tables(position)

    def group_slots(group_routes, group_priority):
        return slot_tables(group_routes, group_priority, 0, EXPERTS)
    slot_pair, slot_live = jax.vmap(group_slots)(routes.reshape(groups, TOK_DEV, TOPK), priority.reshape(groups, TOK_DEV, TOPK))
    offset = jnp.arange(groups, dtype=jnp.int32)[:, None]
    slot_token = slot_pair // TOPK + offset * TOK_DEV
    slot_index = slot_pair + offset * (TOK_DEV * TOPK)
    chosen = (routes[:, :, None] == jnp.arange(EXPERTS, dtype=jnp.int32)[None, None, :]).astype(jnp.float32)

    def forward(x_input, gain_one, gain_two, query_matrix, key_matrix, value_matrix, out_matrix, router_matrix, gate_matrix, up_matrix, down_matrix):
        h_one = low(x_input * inverse_scale(x_input) * gain_one)
        query_pre = low_back(product(h_one, query_matrix))
        key_pre = low_back(product(h_one, key_matrix))
        value = low(low_back(product(h_one, value_matrix)))
        query = low(rotate(query_pre.reshape(count, QH, HD), cosine, sine))
        keys = low(rotate(key_pre.reshape(count, KVH, HD), cosine, sine))
        mixed = attention(query, keys, value.reshape(count, KVH, HD), ancestry)
        mixed = low(low_back(mixed))
        branch = low_back(product(mixed, out_matrix.T))
        x_middle = x_input + branch_scale * branch
        h_two = low(x_middle * inverse_scale(x_middle) * gain_two)
        logits = low_back(product(h_two, router_matrix))
        picked = jnp.einsum('tke,te->tk', chosen, logits, precision=highest)
        gates = jax.nn.softmax(picked, axis=-1)
        slot_weight = gates.reshape(-1)[slot_index] * slot_live

        @jax.checkpoint
        def per_group(group_args):
            tokens_group, weight_group = group_args
            inputs = h_two[tokens_group].reshape(EXPERTS, CAP, D)
            gate_pre = low_back(jnp.einsum('ecd,deh->ech', inputs, gate_matrix, precision=highest))
            up_pre = low_back(jnp.einsum('ecd,deh->ech', inputs, up_matrix, precision=highest))
            active = low(jax.nn.silu(gate_pre) * up_pre)
            expert_out = low_back(jnp.einsum('ech,deh->ecd', active, down_matrix, precision=highest))
            return expert_out.reshape(EXPERTS * CAP, D) * weight_group[:, None]
        weighted = lax.map(per_group, (slot_token, slot_weight))
        expert_mix = low_back(jnp.zeros((count, D), jnp.float32).at[slot_token.reshape(-1)].add(weighted.reshape(-1, D)))
        return x_middle + branch_scale * expert_mix
    floats = (layer_input.astype(jnp.float32), gain_attention, gain_mixture, w_query.astype(jnp.float32), w_key.astype(jnp.float32), w_value.astype(jnp.float32), w_out.astype(jnp.float32), w_router.astype(jnp.float32), w_gate.astype(jnp.float32), w_up.astype(jnp.float32), w_down.astype(jnp.float32))
    result, pullback = jax.vjp(forward, *floats)
    grads = pullback(cotangent.astype(jnp.float32))
    return (result.astype(jnp.bfloat16), grads[0], grads[1], grads[2], grads[3], grads[4], grads[5], grads[6], grads[7], grads[8], grads[9], grads[10])
```

```python
import functools

import jax
import jax.numpy as jnp
from jax import lax
from jax.experimental import pallas as pl
from jax.experimental.pallas import tpu as pltpu
from jax.sharding import Mesh
from jax.sharding import PartitionSpec as P

D = 1536
HD = 64
H = 512
KVH = 8
EXPERTS = 40
TOPK = 8
SEGS = 13
CAP = 230
SLOTS = 256

epsilon = 1e-06
branch_scale = 0.22
score_scale = 0.015625
rope_base = 10000.0
masked_score = -1e30

bf16 = jnp.bfloat16
f32 = jnp.float32
i32 = jnp.int32

QUERY_BLOCK = 256
KEY_BLOCK = 512
VMEM_LIMIT = 60 * 1024 * 1024


def dot(left, right):
    return jnp.dot(left, right, preferred_element_type=f32)


def dot_dims(left, right, left_dim, right_dim):
    return lax.dot_general(
        left, right, (((left_dim,), (right_dim,)), ((), ())), preferred_element_type=f32
    )


def swap(values, axis, bit):
    size = lax.axis_size(axis)
    return lax.ppermute(values, axis, [(i, i ^ bit) for i in range(size)])


def swap_core(values):
    return swap(values, "core", 1)


def chip_bits(chips):
    return [1 << b for b in range(chips.bit_length() - 1)]


def chip_gather(values, chips, descending):
    bits = chip_bits(chips)
    blocks = {0: values}
    for bit in reversed(bits) if descending else bits:
        for j in sorted(blocks):
            blocks[j ^ bit] = swap(blocks[j], "chip", bit)
    return [blocks[j] for j in range(chips)]


def chip_reduce(parts, chips, descending):
    blocks = dict(enumerate(parts))
    bits = chip_bits(chips)
    for bit in reversed(bits) if descending else bits:
        for j in sorted(blocks):
            if j & bit:
                continue
            taken = swap(blocks.pop(j ^ bit), "chip", bit)
            blocks[j] = (blocks[j].astype(f32) + taken.astype(f32)).astype(blocks[j].dtype)
    return blocks[0]


def own_and_other(values, core, share):
    if share == 1:
        return values[0], None
    mine = lax.dynamic_index_in_dim(values, core, 0, keepdims=False)
    other = lax.dynamic_index_in_dim(values, 1 - core, 0, keepdims=False)
    return mine, other


def in_core_order(mine, other, core):
    if other is None:
        return mine[None]
    first = core == 0
    return jnp.stack([jnp.where(first, mine, other), jnp.where(first, other, mine)])


def load_keys(offsets, parts, kv_rows, kv_columns):
    for n, part in enumerate(parts):
        count = part.shape[1]
        start = pl.multiple_of(offsets[n], count)
        kv_columns[:, pl.ds(start, count)] = part[...]
        kv_rows[pl.ds(start, count), :] = part[...].astype(f32).T.astype(bf16)


def visible(path_bits, key_bits, query_start, key_start, shape):
    keys = key_start + lax.broadcasted_iota(i32, shape, 0)
    queries = query_start + lax.broadcasted_iota(i32, shape, 1)
    return ((key_bits & path_bits) != 0) & (keys <= queries)


def attend_forward_kernel(
    offsets, starts, codes, query, path, key_bits, *rest, parts, key_blocks, key_block
):
    kv_parts = rest[:parts]
    out, log_total, kv_rows, kv_columns, padded, peak, total, mixed = rest[parts:]
    step = pl.program_id(0)
    heads, width, count = query.shape[1:]

    @pl.when(step == 0)
    def _():
        load_keys(offsets, kv_parts, kv_rows, kv_columns)
        padded[...] = jnp.zeros_like(padded)

    padded[:, :width, :] = query[0]
    peak[...] = jnp.full_like(peak, masked_score)
    total[...] = jnp.zeros_like(total)
    mixed[...] = jnp.zeros_like(mixed)

    def block(number, masked):
        start = pl.multiple_of(number * key_block, key_block)
        keys = kv_rows[pl.ds(start, key_block), :]
        values = kv_columns[width:, pl.ds(start, key_block)]
        if masked:
            allowed = visible(
                path[0], key_bits[pl.ds(start, key_block), :], starts[step], start, (key_block, count)
            )
        for head in range(heads):
            scores = dot(keys, padded[head])
            if masked:
                scores = jnp.where(allowed, scores, masked_score)
            old = peak[head]
            new = jnp.maximum(old, jnp.max(scores, axis=0, keepdims=True))
            weights = jnp.exp(scores - new)
            factor = jnp.exp(old - new)
            peak[head] = new
            total[head] = total[head] * factor + jnp.sum(weights, axis=0, keepdims=True)
            mixed[head] = mixed[head] * factor + dot(values, weights.astype(bf16))

    @pl.loop(0, key_blocks)
    def _(number):
        code = codes[step * key_blocks + number]

        @pl.when(code == 1)
        def _():
            block(number, True)

        @pl.when(code == 2)
        def _():
            block(number, False)

    for head in range(heads):
        out[0, head] = mixed[head] / total[head]
        log_total[0, head] = peak[head] + jnp.log(total[head])


def attend_backward_kernel(
    offsets,
    starts,
    codes,
    query,
    mixed_grad,
    mixed,
    log_total,
    path,
    key_bits,
    *rest,
    parts,
    key_blocks,
    key_block,
):
    kv_parts = rest[:parts]
    query_grad = rest[parts]
    grad_parts = rest[parts + 1 : 2 * parts + 1]
    (kv_rows, kv_columns, padded, padded_grad, query_rows, grad_rows, delta, query_sum, kv_sum) = rest[
        2 * parts + 1 :
    ]
    step = pl.program_id(0)
    heads, width, count = query.shape[1:]

    @pl.when(step == 0)
    def _():
        load_keys(offsets, kv_parts, kv_rows, kv_columns)
        padded[...] = jnp.zeros_like(padded)
        padded_grad[...] = jnp.zeros_like(padded_grad)
        kv_sum[...] = jnp.zeros_like(kv_sum)

    padded[:, :width, :] = query[0]
    padded_grad[:, width:, :] = mixed_grad[0]
    for head in range(heads):
        delta[head] = jnp.sum(mixed_grad[0, head].astype(f32) * mixed[0, head], axis=0, keepdims=True)
        query_rows[head] = padded[head].astype(f32).T.astype(bf16)
        grad_rows[head] = padded_grad[head].astype(f32).T.astype(bf16)
    query_sum[...] = jnp.zeros_like(query_sum)

    def block(number, masked):
        start = pl.multiple_of(number * key_block, key_block)
        keys = kv_rows[pl.ds(start, key_block), :]
        key_columns = kv_columns[:width, pl.ds(start, key_block)]
        if masked:
            allowed = visible(
                path[0], key_bits[pl.ds(start, key_block), :], starts[step], start, (key_block, count)
            )
        update = kv_sum[pl.ds(start, key_block), :]
        for head in range(heads):
            scores = dot(keys, padded[head])
            if masked:
                scores = jnp.where(allowed, scores, masked_score)
            weights = jnp.exp(scores - log_total[0, head])
            weight_grad = dot(keys, padded_grad[head])
            score_grad = (weights * (weight_grad - delta[head])).astype(bf16)
            update += dot(score_grad, query_rows[head]) + dot(weights.astype(bf16), grad_rows[head])
            query_sum[head] += dot(key_columns, score_grad)
        kv_sum[pl.ds(start, key_block), :] = update

    @pl.loop(0, key_blocks)
    def _(number):
        code = codes[step * key_blocks + number]

        @pl.when(code == 1)
        def _():
            block(number, True)

        @pl.when(code == 2)
        def _():
            block(number, False)

    query_grad[0] = score_scale * query_sum[...]

    @pl.when(step == pl.num_programs(0) - 1)
    def _():
        for n, part in enumerate(grad_parts):
            rows = part.shape[0]
            part[...] = kv_sum[pl.ds(pl.multiple_of(offsets[n], rows), rows), :].astype(part.dtype)


def whole(shape):
    return pl.BlockSpec(shape, lambda *_: (0,) * len(shape), pipeline_mode=pl.Buffered(1))


def attention_specs(groups, heads, rows, block):
    per_group = rows // block

    def four(step, *_):
        return (step // per_group, 0, 0, step % per_group)

    def three(step, *_):
        return (step // per_group, 0, step % per_group)

    return (
        pl.BlockSpec((1, heads, HD, block), four),
        pl.BlockSpec((1, heads, 1, block), four),
        pl.BlockSpec((1, 1, block), three),
    )


def attend_forward(offsets, starts, codes, query, path, key_bits, kv_parts):
    groups, heads, _, rows = query.shape
    block = min(QUERY_BLOCK, rows)
    tokens = key_bits.shape[0]
    key_block = min(KEY_BLOCK, tokens)
    wide, row, flat = attention_specs(groups, heads, rows, block)
    kernel = functools.partial(
        attend_forward_kernel,
        parts=len(kv_parts),
        key_blocks=tokens // key_block,
        key_block=key_block,
    )
    pairs = groups * heads * rows * tokens // 2
    return pl.pallas_call(
        kernel,
        name="attend_forward",
        grid_spec=pltpu.PrefetchScalarGridSpec(
            num_scalar_prefetch=3,
            grid=(groups * rows // block,),
            in_specs=[wide, flat, whole(key_bits.shape)] + [whole(p.shape) for p in kv_parts],
            out_specs=[wide, row],
            scratch_shapes=[
                pltpu.VMEM((tokens, 2 * HD), bf16),
                pltpu.VMEM((2 * HD, tokens), bf16),
                pltpu.VMEM((heads, 2 * HD, block), bf16),
                pltpu.VMEM((heads, 1, block), f32),
                pltpu.VMEM((heads, 1, block), f32),
                pltpu.VMEM((heads, HD, block), f32),
            ],
        ),
        out_shape=[
            jax.ShapeDtypeStruct(query.shape, f32),
            jax.ShapeDtypeStruct((groups, heads, 1, rows), f32),
        ],
        compiler_params=pltpu.CompilerParams(
            dimension_semantics=("arbitrary",), vmem_limit_bytes=VMEM_LIMIT
        ),
        cost_estimate=pl.CostEstimate(
            flops=4 * pairs * HD, transcendentals=pairs, bytes_accessed=8 * 1024 * 1024
        ),
    )(offsets, starts, codes, query, path, key_bits, *kv_parts)


def attend_backward(offsets, starts, codes, query, mixed_grad, mixed, log_total, path, key_bits, kv_parts):
    groups, heads, _, rows = query.shape
    block = min(QUERY_BLOCK, rows)
    tokens = key_bits.shape[0]
    key_block = min(KEY_BLOCK, tokens)
    part_rows = kv_parts[0].shape[1]
    wide, row, flat = attention_specs(groups, heads, rows, block)
    kernel = functools.partial(
        attend_backward_kernel,
        parts=len(kv_parts),
        key_blocks=tokens // key_block,
        key_block=key_block,
    )
    pairs = groups * heads * rows * tokens // 2
    grad_shape = (part_rows, 2 * HD)
    outs = pl.pallas_call(
        kernel,
        name="attend_backward",
        grid_spec=pltpu.PrefetchScalarGridSpec(
            num_scalar_prefetch=3,
            grid=(groups * rows // block,),
            in_specs=[wide, wide, wide, row, flat, whole(key_bits.shape)]
            + [whole(p.shape) for p in kv_parts],
            out_specs=[wide] + [whole(grad_shape) for _ in kv_parts],
            scratch_shapes=[
                pltpu.VMEM((tokens, 2 * HD), bf16),
                pltpu.VMEM((2 * HD, tokens), bf16),
                pltpu.VMEM((heads, 2 * HD, block), bf16),
                pltpu.VMEM((heads, 2 * HD, block), bf16),
                pltpu.VMEM((heads, block, 2 * HD), bf16),
                pltpu.VMEM((heads, block, 2 * HD), bf16),
                pltpu.VMEM((heads, 1, block), f32),
                pltpu.VMEM((heads, HD, block), f32),
                pltpu.VMEM((tokens, 2 * HD), f32),
            ],
        ),
        out_shape=[jax.ShapeDtypeStruct(query.shape, f32)]
        + [jax.ShapeDtypeStruct(grad_shape, bf16) for _ in kv_parts],
        compiler_params=pltpu.CompilerParams(
            dimension_semantics=("arbitrary",), vmem_limit_bytes=VMEM_LIMIT
        ),
        cost_estimate=pl.CostEstimate(
            flops=10 * pairs * HD, transcendentals=pairs, bytes_accessed=16 * 1024 * 1024
        ),
    )(offsets, starts, codes, query, mixed_grad, mixed, log_total, path, key_bits, *kv_parts)
    return outs[0], outs[1:]


def rank_kernel(first, route_rows, priority_rows, route_columns, priority_columns, out, *, experts):
    rows = route_rows.shape[2]
    never = rows * TOPK
    for e in range(experts):
        expert = first[0] + e
        along = jnp.min(
            jnp.where(route_rows[0] == expert, priority_rows[0], never), axis=0, keepdims=True
        )
        down = jnp.min(
            jnp.where(route_columns[0] == expert, priority_columns[0], never), axis=1, keepdims=True
        )
        count = jnp.zeros((8, rows), i32)
        for begin in range(0, rows, 8):
            count += (down[begin : begin + 8] < along).astype(i32)
        rank = jnp.sum(count, axis=0, keepdims=True)
        out[0, e : e + 1, :] = jnp.where((along < never) & (rank < CAP), rank, -1)


def slot_ranks(first, routes, priority, experts):
    groups, rows, _ = routes.shape
    tall = pl.BlockSpec((1, rows, TOPK), lambda g, *_: (g, 0, 0))
    flat = pl.BlockSpec((1, TOPK, rows), lambda g, *_: (g, 0, 0))
    padded = -(-experts // 8) * 8
    return pl.pallas_call(
        functools.partial(rank_kernel, experts=experts),
        name="slot_ranks",
        grid_spec=pltpu.PrefetchScalarGridSpec(
            num_scalar_prefetch=1,
            grid=(groups,),
            in_specs=[flat, flat, tall, tall],
            out_specs=pl.BlockSpec((1, padded, rows), lambda g, *_: (g, 0, 0)),
        ),
        out_shape=jax.ShapeDtypeStruct((groups, padded, rows), i32),
        compiler_params=pltpu.CompilerParams(vmem_limit_bytes=VMEM_LIMIT),
    )(
        first.reshape(1),
        routes.transpose(0, 2, 1),
        priority.transpose(0, 2, 1),
        routes,
        priority,
    )[:, :experts]


def expert_kernel(offsets, tokens, grads, ranks, gates, *rest, parts, groups):
    weights = rest[:parts]
    weighted_out, token_grad, inputs, slot_grads, hidden, pair_grads, matrices = rest[parts:]
    rows = tokens.shape[1]
    for n, part in enumerate(weights):
        count = part.shape[2]
        start = pl.multiple_of(offsets[n], count)
        for m in range(3):
            matrices[m, pl.ds(start, count), :] = part[0, m]
    slot = lax.broadcasted_iota(i32, (SLOTS, rows), 0)
    for g in range(groups):
        inside = slot == ranks[0, g]
        pick = inside.astype(bf16)
        weight = jnp.sum(jnp.where(inside, gates[0, g], 0.0), axis=1, keepdims=True)
        picked = dot(pick, tokens[g]).astype(bf16)
        inputs[0, g * SLOTS : (g + 1) * SLOTS, :] = picked
        gate_pre = dot(picked, matrices[0])
        up_pre = dot(picked, matrices[1])
        sigma = jax.nn.sigmoid(gate_pre)
        silu = gate_pre * sigma
        active = (silu * up_pre).astype(bf16)
        out = dot_dims(active, matrices[2], 1, 1)
        weighted_out[g, 0] = (out * weight).astype(bf16)
        upstream = dot(pick, grads[g])
        pair = jnp.sum(upstream * out, axis=1, keepdims=True)
        pair_grads[0, g] = jnp.sum(jnp.where(inside, pair, 0.0), axis=0, keepdims=True)
        slot_grad = (weight * upstream).astype(bf16)
        slot_grads[0, g * SLOTS : (g + 1) * SLOTS, :] = slot_grad
        act_grad = dot(slot_grad, matrices[2])
        gate_grad = (act_grad * up_pre * sigma * (1.0 + gate_pre * (1.0 - sigma))).astype(bf16)
        up_grad = (act_grad * silu).astype(bf16)
        hidden[0, 0, g * SLOTS : (g + 1) * SLOTS, :] = gate_grad
        hidden[0, 1, g * SLOTS : (g + 1) * SLOTS, :] = up_grad
        hidden[0, 2, g * SLOTS : (g + 1) * SLOTS, :] = active
        token_grad[g, 0] = (
            dot_dims(gate_grad, matrices[0], 1, 1) + dot_dims(up_grad, matrices[1], 1, 1)
        ).astype(bf16)


def run_experts(offsets, tokens, grads, ranks, gates, weight_parts):
    groups, rows, _ = tokens.shape
    experts, _, part_rows, _ = weight_parts[0].shape
    slots = groups * SLOTS
    per_expert = pl.BlockSpec((1, groups, 1, rows), lambda e, *_: (e, 0, 0, 0))
    by_group = pl.BlockSpec((groups, 1, SLOTS, D), lambda e, *_: (0, e, 0, 0))
    stash = pl.BlockSpec((1, slots, D), lambda e, *_: (e, 0, 0))
    flops = experts * slots * 2 * D * (2 * rows + 6 * H)
    return pl.pallas_call(
        functools.partial(expert_kernel, parts=len(weight_parts), groups=groups),
        name="experts",
        grid_spec=pltpu.PrefetchScalarGridSpec(
            num_scalar_prefetch=1,
            grid=(experts,),
            in_specs=[whole(tokens.shape), whole(grads.shape), per_expert, per_expert]
            + [pl.BlockSpec((1, 3, part_rows, H), lambda e, *_: (e, 0, 0, 0)) for _ in weight_parts],
            out_specs=[
                by_group,
                by_group,
                stash,
                stash,
                pl.BlockSpec((1, 3, slots, H), lambda e, *_: (e, 0, 0, 0)),
                per_expert,
            ],
            scratch_shapes=[pltpu.VMEM((3, D, H), bf16)],
        ),
        out_shape=[
            jax.ShapeDtypeStruct((groups, experts, SLOTS, D), bf16),
            jax.ShapeDtypeStruct((groups, experts, SLOTS, D), bf16),
            jax.ShapeDtypeStruct((experts, slots, D), bf16),
            jax.ShapeDtypeStruct((experts, slots, D), bf16),
            jax.ShapeDtypeStruct((experts, 3, slots, H), bf16),
            jax.ShapeDtypeStruct((experts, groups, 1, rows), f32),
        ],
        compiler_params=pltpu.CompilerParams(
            dimension_semantics=("arbitrary",), vmem_limit_bytes=VMEM_LIMIT
        ),
        cost_estimate=pl.CostEstimate(
            flops=flops, transcendentals=experts * slots * H, bytes_accessed=64 * 1024 * 1024
        ),
    )(offsets, tokens, grads, ranks, gates, *weight_parts)


def expert_grad_kernel(offsets, inputs, slot_grads, hidden, *rest, parts):
    outs = rest[:parts]
    total = rest[parts]
    for m in range(3):
        left = inputs if m < 2 else slot_grads
        total[...] = dot_dims(left[0], hidden[0, m], 0, 0)
        for n, out in enumerate(outs):
            count = out.shape[2]
            out[0, m] = total[pl.ds(pl.multiple_of(offsets[n], count), count), :].astype(bf16)


def expert_grads(offsets, inputs, slot_grads, hidden, parts, part_rows):
    experts, slots, _ = inputs.shape
    stash = pl.BlockSpec((1, slots, D), lambda e, *_: (e, 0, 0))
    return pl.pallas_call(
        functools.partial(expert_grad_kernel, parts=parts),
        name="expert_grads",
        grid_spec=pltpu.PrefetchScalarGridSpec(
            num_scalar_prefetch=1,
            grid=(experts,),
            in_specs=[stash, stash, pl.BlockSpec((1, 3, slots, H), lambda e, *_: (e, 0, 0, 0))],
            out_specs=[
                pl.BlockSpec((1, 3, part_rows, H), lambda e, *_: (e, 0, 0, 0)) for _ in range(parts)
            ],
            scratch_shapes=[pltpu.VMEM((D, H), f32)],
        ),
        out_shape=[jax.ShapeDtypeStruct((experts, 3, part_rows, H), bf16) for _ in range(parts)],
        compiler_params=pltpu.CompilerParams(
            dimension_semantics=("arbitrary",), vmem_limit_bytes=VMEM_LIMIT
        ),
        cost_estimate=pl.CostEstimate(
            flops=experts * slots * 2 * D * 3 * H, transcendentals=0, bytes_accessed=48 * 1024 * 1024
        ),
    )(offsets, inputs, slot_grads, hidden)


def combine_kernel(ranks, rows_in, out, *, experts):
    count = out.shape[0]
    slot = lax.broadcasted_iota(i32, (count, SLOTS), 1)
    pick = jnp.concatenate(
        [(ranks[:, e : e + 1] == slot).astype(bf16) for e in range(experts)], axis=1
    )
    out[...] = dot(pick, rows_in[...]).astype(bf16)


def combine(ranks, slot_rows):
    rows, experts = ranks.shape
    block = min(256, rows)
    return pl.pallas_call(
        functools.partial(combine_kernel, experts=experts),
        name="combine",
        grid=(rows // block,),
        in_specs=[
            pl.BlockSpec((block, experts), lambda i: (i, 0)),
            whole((experts * SLOTS, D)),
        ],
        out_specs=pl.BlockSpec((block, D), lambda i: (i, 0)),
        out_shape=jax.ShapeDtypeStruct((rows, D), bf16),
        compiler_params=pltpu.CompilerParams(vmem_limit_bytes=VMEM_LIMIT),
        cost_estimate=pl.CostEstimate(
            flops=2 * rows * experts * SLOTS * D, transcendentals=0, bytes_accessed=8 * 1024 * 1024
        ),
    )(ranks, slot_rows.reshape(experts * SLOTS, D))


def rotate(values, cosine, sine):
    first = values[..., : HD // 2, :]
    second = values[..., HD // 2 :, :]
    return jnp.concatenate([first * cosine - second * sine, second * cosine + first * sine], axis=-2)


def tree_tables(ancestry, own_all, token_starts, query_block, key_block):
    groups, rows, _ = ancestry.shape
    tokens = own_all.shape[0]
    segments = jnp.arange(SEGS, dtype=i32)
    index = jnp.arange(tokens, dtype=i32)
    member = own_all[None, :] == segments[:, None]
    begin = jnp.min(jnp.where(member, index[None, :], tokens), axis=1)
    length = jnp.sum(member.astype(i32), axis=1)
    on_path = jnp.any(ancestry[:, :, :, None] == segments, axis=2)
    at = token_starts[:, None] + jnp.arange(rows, dtype=i32)[None, :]
    before = jnp.clip(at[:, :, None] - begin, 0, length)
    position = jnp.sum(jnp.where(on_path, before, 0), axis=2)
    bits = jnp.sum(on_path.astype(i32) << segments, axis=2)
    blocked = on_path.reshape(groups * rows // query_block, query_block, SEGS)
    path_any = jnp.any(blocked, axis=1)
    path_all = jnp.all(blocked, axis=1)
    keys = jnp.any(member.reshape(SEGS, tokens // key_block, key_block), axis=2).T
    some = jnp.any(path_any[:, None, :] & keys[None, :, :], axis=2)
    every = jnp.all(path_all[:, None, :] | ~keys[None, :, :], axis=2)
    query_start = at.reshape(-1, query_block)[:, 0]
    key_start = jnp.arange(tokens // key_block, dtype=i32) * key_block
    some &= key_start[None, :] < query_start[:, None] + query_block
    every &= key_start[None, :] + key_block <= query_start[:, None] + 1
    codes = jnp.where(some, jnp.where(every, 2, 1), 0).astype(i32)
    return position, bits, query_start, codes.reshape(-1)


def body(
    layer_input,
    cotangent,
    gain_attention,
    gain_mixture,
    w_query,
    w_key,
    w_value,
    w_out,
    w_router,
    w_gate,
    w_up,
    w_down,
    routes,
    priority,
    ancestry,
):
    chips, share, columns = lax.axis_size("chip"), lax.axis_size("core"), lax.axis_size("col")
    chip, core, column = lax.axis_index("chip"), lax.axis_index("core"), lax.axis_index("col")
    row_axes = ("chip", "core")
    rows, width = layer_input.shape
    weight_rows = w_query.shape[0]
    query_heads = w_query.shape[1] // HD
    key_heads = w_key.shape[1] // HD
    group = query_heads // key_heads
    own_heads = key_heads // share
    experts = w_gate.shape[1] // share
    tokens_all = rows * chips * share
    query_block = min(QUERY_BLOCK, rows)
    key_block = min(KEY_BLOCK, tokens_all)
    token_block = rows // columns

    places = jnp.stack(
        [(chip ^ j) * share + (core ^ h) for j in range(chips) for h in range(share)]
    ).astype(i32)
    token_offsets = places * rows
    feature_offsets = places * weight_rows

    def both(values):
        return jnp.stack([values] + ([swap_core(values)] if share == 2 else []))

    def gather_parts(own, other):
        halves = [chip_gather(own, chips, False)]
        if share == 2:
            halves.append(chip_gather(other, chips, True))
        return [halves[h][j] for j in range(chips) for h in range(share)]

    def reduce_parts(parts):
        own = chip_reduce(parts[0::share], chips, False)
        other = chip_reduce(parts[1::share], chips, True) if share == 2 else None
        return own, other

    x_full = lax.all_gather(layer_input, "col", axis=1, tiled=True)
    own_all = lax.all_gather(ancestry[:, 0], row_axes, axis=0, tiled=True)
    project = lax.all_gather(
        jnp.concatenate([w_query, w_key, w_value], axis=1), row_axes, axis=0, tiled=True
    )
    gains = lax.all_gather(jnp.stack([gain_attention, gain_mixture]), "col", axis=1, tiled=True)
    cotangent_full = lax.all_gather(cotangent, "col", axis=1, tiled=True)
    out_columns = lax.all_gather(w_out, "col", axis=1, tiled=True)
    out_router = lax.all_gather(
        jnp.concatenate([out_columns, w_router], axis=1), row_axes, axis=0, tiled=True
    )
    index_arrays = both(jnp.concatenate([routes, priority, ancestry], axis=1))
    all_routes = index_arrays[:, :, :TOPK]
    all_priority = index_arrays[:, :, TOPK : 2 * TOPK]
    all_ancestry = index_arrays[:, :, 2 * TOPK :]

    stacked = jnp.stack([w_gate, w_up, w_down]).transpose(2, 0, 1, 3)
    stacked = stacked.reshape(share, experts, 3, weight_rows, H)
    own_weights, other_weights = own_and_other(stacked, core, share)
    weight_parts = gather_parts(
        own_weights, swap_core(other_weights) if share == 2 else None
    )

    token_starts = jnp.stack([(chip * share + (core ^ g)) * rows for g in range(share)]).astype(i32)
    position, path_bits, query_starts, codes = tree_tables(
        all_ancestry, own_all, token_starts, query_block, key_block
    )
    key_bits = (jnp.int32(1) << own_all)[:, None]
    frequency = rope_base ** (-(jnp.arange(HD // 2, dtype=f32) * 2.0) / HD)
    angle = position.astype(f32)[:, None, :] * frequency[None, :, None]
    cosine, sine = jnp.cos(angle), jnp.sin(angle)
    first_expert = (column * (experts * share) + core * experts).astype(i32)
    ranks = slot_ranks(first_expert, all_routes, all_priority, experts)
    rank_columns = ranks.transpose(0, 2, 1)
    expert_ids = jnp.arange(EXPERTS, dtype=i32)
    chosen = jnp.any(all_routes[:, None, :, :] == expert_ids[None, :, None, None], axis=3)

    x_wide = x_full.astype(f32)
    inverse_one = lax.rsqrt(jnp.mean(x_wide * x_wide, axis=1, keepdims=True) + epsilon)
    h_one = (x_wide * inverse_one * gains[0][None, :]).astype(bf16)
    projected = dot_dims(project, h_one, 0, 1)
    query_width, key_width = query_heads * HD, key_heads * HD
    query = rotate(
        projected[:query_width].reshape(share, own_heads, group, HD, rows), cosine[0], sine[0]
    )
    query = (query.astype(bf16).astype(f32) * score_scale).astype(bf16)
    keys = rotate(
        projected[query_width : query_width + key_width].reshape(share, own_heads, HD, rows),
        cosine[0],
        sine[0],
    ).astype(bf16)
    values = projected[query_width + key_width :].reshape(share, own_heads, HD, rows).astype(bf16)
    sent = jnp.concatenate(
        [keys[:, :, None], values[:, :, None], query], axis=2
    )
    own_sent, other_sent = own_and_other(sent, core, share)
    received = [own_sent] + ([swap_core(other_sent)] if share == 2 else [])
    query_groups = jnp.stack([r[:, 2:] for r in received], axis=1)
    pairs = [r[:, :2].reshape(own_heads, 2 * HD, rows) for r in received]
    kv_parts = gather_parts(pairs[0], pairs[-1])

    attend_outs = [
        attend_forward(
            token_offsets,
            query_starts,
            codes,
            query_groups[head],
            path_bits[:, None, :],
            key_bits,
            [p[head] for p in kv_parts],
        )
        for head in range(own_heads)
    ]
    mixed_f = jnp.stack([o[0] for o in attend_outs])
    mixed_b = mixed_f.astype(bf16)
    mixed_own = mixed_b[:, 0]
    mixed_other = swap_core(mixed_b[:, 1]) if share == 2 else None
    mixed = in_core_order(mixed_own, mixed_other, core).reshape(query_width, rows)
    mixed_full = lax.all_gather(mixed, "col", axis=0, tiled=True)
    full_out = out_router[:, :D]
    full_router = out_router[:, D:]
    branch = dot_dims(mixed_full, full_out, 0, 1)
    x_middle = x_wide + branch_scale * branch
    inverse_two = lax.rsqrt(jnp.mean(x_middle * x_middle, axis=1, keepdims=True) + epsilon)
    h_two = (x_middle * inverse_two * gains[1][None, :]).astype(bf16)
    h_two_groups = both(h_two)
    grad_out = cotangent_full.astype(f32)
    mix_grads = both((branch_scale * grad_out).astype(bf16))

    logits = lax.dot_general(
        full_router, h_two_groups, (((0,), (2,)), ((), ())), preferred_element_type=f32
    ).transpose(1, 0, 2)
    shown = jnp.where(chosen, logits, masked_score)
    raised = jnp.where(chosen, jnp.exp(logits - jnp.max(shown, axis=1, keepdims=True)), 0.0)
    gates = raised / jnp.sum(raised, axis=1, keepdims=True)
    own_gates = lax.dynamic_slice_in_dim(gates, first_expert, experts, 1)
    weighted_out, slot_token_grads, inputs, slot_grads, hidden, pair_rows = run_experts(
        feature_offsets,
        h_two_groups,
        mix_grads,
        ranks.transpose(1, 0, 2)[:, :, None, :],
        own_gates.transpose(1, 0, 2)[:, :, None, :],
        weight_parts,
    )

    def combine_groups(slot_rows):
        if share == 1:
            return combine(rank_columns[0], slot_rows[0])
        received = swap_core(combine(rank_columns[1], slot_rows[1]))
        own = combine(rank_columns[0], slot_rows[0])
        return (own.astype(f32) + received.astype(f32)).astype(bf16)

    token_sum = combine_groups(slot_token_grads)
    token_grads = lax.psum_scatter(token_sum, "col", scatter_dimension=0, tiled=True).astype(f32)
    grad_parts = expert_grads(
        feature_offsets, inputs, slot_grads, hidden, chips * share, weight_rows
    )
    own_sums, other_sums = reduce_parts(grad_parts)
    returned = swap_core(other_sums) if share == 2 else None
    matrix_sums = in_core_order(own_sums, returned, core).reshape(
        share * experts, 3, weight_rows, H
    )
    matrix_grads = matrix_sums.astype(f32).transpose(1, 2, 0, 3)
    mix_sum = combine_groups(weighted_out)
    mix_slice = lax.psum_scatter(mix_sum, "col", scatter_dimension=1, tiled=True).astype(f32)
    feature_start = column * width
    x_middle_slice = lax.dynamic_slice_in_dim(x_middle, feature_start, width, 1)
    result = (x_middle_slice + branch_scale * mix_slice).astype(bf16)

    pair_rows = pair_rows[:, :, 0]
    pair_other = swap_core(pair_rows[:, 1]) if share == 2 else None
    pair_columns = in_core_order(pair_rows[:, 0], pair_other, core).reshape(share * experts, rows)
    pair_grad = lax.all_gather(pair_columns, "col", axis=0, tiled=True)
    picked_grad = gates[0] * (pair_grad - jnp.sum(gates[0] * pair_grad, axis=0, keepdims=True))
    logit_grad = picked_grad.astype(bf16)

    token_start = column * token_block

    def own_tokens(array):
        return lax.dynamic_slice_in_dim(array, token_start, token_block, 0)

    h_two_grad = token_grads + dot_dims(
        lax.dynamic_slice_in_dim(logit_grad, token_start, token_block, 1), full_router, 0, 1
    )
    x_part, inverse_part = own_tokens(x_middle), own_tokens(inverse_two)
    scaled_two = h_two_grad * gains[1][None, :]
    inner_two = jnp.sum(scaled_two * x_part, axis=1, keepdims=True)
    x_middle_grad = (
        own_tokens(grad_out) + inverse_part * scaled_two - x_part * inverse_part**3 * inner_two / D
    )
    gain_mixture_part = jnp.sum(h_two_grad * x_part * inverse_part, axis=0)
    branch_grad = lax.all_gather(
        (branch_scale * x_middle_grad).astype(bf16), "col", axis=0, tiled=True
    )

    own_out = lax.dynamic_slice_in_dim(full_out, column * query_width, query_width, 1)
    mixed_grad = dot_dims(own_out, branch_grad, 0, 1).astype(bf16)
    own_grad, other_grad = own_and_other(
        mixed_grad.reshape(share, own_heads, group, HD, rows), core, share
    )
    grad_groups = jnp.stack(
        [own_grad] + ([swap_core(other_grad)] if share == 2 else []), axis=1
    )
    backward_outs = [
        attend_backward(
            token_offsets,
            query_starts,
            codes,
            query_groups[head],
            grad_groups[head],
            attend_outs[head][0],
            attend_outs[head][1],
            path_bits[:, None, :],
            key_bits,
            [p[head] for p in kv_parts],
        )
        for head in range(own_heads)
    ]
    query_grad = jnp.stack([o[0] for o in backward_outs])
    query_grad = rotate(
        query_grad, cosine[None, :, None], -sine[None, :, None]
    ).astype(bf16)
    query_other = swap_core(query_grad[:, 1]) if share == 2 else None
    query_pre_grad = in_core_order(query_grad[:, 0], query_other, core).reshape(query_width, rows)
    kv_own, kv_other = reduce_parts(
        [jnp.stack([o[1][n] for o in backward_outs]) for n in range(chips * share)]
    )
    kv_other = swap_core(kv_other) if share == 2 else None
    kv_grad = in_core_order(kv_own, kv_other, core).astype(f32)
    kv_grad = kv_grad.transpose(0, 1, 3, 2).reshape(key_heads, 2 * HD, rows)
    key_pre_grad = (
        rotate(kv_grad[:, :HD], cosine[0], -sine[0]).astype(bf16).reshape(key_width, rows)
    )
    value_pre_grad = kv_grad[:, HD:].astype(bf16).reshape(key_width, rows)
    project_grad = jnp.concatenate([query_pre_grad, key_pre_grad, value_pre_grad], axis=0)

    h_one_part = dot_dims(project_grad, project, 0, 1)
    inner_one = lax.psum(
        jnp.sum(h_one_part * gains[0][None, :] * x_wide, axis=1), "col"
    )[:, None]
    h_one_grad = lax.psum_scatter(
        h_one_part.astype(bf16), "col", scatter_dimension=1, tiled=True
    ).astype(f32)
    x_slice = layer_input.astype(f32)
    middle_slice = lax.dynamic_slice_in_dim(branch_grad, feature_start, width, 1).astype(f32)
    input_grad = (
        middle_slice * (1.0 / branch_scale)
        + inverse_one * h_one_grad * gain_attention[None, :]
        - x_slice * inverse_one**3 * inner_one / D
    )
    gain_attention_part = jnp.sum(h_one_grad * x_slice * inverse_one, axis=0)

    early = jnp.concatenate(
        [dot_dims(branch_grad, mixed, 0, 1), dot_dims(h_two, logit_grad, 0, 1)], axis=1
    )
    early_sums = lax.psum_scatter(
        early.astype(bf16), row_axes, scatter_dimension=0, tiled=True
    ).astype(f32)
    late_sums = lax.psum_scatter(
        dot_dims(h_one, project_grad, 0, 1).astype(bf16), row_axes, scatter_dimension=0, tiled=True
    ).astype(f32)
    gain_parts = jnp.stack(
        [
            lax.dynamic_update_slice_in_dim(
                jnp.zeros((D,), f32), gain_attention_part, feature_start, 0
            ),
            gain_mixture_part,
        ]
    )
    gain_sums = lax.dynamic_slice_in_dim(
        lax.psum(gain_parts, ("chip", "core", "col")), feature_start, width, 1
    )
    return (
        result,
        input_grad,
        gain_sums[0],
        gain_sums[1],
        late_sums[:, :query_width],
        late_sums[:, query_width : query_width + key_width],
        late_sums[:, query_width + key_width :],
        early_sums[:, :query_width],
        early_sums[:, query_width:],
        matrix_grads[0],
        matrix_grads[1],
        matrix_grads[2],
    )


def solution(mesh):
    rows, columns = mesh.shape["row"], mesh.shape["col"]
    halves = rows % 2 == 0 and EXPERTS // columns % 2 == 0 and KVH // columns % 2 == 0
    share = 2 if halves else 1
    split = Mesh(mesh.devices.reshape(rows // share, share, columns), ("chip", "core", "col"))
    row = ("chip", "core")
    return jax.shard_map(
        body,
        mesh=split,
        in_specs=(
            P(row, "col"),
            P(row, "col"),
            P("col"),
            P("col"),
            P(row, "col"),
            P(row, "col"),
            P(row, "col"),
            P(row, "col"),
            P(row, None),
            P(row, "col", None),
            P(row, "col", None),
            P(row, "col", None),
            P(row, None),
            P(row, None),
            P(row, None),
        ),
        out_specs=(
            P(row, "col"),
            P(row, "col"),
            P("col"),
            P("col"),
            P(row, "col"),
            P(row, "col"),
            P(row, "col"),
            P(row, "col"),
            P(row, None),
            P(row, "col", None),
            P(row, "col", None),
            P(row, "col", None),
        ),
        check_vma=False,
    )
```

```python
import functools

import jax
import jax.numpy as jnp
from jax import lax
from jax.experimental.layout import Layout, with_layout_constraint
from jax.experimental import pallas as pl
from jax.experimental.pallas import tpu as pltpu
from jax.sharding import Mesh
from jax.sharding import PartitionSpec as P

D = 1536
HD = 64
H = 512
KVH = 8
EXPERTS = 40
TOPK = 8
SEGS = 13
CAP = 230
SLOTS = 256

epsilon = 1e-06
branch_scale = 0.22
score_scale = 0.015625
rope_base = 10000.0
masked_score = -1e30

bf16 = jnp.bfloat16
f32 = jnp.float32
i32 = jnp.int32

QUERY_BLOCK = 512
KEY_BLOCK = 512
VMEM_LIMIT = 60 * 1024 * 1024


def dot(left, right):
    return jnp.dot(left, right, preferred_element_type=f32)


def dot_dims(left, right, left_dim, right_dim):
    return lax.dot_general(
        left, right, (((left_dim,), (right_dim,)), ((), ())), preferred_element_type=f32
    )


def swap(values, axis, bit):
    size = lax.axis_size(axis)
    return lax.ppermute(values, axis, [(i, i ^ bit) for i in range(size)])


def swap_core(values):
    return swap(values, "core", 1)


def chip_bits(chips):
    return [1 << b for b in range(chips.bit_length() - 1)]


def half_bits(chips, half):
    bits = chip_bits(chips)
    return bits if half == 0 else bits[::-1]


def gather_rounds(chips, halves):
    rounds = []
    for level in range(len(chip_bits(chips))):
        moves = []
        for half in range(halves):
            bits = half_bits(chips, half)
            held = [0]
            for bit in bits[:level]:
                held += [j ^ bit for j in held]
            moves.append([(half, j, bits[level]) for j in sorted(held)])
        rounds += [list(r) for r in zip(*moves)]
    return rounds


def run_gather(held, rounds):
    held = dict(held)
    for moves in rounds:
        for half, j, bit in moves:
            held[half, j ^ bit] = swap(held[half, j], "chip", bit)
    return held


def gather_parts(values, chips):
    held = run_gather(
        {(h, 0): v for h, v in enumerate(values)}, gather_rounds(chips, len(values))
    )
    return listed(held, chips)


def listed(held, chips):
    halves = len(held) // chips
    return [held[h, j] for j in range(chips) for h in range(halves)]


def reduce_levels(chips, halves):
    levels = []
    for level in range(len(chip_bits(chips))):
        moves = []
        for half in range(halves):
            bits = half_bits(chips, half)
            done = sum(bits[: level + 1])
            moves.append([(half, j, bits[level]) for j in range(chips) if not j & done])
        levels.append([list(r) for r in zip(*moves)])
    return levels


def take(held, moves):
    return {(h, j): swap(held[h, j ^ bit], "chip", bit) for h, j, bit in moves}


def add_taken(held, taken):
    sums = {k: (held[k].astype(f32) + v.astype(f32)).astype(v.dtype) for k, v in taken.items()}
    return {**held, **sums}


def reduce_parts(parts, chips, share):
    held = {(h, j): parts[j * share + h] for j in range(chips) for h in range(share)}
    for rounds in reduce_levels(chips, share):
        taken = {}
        for moves in rounds:
            taken.update(take(held, moves))
        held = add_taken(held, taken)
    return [held[h, 0] for h in range(share)]


def column_shifts(values_for):
    size = lax.axis_size("col")
    me = lax.axis_index("col")
    return [
        (
            (me - d) % size,
            lax.ppermute(values_for((me + d) % size), "col", [(i, (i + d) % size) for i in range(size)]),
        )
        for d in range(1, size)
    ]


def column_sum(values):
    for _, other in column_shifts(lambda _: values):
        values = values + other
    return values


def column_rows(values):
    rows = values.shape[0]
    size = lax.axis_size("col")
    out = jnp.zeros((size * rows,) + values.shape[1:], values.dtype)
    for c, part in [(lax.axis_index("col"), values)] + column_shifts(lambda _: values):
        out = lax.dynamic_update_slice_in_dim(out, part, c * rows, 0)
    return out


def row_sum(values):
    chips, share = lax.axis_size("chip"), lax.axis_size("core")
    size = chips * share
    total = values
    for n in range(1, size):
        total = total + lax.ppermute(values, ("chip", "core"), [(i, i ^ n) for i in range(size)])
    return total


def tie(*trees):
    return lax.optimization_barrier(trees)


def own_and_other(values, core, share):
    if share == 1:
        return values[0], None
    mine = lax.dynamic_index_in_dim(values, core, 0, keepdims=False)
    other = lax.dynamic_index_in_dim(values, 1 - core, 0, keepdims=False)
    return mine, other


def in_core_order(mine, other, core):
    if other is None:
        return mine[None]
    first = core == 0
    return jnp.stack([jnp.where(first, mine, other), jnp.where(first, other, mine)])


def column_of(row):
    return jnp.broadcast_to(row, (8, row.shape[1])).T[:, :1]


def attend_forward_kernel(
    offsets, starts, codes, query, path, key_bits, *rest, parts, key_blocks, key_block
):
    kv_parts = rest[:parts]
    out, rounded, log_total, key_columns, value_rows, query_rows, peak, mixed, paths = rest[parts:]
    step = pl.program_id(0)
    heads, width, count = query.shape[1:]

    @pl.when(step == 0)
    def _():
        for n, part in enumerate(kv_parts):
            rows = part.shape[1]
            start = pl.multiple_of(offsets[n], rows)
            key_columns[:, pl.ds(start, rows)] = part[:width, :]
            turned = pltpu.roll(part[...].astype(f32).T, width, 1)
            lane = lax.broadcasted_iota(i32, turned.shape, 1)
            value_rows[pl.ds(start, rows), :] = jnp.where(lane < width, turned, 1.0).astype(bf16)

    for head in range(heads):
        query_rows[head * count : (head + 1) * count] = query[0, head].astype(f32).T.astype(bf16)
    paths[...] = jnp.broadcast_to(path[0], (8, count)).T
    peak[...] = jnp.full_like(peak, masked_score)
    mixed[...] = jnp.zeros_like(mixed)

    def block(number, masked):
        start = pl.multiple_of(number * key_block, key_block)
        scores = dot(query_rows[...], key_columns[:, pl.ds(start, key_block)])
        if masked:
            keys = start + lax.broadcasted_iota(i32, (count, key_block), 1)
            queries = starts[step] + lax.broadcasted_iota(i32, (count, key_block), 0)
            on_path = (paths[:, :1] & key_bits[:, pl.ds(start, key_block)]) != 0
            allowed = on_path & (keys <= queries)
            scores = jnp.where(
                allowed[None], scores.reshape(heads, count, key_block), masked_score
            ).reshape(heads * count, key_block)
        old = peak[...]
        new = jnp.maximum(old, jnp.max(scores, axis=1, keepdims=True))
        weights = jnp.exp(scores - jnp.tile(new, (1, key_block // 128))).astype(bf16)
        mixed[...] = mixed[...] * jnp.exp(old - new) + dot(
            weights, value_rows[pl.ds(start, key_block), :]
        )
        peak[...] = new

    @pl.loop(0, key_blocks)
    def _(number):
        code = codes[step * key_blocks + number]

        @pl.when(code == 1)
        def _():
            block(number, True)

        @pl.when(code == 2)
        def _():
            block(number, False)

    lane = lax.broadcasted_iota(i32, (count, 2 * width), 1)
    for head in range(heads):
        at = slice(head * count, (head + 1) * count)
        sums = mixed[at]
        turned = jnp.where(
            lane < width, sums / pltpu.roll(sums, width, 1), peak[at] + jnp.log(sums)
        ).T
        out[0, head] = turned[:width]
        rounded[0, head] = turned[:width].astype(bf16)
        log_total[0, head] = turned[width : width + 1]


def attend_backward_kernel(
    offsets,
    starts,
    codes,
    query,
    mixed_grad,
    mixed,
    log_total,
    path,
    key_bits,
    *rest,
    parts,
    key_blocks,
    key_block,
):
    kv_parts = rest[:parts]
    query_grad = rest[parts]
    grad_parts = rest[parts + 1 : 2 * parts + 1]
    (kv_rows, key_columns, padded, padded_grad, query_rows, grad_rows, row_terms, query_sum, kv_sum) = (
        rest[2 * parts + 1 :]
    )
    step = pl.program_id(0)
    heads, width, count = query.shape[1:]

    @pl.when(step == 0)
    def _():
        for n, part in enumerate(kv_parts):
            rows = part.shape[1]
            start = pl.multiple_of(offsets[n], rows)
            key_columns[:, pl.ds(start, rows)] = part[:width, :]
            kv_rows[pl.ds(start, rows), :] = part[...].astype(f32).T.astype(bf16)
        padded[...] = jnp.zeros_like(padded)
        padded_grad[...] = jnp.zeros_like(padded_grad)
        kv_sum[...] = jnp.zeros_like(kv_sum)

    for head in range(heads):
        at = slice(head * count, (head + 1) * count)
        padded[:width, at] = query[0, head]
        padded_grad[width:, at] = mixed_grad[0, head]
        row_terms[0:1, at] = log_total[0, head]
        row_terms[1:2, at] = jnp.sum(
            mixed_grad[0, head].astype(f32) * mixed[0, head], axis=0, keepdims=True
        )
    query_rows[...] = padded[...].astype(f32).T.astype(bf16)
    grad_rows[...] = padded_grad[...].astype(f32).T.astype(bf16)
    query_sum[...] = jnp.zeros_like(query_sum)

    def block(number, masked):
        start = pl.multiple_of(number * key_block, key_block)
        rows = kv_rows[pl.ds(start, key_block), :]
        scores = dot(rows, padded[...])
        if masked:
            keys = start + lax.broadcasted_iota(i32, (key_block, count), 0)
            queries = starts[step] + lax.broadcasted_iota(i32, (key_block, count), 1)
            on_path = (path[0] & column_of(key_bits[:, pl.ds(start, key_block)])) != 0
            allowed = on_path & (keys <= queries)
            scores = jnp.where(jnp.concatenate([allowed] * heads, axis=1), scores, masked_score)
        weights = jnp.exp(scores - row_terms[0:1, :])
        weight_grad = dot(rows, padded_grad[...])
        score_grad = (weights * (weight_grad - row_terms[1:2, :])).astype(bf16)
        kv_sum[pl.ds(start, key_block), :] += dot(score_grad, query_rows[...]) + dot(
            weights.astype(bf16), grad_rows[...]
        )
        query_sum[...] += dot(key_columns[:, pl.ds(start, key_block)], score_grad)

    @pl.loop(0, key_blocks)
    def _(number):
        code = codes[step * key_blocks + number]

        @pl.when(code == 1)
        def _():
            block(number, True)

        @pl.when(code == 2)
        def _():
            block(number, False)

    for head in range(heads):
        query_grad[0, head] = score_scale * query_sum[:, head * count : (head + 1) * count]

    @pl.when(step == pl.num_programs(0) - 1)
    def _():
        for n, part in enumerate(grad_parts):
            rows = part.shape[0]
            part[...] = kv_sum[pl.ds(pl.multiple_of(offsets[n], rows), rows), :].astype(part.dtype)


def whole(shape):
    return pl.BlockSpec(shape, lambda *_: (0,) * len(shape), pipeline_mode=pl.Buffered(1))


def attention_specs(heads, rows, block):
    per_group = rows // block

    def four(step, *_):
        return (step // per_group, 0, 0, step % per_group)

    return pl.BlockSpec((1, heads, HD, block), four), pl.BlockSpec((1, heads, 1, block), four)


def attend_forward(offsets, starts, codes, query, path_bits, key_bits, kv_parts):
    groups, heads, _, rows = query.shape
    block = min(QUERY_BLOCK, rows)
    per_group = rows // block
    tokens = key_bits.shape[1]
    key_block = min(KEY_BLOCK, tokens)
    wide, row = attention_specs(heads, rows, block)
    kernel = functools.partial(
        attend_forward_kernel,
        parts=len(kv_parts),
        key_blocks=tokens // key_block,
        key_block=key_block,
    )
    return pl.pallas_call(
        kernel,
        name="attend_forward",
        grid_spec=pltpu.PrefetchScalarGridSpec(
            num_scalar_prefetch=3,
            grid=(groups * per_group,),
            in_specs=[
                wide,
                pl.BlockSpec((1, 1, block), lambda s, *_: (s // per_group, 0, s % per_group)),
                whole(key_bits.shape),
            ]
            + [whole(p.shape) for p in kv_parts],
            out_specs=[wide, wide, row],
            scratch_shapes=[
                pltpu.VMEM((HD, tokens), bf16),
                pltpu.VMEM((tokens, 2 * HD), bf16),
                pltpu.VMEM((heads * block, HD), bf16),
                pltpu.VMEM((heads * block, 2 * HD), f32),
                pltpu.VMEM((heads * block, 2 * HD), f32),
                pltpu.VMEM((block, 8), i32),
            ],
        ),
        out_shape=[
            jax.ShapeDtypeStruct(query.shape, f32),
            jax.ShapeDtypeStruct(query.shape, bf16),
            jax.ShapeDtypeStruct((groups, heads, 1, rows), f32),
        ],
        compiler_params=pltpu.CompilerParams(
            dimension_semantics=("arbitrary",), vmem_limit_bytes=VMEM_LIMIT
        ),
    )(offsets, starts, codes, query, path_bits[:, None, :], key_bits, *kv_parts)


def attend_backward(
    offsets, starts, codes, query, mixed_grad, mixed, log_total, path_bits, key_bits, kv_parts
):
    groups, heads, _, rows = query.shape
    block = min(QUERY_BLOCK, rows)
    per_group = rows // block
    tokens = key_bits.shape[1]
    key_block = min(KEY_BLOCK, tokens)
    wide, row = attention_specs(heads, rows, block)
    grad_shape = (kv_parts[0].shape[1], 2 * HD)
    kernel = functools.partial(
        attend_backward_kernel,
        parts=len(kv_parts),
        key_blocks=tokens // key_block,
        key_block=key_block,
    )
    outs = pl.pallas_call(
        kernel,
        name="attend_backward",
        grid_spec=pltpu.PrefetchScalarGridSpec(
            num_scalar_prefetch=3,
            grid=(groups * per_group,),
            in_specs=[
                wide,
                wide,
                wide,
                row,
                pl.BlockSpec((1, 1, block), lambda s, *_: (s // per_group, 0, s % per_group)),
                whole(key_bits.shape),
            ]
            + [whole(p.shape) for p in kv_parts],
            out_specs=[wide] + [whole(grad_shape) for _ in kv_parts],
            scratch_shapes=[
                pltpu.VMEM((tokens, 2 * HD), bf16),
                pltpu.VMEM((HD, tokens), bf16),
                pltpu.VMEM((2 * HD, heads * block), bf16),
                pltpu.VMEM((2 * HD, heads * block), bf16),
                pltpu.VMEM((heads * block, 2 * HD), bf16),
                pltpu.VMEM((heads * block, 2 * HD), bf16),
                pltpu.VMEM((8, heads * block), f32),
                pltpu.VMEM((HD, heads * block), f32),
                pltpu.VMEM((tokens, 2 * HD), f32),
            ],
        ),
        out_shape=[jax.ShapeDtypeStruct(query.shape, f32)]
        + [jax.ShapeDtypeStruct(grad_shape, bf16) for _ in kv_parts],
        compiler_params=pltpu.CompilerParams(
            dimension_semantics=("arbitrary",), vmem_limit_bytes=VMEM_LIMIT
        ),
    )(
        offsets,
        starts,
        codes,
        query,
        mixed_grad,
        mixed,
        log_total,
        path_bits[:, None, :],
        key_bits,
        *kv_parts,
    )
    return outs[0], outs[1:]


def rank_kernel(first, route_rows, priority_rows, route_columns, priority_columns, out, *, experts):
    rows = route_rows.shape[2]
    never = rows * TOPK
    for e in range(experts):
        expert = first[0] + e
        along = jnp.min(
            jnp.where(route_rows[0] == expert, priority_rows[0], never), axis=0, keepdims=True
        )
        down = jnp.min(
            jnp.where(route_columns[0] == expert, priority_columns[0], never), axis=1, keepdims=True
        )
        count = jnp.zeros((8, rows), i32)
        for begin in range(0, rows, 8):
            count += (down[begin : begin + 8] < along).astype(i32)
        rank = jnp.sum(count, axis=0, keepdims=True)
        out[0, e : e + 1, :] = jnp.where((along < never) & (rank < CAP), rank, -1)
    if out.shape[1] > experts:
        out[0, experts:, :] = jnp.full((out.shape[1] - experts, rows), -1, i32)


def slot_ranks(first, routes, priority, experts):
    groups, rows, _ = routes.shape
    tall = pl.BlockSpec((1, rows, TOPK), lambda g, *_: (g, 0, 0))
    flat = pl.BlockSpec((1, TOPK, rows), lambda g, *_: (g, 0, 0))
    padded = -(-experts // 8) * 8
    return pl.pallas_call(
        functools.partial(rank_kernel, experts=experts),
        name="slot_ranks",
        grid_spec=pltpu.PrefetchScalarGridSpec(
            num_scalar_prefetch=1,
            grid=(groups,),
            in_specs=[flat, flat, tall, tall],
            out_specs=pl.BlockSpec((1, padded, rows), lambda g, *_: (g, 0, 0)),
        ),
        out_shape=jax.ShapeDtypeStruct((groups, padded, rows), i32),
        compiler_params=pltpu.CompilerParams(vmem_limit_bytes=VMEM_LIMIT),
    )(
        first.reshape(1),
        routes.transpose(0, 2, 1),
        priority.transpose(0, 2, 1),
        routes,
        priority,
    )


def expert_kernel(offsets, first, ranks, *rest, parts, groups):
    gates, rest = rest[:groups], rest[groups:]
    tokens, rest = rest[:groups], rest[groups:]
    grads, rest = rest[:groups], rest[groups:]
    weights = rest[:parts]
    weighted_out, token_grad, inputs, slot_grads, hidden, pair_grads, matrices = rest[parts:]
    rows = tokens[0].shape[0]
    e = pl.program_id(0)
    for n, part in enumerate(weights):
        count = part.shape[2]
        for m in range(3):
            matrices[m, pl.ds(pl.multiple_of(offsets[n], count), count), :] = part[m, 0]
    slot = lax.broadcasted_iota(i32, (SLOTS, rows), 0)
    for g in range(groups):
        at = slice(g * SLOTS, (g + 1) * SLOTS)
        inside = slot == ranks[g, pl.ds(e, 1), :]
        pick = inside.astype(bf16)
        gate = gates[g][pl.ds(first[0] + e, 1), :]
        weight = jnp.sum(jnp.where(inside, gate, 0.0), axis=1, keepdims=True)
        picked = dot(pick, tokens[g][...]).astype(bf16)
        inputs[0, at, :] = picked
        gate_pre = dot(picked, matrices[0])
        up_pre = dot(picked, matrices[1])
        sigma = jax.nn.sigmoid(gate_pre)
        silu = gate_pre * sigma
        active = (silu * up_pre).astype(bf16)
        out = dot_dims(active, matrices[2], 1, 1)
        weighted_out[g, 0] = (out * weight).astype(bf16)
        upstream = dot(pick, grads[g][...])
        pair = jnp.sum(upstream * out, axis=1, keepdims=True)
        pair_grads[g, pl.ds(e, 1), :] = jnp.sum(jnp.where(inside, pair, 0.0), axis=0, keepdims=True)
        slot_grad = (weight * upstream).astype(bf16)
        slot_grads[0, at, :] = slot_grad
        act_grad = dot(slot_grad, matrices[2])
        gate_grad = (act_grad * up_pre * sigma * (1.0 + gate_pre * (1.0 - sigma))).astype(bf16)
        up_grad = (act_grad * silu).astype(bf16)
        hidden[0, 0, at, :] = gate_grad
        hidden[0, 1, at, :] = up_grad
        hidden[0, 2, at, :] = active
        token_grad[g, 0] = (
            dot_dims(gate_grad, matrices[0], 1, 1) + dot_dims(up_grad, matrices[1], 1, 1)
        ).astype(bf16)


def run_experts(offsets, first, ranks, gates, tokens, grads, weight_parts):
    groups = len(tokens)
    rows = tokens[0].shape[0]
    _, experts, part_rows, _ = weight_parts[0].shape
    parts = len(weight_parts)
    slots = groups * SLOTS
    by_group = pl.BlockSpec((groups, 1, SLOTS, D), lambda e, *_: (0, e, 0, 0))
    stash = pl.BlockSpec((1, slots, D), lambda e, *_: (e, 0, 0))
    return pl.pallas_call(
        functools.partial(expert_kernel, parts=parts, groups=groups),
        name="experts",
        grid_spec=pltpu.PrefetchScalarGridSpec(
            num_scalar_prefetch=2,
            grid=(experts,),
            in_specs=[whole(ranks.shape)]
            + [whole((EXPERTS, rows)) for _ in range(groups)]
            + [whole((rows, D)) for _ in range(2 * groups)]
            + [pl.BlockSpec((3, 1, part_rows, H), lambda e, *_: (0, e, 0, 0)) for _ in weight_parts],
            out_specs=[
                by_group,
                by_group,
                stash,
                stash,
                pl.BlockSpec((1, 3, slots, H), lambda e, *_: (e, 0, 0, 0)),
                whole(ranks.shape),
            ],
            scratch_shapes=[pltpu.VMEM((3, D, H), bf16)],
        ),
        out_shape=[
            jax.ShapeDtypeStruct((groups, experts, SLOTS, D), bf16),
            jax.ShapeDtypeStruct((groups, experts, SLOTS, D), bf16),
            jax.ShapeDtypeStruct((experts, slots, D), bf16),
            jax.ShapeDtypeStruct((experts, slots, D), bf16),
            jax.ShapeDtypeStruct((experts, 3, slots, H), bf16),
            jax.ShapeDtypeStruct(ranks.shape, f32),
        ],
        compiler_params=pltpu.CompilerParams(
            dimension_semantics=("arbitrary",), vmem_limit_bytes=VMEM_LIMIT
        ),
    )(
        offsets,
        first.reshape(1),
        ranks,
        *gates,
        *tokens,
        *grads,
        *weight_parts,
    )


def expert_grad_kernel(offsets, inputs, slot_grads, hidden, *rest):
    outs, total = rest[:-1], rest[-1]
    for m in range(3):
        left = inputs if m < 2 else slot_grads
        total[...] = dot_dims(left[0], hidden[0, m], 0, 0)
        for n, out in enumerate(outs):
            count = out.shape[2]
            out[m, 0] = total[pl.ds(pl.multiple_of(offsets[n], count), count), :].astype(bf16)


def expert_grads(offsets, inputs, slot_grads, hidden, parts, part_rows):
    experts, slots, _ = inputs.shape
    stash = pl.BlockSpec((1, slots, D), lambda e, *_: (e, 0, 0))
    return pl.pallas_call(
        expert_grad_kernel,
        name="expert_grads",
        grid_spec=pltpu.PrefetchScalarGridSpec(
            num_scalar_prefetch=1,
            grid=(experts,),
            in_specs=[stash, stash, pl.BlockSpec((1, 3, slots, H), lambda e, *_: (e, 0, 0, 0))],
            out_specs=[
                pl.BlockSpec((3, 1, part_rows, H), lambda e, *_: (0, e, 0, 0)) for _ in range(parts)
            ],
            scratch_shapes=[pltpu.VMEM((D, H), f32)],
        ),
        out_shape=[jax.ShapeDtypeStruct((3, experts, part_rows, H), bf16) for _ in range(parts)],
        compiler_params=pltpu.CompilerParams(
            dimension_semantics=("arbitrary",), vmem_limit_bytes=VMEM_LIMIT
        ),
    )(offsets, inputs, slot_grads, hidden)


def combine_kernel(ranks, rows_in, out, *, experts):
    count = out.shape[0]
    slot = lax.broadcasted_iota(i32, (count, SLOTS), 1)
    pick = jnp.concatenate(
        [(ranks[0, :, e : e + 1] == slot).astype(bf16) for e in range(experts)], axis=1
    )
    out[...] = dot(pick, rows_in[0]).astype(bf16)


def combine(ranks, slot_rows, g):
    groups, rows, columns = ranks.shape
    experts = slot_rows.shape[1]
    block = min(256, rows)
    return pl.pallas_call(
        functools.partial(combine_kernel, experts=experts),
        name="combine",
        grid=(rows // block,),
        in_specs=[
            pl.BlockSpec((1, block, columns), lambda i: (g, i, 0)),
            pl.BlockSpec(
                (1, experts * SLOTS, D), lambda i: (g, 0, 0), pipeline_mode=pl.Buffered(1)
            ),
        ],
        out_specs=pl.BlockSpec((block, D), lambda i: (i, 0)),
        out_shape=jax.ShapeDtypeStruct((rows, D), bf16),
        compiler_params=pltpu.CompilerParams(vmem_limit_bytes=VMEM_LIMIT),
    )(ranks, slot_rows.reshape(groups, experts * SLOTS, D))


def project_kernel(mixed, x, gain, matrix, middle, normed, inverse):
    branch = dot_dims(mixed[...].astype(f32).T.astype(bf16), matrix[:, :D], 1, 1)
    total = x[...].astype(f32) + branch_scale * branch
    scale = lax.rsqrt(jnp.mean(total * total, axis=1, keepdims=True) + epsilon)
    middle[...] = total
    inverse[...] = scale
    normed[...] = (total * scale * gain[...]).astype(bf16)


def project_out(mixed, x, gain, matrix):
    rows = x.shape[0]
    block = min(256, rows)
    tall = pl.BlockSpec((block, D), lambda i: (i, 0))
    return pl.pallas_call(
        project_kernel,
        name="project_out",
        grid=(rows // block,),
        in_specs=[
            pl.BlockSpec((D, block), lambda i: (0, i)),
            tall,
            whole(gain.shape),
            whole(matrix.shape),
        ],
        out_specs=[tall, tall, pl.BlockSpec((block, 1), lambda i: (i, 0))],
        out_shape=[
            jax.ShapeDtypeStruct((rows, D), f32),
            jax.ShapeDtypeStruct((rows, D), bf16),
            jax.ShapeDtypeStruct((rows, 1), f32),
        ],
        compiler_params=pltpu.CompilerParams(
            dimension_semantics=("arbitrary",), vmem_limit_bytes=VMEM_LIMIT
        ),
    )(mixed, x, gain, matrix)


def rotate(values, cosine, sine):
    first = values[..., : HD // 2, :]
    second = values[..., HD // 2 :, :]
    return jnp.concatenate([first * cosine - second * sine, second * cosine + first * sine], axis=-2)


def rotate_back(values, cosine, sine):
    first = values[..., : HD // 2, :]
    second = values[..., HD // 2 :, :]
    return jnp.concatenate([first * cosine + second * sine, second * cosine - first * sine], axis=-2)


def tree_tables(ancestry, own_all, token_starts, query_block, key_block):
    groups, rows, _ = ancestry.shape
    tokens = own_all.shape[0]
    segments = jnp.arange(SEGS, dtype=i32)
    index = jnp.arange(tokens, dtype=i32)
    member = own_all[None, :] == segments[:, None]
    begin = jnp.min(jnp.where(member, index[None, :], tokens), axis=1)
    length = jnp.sum(member.astype(i32), axis=1)
    on_path = jnp.any(ancestry[:, :, :, None] == segments, axis=2)
    at = token_starts[:, None] + jnp.arange(rows, dtype=i32)[None, :]
    before = jnp.clip(at[:, :, None] - begin, 0, length)
    position = jnp.sum(jnp.where(on_path, before, 0), axis=2)
    bits = jnp.sum(on_path.astype(i32) << segments, axis=2)
    blocked = on_path.reshape(groups * rows // query_block, query_block, SEGS)
    path_any = jnp.any(blocked, axis=1)
    path_all = jnp.all(blocked, axis=1)
    keys = jnp.any(member.reshape(SEGS, tokens // key_block, key_block), axis=2).T
    some = jnp.any(path_any[:, None, :] & keys[None, :, :], axis=2)
    every = jnp.all(path_all[:, None, :] | ~keys[None, :, :], axis=2)
    query_start = at.reshape(-1, query_block)[:, 0]
    key_start = jnp.arange(tokens // key_block, dtype=i32) * key_block
    some &= key_start[None, :] < query_start[:, None] + query_block
    every &= key_start[None, :] + key_block <= query_start[:, None] + 1
    codes = jnp.where(some, jnp.where(every, 2, 1), 0).astype(i32)
    return position, bits, query_start, codes.reshape(-1)


def body(
    layer_input,
    cotangent,
    gain_attention,
    gain_mixture,
    w_query,
    w_key,
    w_value,
    w_out,
    w_router,
    w_gate,
    w_up,
    w_down,
    routes,
    priority,
    ancestry,
):
    chips, share, columns = lax.axis_size("chip"), lax.axis_size("core"), lax.axis_size("col")
    chip, core, column = lax.axis_index("chip"), lax.axis_index("core"), lax.axis_index("col")
    row_axes = ("chip", "core")
    rows, width = layer_input.shape
    weight_rows = w_query.shape[0]
    query_heads = w_query.shape[1] // HD
    key_heads = w_key.shape[1] // HD
    group = query_heads // key_heads
    own_heads = key_heads // share
    experts = w_gate.shape[1] // share
    tokens_all = rows * chips * share
    query_block = min(QUERY_BLOCK, rows)
    key_block = min(KEY_BLOCK, tokens_all)
    token_block = rows // columns

    places = [(chip ^ j) * share + (core ^ h) for j in range(chips) for h in range(share)]
    token_offsets = jnp.stack([p * rows for p in places]).astype(i32)
    feature_offsets = jnp.stack([p * weight_rows for p in places]).astype(i32)

    def groups_of(values):
        return [values] + ([swap_core(values)] if share == 2 else [])

    x_full = lax.all_gather(layer_input, "col", axis=1, tiled=True)
    cotangent_full = lax.all_gather(cotangent, "col", axis=1, tiled=True)
    index_groups = groups_of(jnp.concatenate([routes, priority, ancestry], axis=1))
    index_arrays = jnp.stack(index_groups)
    all_routes = index_arrays[:, :, :TOPK]
    all_priority = index_arrays[:, :, TOPK : 2 * TOPK]
    all_ancestry = index_arrays[:, :, 2 * TOPK :]

    stacked = jnp.stack([m.transpose(1, 0, 2) for m in (w_gate, w_up, w_down)])
    stacked = stacked.reshape(3, share, experts, weight_rows, H).transpose(1, 0, 2, 3, 4)
    own_weights, other_weights = own_and_other(stacked, core, share)
    starts = [own_weights] + ([swap_core(other_weights)] if share == 2 else [])

    local_project = jnp.concatenate([w_query, w_key, w_value], axis=1)
    local_project, segments_here, starts[0] = tie(local_project, ancestry[:, 0], starts[0])
    own_all = lax.all_gather(segments_here, row_axes, axis=0, tiled=True)
    project = jnp.concatenate(
        [
            lax.all_gather(local_project[:, n : n + 256], row_axes, axis=0, tiled=True)
            for n in range(0, local_project.shape[1], 256)
        ],
        axis=1,
    )
    gain_rows = column_rows(jnp.concatenate([gain_attention, gain_mixture])[None, :])
    gains = gain_rows.reshape(columns, 2, width).transpose(1, 0, 2).reshape(2, D)
    out_columns = jnp.zeros((weight_rows, D), bf16)
    for c, part in [(column, w_out)] + column_shifts(lambda _: w_out):
        out_columns = lax.dynamic_update_slice_in_dim(out_columns, part, c * part.shape[1], 1)
    out_columns, project, own_all = tie(out_columns, project, own_all)
    out_router = lax.all_gather(
        jnp.concatenate([out_columns, w_router], axis=1), row_axes, axis=0, tiled=True
    )

    rounds = gather_rounds(chips, share)
    project, own_all, starts = tie(project, own_all, starts)
    weights_held = run_gather({(h, 0): v for h, v in enumerate(starts)}, rounds[:1])

    token_starts = jnp.stack([(chip * share + (core ^ g)) * rows for g in range(share)]).astype(i32)
    position, path_bits, query_starts, codes = tree_tables(
        all_ancestry, own_all, token_starts, query_block, key_block
    )
    frequency = rope_base ** (-(jnp.arange(HD // 2, dtype=f32) * 2.0) / HD)
    angle = position.astype(f32)[:, None, :] * frequency[None, :, None]
    by_rows = Layout(major_to_minor=(0, 1, 2))
    cosine = with_layout_constraint(jnp.cos(angle), by_rows)
    sine = with_layout_constraint(jnp.sin(angle), by_rows)
    first_expert = (column * (experts * share) + core * experts).astype(i32)
    ranks = slot_ranks(first_expert, all_routes, all_priority, experts)
    rank_columns = ranks.transpose(0, 2, 1)
    expert_ids = jnp.arange(EXPERTS, dtype=i32)
    chosen = jnp.any(all_routes[:, None, :, :] == expert_ids[None, :, None, None], axis=3)

    x_full, weights_held = tie(x_full, weights_held)
    x_wide = x_full.astype(f32)
    inverse_one = lax.rsqrt(jnp.mean(x_wide * x_wide, axis=1, keepdims=True) + epsilon)
    h_one = (x_wide * inverse_one * gains[0][None, :]).astype(bf16)
    key_bits = (jnp.int32(1) << own_all)[None, :]
    h_one, ranks, rank_columns, cosine, sine, path_bits, codes, chosen, key_bits = tie(
        h_one, ranks, rank_columns, cosine, sine, path_bits, codes, chosen, key_bits
    )
    projected = dot_dims(project, h_one, 0, 1)
    query_width, key_width = query_heads * HD, key_heads * HD
    query = rotate(
        projected[:query_width].reshape(share, own_heads, group, HD, rows), cosine[0], sine[0]
    )
    query = (query.astype(bf16).astype(f32) * score_scale).astype(bf16)
    keys = rotate(
        projected[query_width : query_width + key_width].reshape(share, own_heads, HD, rows),
        cosine[0],
        sine[0],
    ).astype(bf16)
    values = projected[query_width + key_width :].reshape(share, own_heads, HD, rows).astype(bf16)
    sent = jnp.concatenate([keys[:, :, None], values[:, :, None], query], axis=2)
    own_sent, other_sent = own_and_other(sent, core, share)
    received = [own_sent] + ([swap_core(other_sent)] if share == 2 else [])
    query_groups = jnp.stack([r[:, 2:] for r in received], axis=1)
    pairs = [r[:, :2].reshape(own_heads, 2 * HD, rows) for r in received]
    pairs, weights_held = tie(pairs, weights_held)
    kv_parts = gather_parts(pairs, chips)
    kv_parts, weights_held = tie(kv_parts, weights_held)
    weights_held = run_gather(weights_held, rounds[1 : len(rounds) - 1])

    attend_outs = [
        attend_forward(
            token_offsets,
            query_starts,
            codes,
            query_groups[head],
            path_bits,
            key_bits,
            [p[head] for p in kv_parts],
        )
        for head in range(own_heads)
    ]
    mixed_b = jnp.stack([o[1] for o in attend_outs])
    mixed_b, weights_held, cotangent_full, out_router = tie(
        mixed_b, weights_held, cotangent_full, out_router
    )
    weights_held = run_gather(weights_held, rounds[len(rounds) - 1 :])
    mixed_other = swap_core(mixed_b[:, 1]) if share == 2 else None
    mixed = in_core_order(mixed_b[:, 0], mixed_other, core).reshape(query_width, rows)
    mixed_full = lax.all_gather(mixed, "col", axis=0, tiled=True)
    mixed_full, weights_held = tie(mixed_full, weights_held)
    mix_grads = groups_of((branch_scale * cotangent_full.astype(f32)).astype(bf16))
    x_middle, h_two, inverse_two = project_out(
        mixed_full, x_full, gains[1:2], out_router
    )
    full_router = out_router[:, D:]
    h_two_groups = groups_of(h_two)

    def gates_of(tokens, picks):
        logits = dot_dims(full_router, tokens, 0, 1)
        shown = jnp.where(picks, logits, masked_score)
        raised = jnp.where(picks, jnp.exp(logits - jnp.max(shown, axis=0, keepdims=True)), 0.0)
        return raised / jnp.sum(raised, axis=0, keepdims=True)

    gates = [gates_of(h_two_groups[g], chosen[g]) for g in range(share)]
    weighted_out, slot_token_grads, inputs, slot_grads, hidden, pair_rows = run_experts(
        feature_offsets,
        first_expert,
        ranks,
        gates,
        h_two_groups,
        mix_grads,
        listed(weights_held, chips),
    )

    def combine_groups(slot_rows):
        if share == 1:
            return combine(rank_columns, slot_rows, 0)
        received = swap_core(combine(rank_columns, slot_rows, 1))
        own = combine(rank_columns, slot_rows, 0)
        return (own.astype(f32) + received.astype(f32)).astype(bf16)

    token_sum = combine_groups(slot_token_grads)
    token_grads = lax.psum_scatter(token_sum, "col", scatter_dimension=0, tiled=True)
    pair_other = swap_core(pair_rows[1, :experts]) if share == 2 else None
    pair_columns = in_core_order(pair_rows[0, :experts], pair_other, core)
    pair_columns = pair_columns.reshape(share * experts, rows)
    pair_grad = column_rows(pair_columns)
    picked_grad = gates[0] * (pair_grad - jnp.sum(gates[0] * pair_grad, axis=0, keepdims=True))
    logit_grad = picked_grad.astype(bf16)
    mix_sum = combine_groups(weighted_out)

    levels = reduce_levels(chips, share)
    first = [[m for m in moves if m[1]] for moves in levels[0]]
    last = [[m for m in moves if not m[1]] for moves in levels[0]]
    parts = expert_grads(feature_offsets, inputs, slot_grads, hidden, chips * share, weight_rows)
    sums_held = {(h, j): parts[j * share + h] for j in range(chips) for h in range(share)}
    first_taken = {}
    for moves in first:
        first_taken.update(take(sums_held, moves))
    staying = [sums_held.pop((h, 0)) for h in range(share)]
    token_grads, staying, mix_sum, logit_grad = tie(token_grads, staying, mix_sum, logit_grad)
    token_grads = token_grads.astype(f32)

    token_start = column * token_block

    def own_tokens(array):
        return lax.dynamic_slice_in_dim(array, token_start, token_block, 0)

    h_two_grad = token_grads + dot_dims(
        lax.dynamic_slice_in_dim(logit_grad, token_start, token_block, 1), full_router, 0, 1
    )
    x_part, inverse_part = own_tokens(x_middle), own_tokens(inverse_two)
    scaled_two = h_two_grad * gains[1][None, :]
    inner_two = jnp.sum(scaled_two * x_part, axis=1, keepdims=True)
    x_middle_grad = (
        own_tokens(cotangent_full).astype(f32)
        + inverse_part * scaled_two
        - x_part * inverse_part**3 * inner_two / D
    )
    gain_mixture_part = jnp.sum(h_two_grad * x_part * inverse_part, axis=0)
    branch_grad = lax.all_gather(
        (branch_scale * x_middle_grad).astype(bf16), "col", axis=0, tiled=True
    )
    sums_held = add_taken(sums_held, first_taken)
    branch_grad, mix_sum, sums_held = tie(branch_grad, mix_sum, sums_held)
    arrived = [[part] for part in staying]
    for rounds_here in levels[1:]:
        passed = {}
        for moves in rounds_here:
            passed.update(take(sums_held, moves))
        for h in range(share):
            if (h, 0) in passed:
                arrived[h].append(passed.pop((h, 0)))
        sums_held = add_taken(sums_held, passed)
    for moves in last:
        for (h, _), part in take(sums_held, moves).items():
            arrived[h].append(part)

    own_out = lax.dynamic_slice_in_dim(out_router, column * query_width, query_width, 1)
    mixed_grad = dot_dims(own_out, branch_grad, 0, 1).astype(bf16)
    own_grad, other_grad = own_and_other(
        mixed_grad.reshape(share, own_heads, group, HD, rows), core, share
    )
    grad_groups = jnp.stack(
        [own_grad] + ([swap_core(other_grad)] if share == 2 else []), axis=1
    )
    backward_outs = [
        attend_backward(
            token_offsets,
            query_starts,
            codes,
            query_groups[head],
            grad_groups[head],
            attend_outs[head][0],
            attend_outs[head][2],
            path_bits,
            key_bits,
            [p[head] for p in kv_parts],
        )
        for head in range(own_heads)
    ]
    mix_slice = lax.psum_scatter(mix_sum, "col", scatter_dimension=1, tiled=True).astype(f32)
    feature_start = column * width
    x_middle_slice = lax.dynamic_slice_in_dim(x_middle, feature_start, width, 1)
    result = (x_middle_slice + branch_scale * mix_slice).astype(bf16)
    backward_outs, arrived, branch_later = tie(backward_outs, arrived, branch_grad)
    query_grad = jnp.stack([o[0] for o in backward_outs])
    query_grad = rotate_back(query_grad, cosine[None, :, None], sine[None, :, None]).astype(bf16)
    query_other = swap_core(query_grad[:, 1]) if share == 2 else None
    query_pre_grad = in_core_order(query_grad[:, 0], query_other, core).reshape(query_width, rows)
    kv_sums = reduce_parts(
        [jnp.stack([o[1][n] for o in backward_outs]) for n in range(chips * share)], chips, share
    )
    kv_other = swap_core(kv_sums[1]) if share == 2 else None
    kv_grad = in_core_order(kv_sums[0], kv_other, core).astype(f32)
    kv_grad = kv_grad.transpose(0, 1, 3, 2).reshape(key_heads, 2 * HD, rows)
    key_pre_grad = (
        rotate_back(kv_grad[:, :HD], cosine[0], sine[0]).astype(bf16).reshape(key_width, rows)
    )
    value_pre_grad = kv_grad[:, HD:].astype(bf16).reshape(key_width, rows)
    project_grad = jnp.concatenate([query_pre_grad, key_pre_grad, value_pre_grad], axis=0)

    (project_grad,) = tie(project_grad)
    h_one_part = dot(project, project_grad).astype(bf16)
    h_one_part, project_grad = tie(h_one_part, project_grad)
    h_one_grad = lax.psum_scatter(h_one_part, "col", scatter_dimension=0, tiled=True)
    inner_one = column_sum(jnp.sum(project_grad.astype(f32) * projected, axis=0))[:, None]
    sums = [functools.reduce(jnp.add, [p.astype(f32) for p in own]).astype(bf16) for own in arrived]
    returned = swap_core(sums[1]) if share == 2 else None
    late = dot_dims(h_one, project_grad, 0, 1)
    early = [dot_dims(branch_later, mixed, 0, 1), dot_dims(h_two, logit_grad, 0, 1)]
    small_grads = jnp.concatenate([late] + early, axis=1).astype(bf16)
    gain_attention_part = jnp.sum(late * project.astype(f32), axis=1) / gains[0]
    gain_parts = jnp.stack([gain_attention_part, gain_mixture_part])

    def own_features(array, c):
        return lax.dynamic_slice_in_dim(array, c * width, width, 1)

    gain_sums = own_features(gain_parts, column)
    for _, other in column_shifts(lambda c: own_features(gain_parts, c)):
        gain_sums = gain_sums + other
    small_held = {
        (h, j): lax.dynamic_slice_in_dim(
            small_grads, places[j * share + h] * weight_rows, weight_rows, 0
        )
        for j in range(chips)
        for h in range(share)
    }
    for rounds_here in levels:
        taken = {}
        for moves in rounds_here:
            taken.update(take(small_held, moves))
        small_held = add_taken(small_held, taken)
    gain_sums = row_sum(gain_sums)
    small_sum = small_held[0, 0].astype(f32)
    if share == 2:
        small_sum = small_sum + swap_core(small_held[1, 0]).astype(f32)
    matrix_grads = [
        in_core_order(sums[0][m], None if returned is None else returned[m], core)
        .astype(f32)
        .reshape(share * experts, weight_rows, H)
        .transpose(1, 0, 2)
        for m in range(3)
    ]
    h_one_grad, matrix_grads, small_sum, gain_sums, inner_one = tie(
        h_one_grad, matrix_grads, small_sum, gain_sums, inner_one
    )
    x_slice = layer_input.astype(f32)
    middle_slice = lax.dynamic_slice_in_dim(branch_grad, feature_start, width, 1).astype(f32)
    input_grad = (
        middle_slice * (1.0 / branch_scale)
        + inverse_one * h_one_grad.astype(f32).T * gain_attention[None, :]
        - x_slice * inverse_one**2 * inner_one / D
    )
    kv_width = query_width + 2 * key_width
    return (
        result,
        input_grad,
        gain_sums[0],
        gain_sums[1],
        small_sum[:, :query_width],
        small_sum[:, query_width : query_width + key_width],
        small_sum[:, query_width + key_width : kv_width],
        small_sum[:, kv_width : kv_width + query_width],
        small_sum[:, kv_width + query_width :],
        *matrix_grads,
    )


def solution(mesh):
    rows, columns = mesh.shape["row"], mesh.shape["col"]
    halves = rows % 2 == 0 and EXPERTS // columns % 2 == 0 and KVH // columns % 2 == 0
    share = 2 if halves else 1
    split = Mesh(mesh.devices.reshape(rows // share, share, columns), ("chip", "core", "col"))
    row = ("chip", "core")
    return jax.shard_map(
        body,
        mesh=split,
        in_specs=(
            P(row, "col"),
            P(row, "col"),
            P("col"),
            P("col"),
            P(row, "col"),
            P(row, "col"),
            P(row, "col"),
            P(row, "col"),
            P(row, None),
            P(row, "col", None),
            P(row, "col", None),
            P(row, "col", None),
            P(row, None),
            P(row, None),
            P(row, None),
        ),
        out_specs=(
            P(row, "col"),
            P(row, "col"),
            P("col"),
            P("col"),
            P(row, "col"),
            P(row, "col"),
            P(row, "col"),
            P(row, "col"),
            P(row, None),
            P(row, "col", None),
            P(row, "col", None),
            P(row, "col", None),
        ),
        check_vma=False,
    )
```

```python
import functools

import jax
import jax.numpy as jnp
from jax import lax
from jax.experimental.layout import Layout, with_layout_constraint
from jax.experimental import pallas as pl
from jax.experimental.pallas import tpu as pltpu
from jax.sharding import Mesh
from jax.sharding import PartitionSpec as P

D = 1536
HD = 64
H = 512
KVH = 8
EXPERTS = 40
TOPK = 8
SEGS = 13
CAP = 230
SLOTS = 256

epsilon = 1e-06
branch_scale = 0.22
score_scale = 0.015625
rope_base = 10000.0
masked_score = -1e30

bf16 = jnp.bfloat16
f32 = jnp.float32
i32 = jnp.int32

QUERY_BLOCK = 512
KEY_BLOCK = 512
VMEM_LIMIT = 60 * 1024 * 1024


def dot(left, right):
    return jnp.dot(left, right, preferred_element_type=f32)


def dot_dims(left, right, left_dim, right_dim):
    return lax.dot_general(
        left, right, (((left_dim,), (right_dim,)), ((), ())), preferred_element_type=f32
    )


def swap(values, axis, bit):
    size = lax.axis_size(axis)
    return lax.ppermute(values, axis, [(i, i ^ bit) for i in range(size)])


def swap_core(values):
    return swap(values, "core", 1)


def chip_bits(chips):
    return [1 << b for b in range(chips.bit_length() - 1)]


def half_bits(chips, half):
    bits = chip_bits(chips)
    return bits if half == 0 else bits[::-1]


def gather_rounds(chips, halves):
    rounds = []
    for level in range(len(chip_bits(chips))):
        moves = []
        for half in range(halves):
            bits = half_bits(chips, half)
            held = [0]
            for bit in bits[:level]:
                held += [j ^ bit for j in held]
            moves.append([(half, j, bits[level]) for j in sorted(held)])
        rounds += [list(r) for r in zip(*moves)]
    return rounds


def run_gather(held, rounds):
    held = dict(held)
    for moves in rounds:
        for half, j, bit in moves:
            held[half, j ^ bit] = swap(held[half, j], "chip", bit)
    return held


def gather_parts(values, chips):
    held = run_gather(
        {(h, 0): v for h, v in enumerate(values)}, gather_rounds(chips, len(values))
    )
    return listed(held, chips)


def listed(held, chips):
    halves = len(held) // chips
    return [held[h, j] for j in range(chips) for h in range(halves)]


def reduce_levels(chips, halves):
    levels = []
    for level in range(len(chip_bits(chips))):
        moves = []
        for half in range(halves):
            bits = half_bits(chips, half)
            done = sum(bits[: level + 1])
            moves.append([(half, j, bits[level]) for j in range(chips) if not j & done])
        levels.append([list(r) for r in zip(*moves)])
    return levels


def take(held, moves):
    return {(h, j): swap(held[h, j ^ bit], "chip", bit) for h, j, bit in moves}


def add_taken(held, taken):
    sums = {k: (held[k].astype(f32) + v.astype(f32)).astype(v.dtype) for k, v in taken.items()}
    return {**held, **sums}


def reduce_parts(parts, chips, share):
    held = {(h, j): parts[j * share + h] for j in range(chips) for h in range(share)}
    for rounds in reduce_levels(chips, share):
        taken = {}
        for moves in rounds:
            taken.update(take(held, moves))
        held = add_taken(held, taken)
    return [held[h, 0] for h in range(share)]


def pick(core, values):
    return jnp.where(core == 0, values[0], values[-1])


def shared_places(chips, share, core):
    chip = lax.axis_index("chip")
    places = []
    for p in range(chips):
        jumps = [
            sum(b for t, b in enumerate(half_bits(chips, k)) if p >> t & 1) for k in range(share)
        ]
        places.append((chip ^ pick(core, jumps)) * share + core)
    return places


def shared_swap(values, level):
    chips, share = lax.axis_size("chip"), lax.axis_size("core")
    pairs = [
        (c * share + k, (c ^ half_bits(chips, k)[level]) * share + k)
        for c in range(chips)
        for k in range(share)
    ]
    return lax.ppermute(values, ("chip", "core"), pairs)


def shared_level(blocks, level):
    return blocks + [shared_swap(b, level) for b in blocks]


def shared_rows(blocks):
    chips, share, core = lax.axis_size("chip"), lax.axis_size("core"), lax.axis_index("core")
    places = shared_places(chips, share, core)
    parts = list(blocks)
    if share == 2:
        parts += [swap_core(b) for b in blocks]
        places = places + shared_places(chips, share, 1 - core)
    rows = blocks[0].shape[0]
    return place_rows(jnp.stack([p * rows for p in places]).astype(i32), parts)


def shared_reduce(values, rows):
    chips, share, core = lax.axis_size("chip"), lax.axis_size("core"), lax.axis_index("core")

    def blocks_of(k):
        return jnp.stack(
            [
                lax.dynamic_slice_in_dim(values, p * rows, rows, 0)
                for p in shared_places(chips, share, k)
            ]
        )

    def add(left, right):
        return (left.astype(f32) + right.astype(f32)).astype(left.dtype)

    held = blocks_of(core)
    if share == 2:
        held = add(held, swap_core(blocks_of(1 - core)))
    for level in reversed(range(len(chip_bits(chips)))):
        half = 1 << level
        held = add(held[:half], shared_swap(held[half:], level))
    return held[0].astype(f32)


def column_shifts(values_for):
    size = lax.axis_size("col")
    me = lax.axis_index("col")
    return [
        (
            (me - d) % size,
            lax.ppermute(values_for((me + d) % size), "col", [(i, (i + d) % size) for i in range(size)]),
        )
        for d in range(1, size)
    ]


def column_sum(values):
    for _, other in column_shifts(lambda _: values):
        values = values + other
    return values


def column_rows(values):
    rows = values.shape[0]
    size = lax.axis_size("col")
    out = jnp.zeros((size * rows,) + values.shape[1:], values.dtype)
    for c, part in [(lax.axis_index("col"), values)] + column_shifts(lambda _: values):
        out = lax.dynamic_update_slice_in_dim(out, part, c * rows, 0)
    return out


def row_sum(values):
    for axis in ("core", "chip"):
        for bit in chip_bits(lax.axis_size(axis)):
            values = values + swap(values, axis, bit)
    return values


def tie(*trees):
    return lax.optimization_barrier(trees)


def own_and_other(values, core, share):
    if share == 1:
        return values[0], None
    mine = lax.dynamic_index_in_dim(values, core, 0, keepdims=False)
    other = lax.dynamic_index_in_dim(values, 1 - core, 0, keepdims=False)
    return mine, other


def in_core_order(mine, other, core):
    if other is None:
        return mine[None]
    first = core == 0
    return jnp.stack([jnp.where(first, mine, other), jnp.where(first, other, mine)])


def column_of(row):
    return jnp.broadcast_to(row, (8, row.shape[1])).T[:, :1]


def attend_forward_kernel(
    offsets, starts, codes, query, path, key_bits, *rest, parts, key_blocks, key_block
):
    kv_parts = rest[:parts]
    out, rounded, log_total, key_columns, value_rows, query_rows, peak, mixed, paths = rest[parts:]
    step = pl.program_id(0)
    heads, width, count = query.shape[1:]

    @pl.when(step == 0)
    def _():
        for n, part in enumerate(kv_parts):
            rows = part.shape[1]
            start = pl.multiple_of(offsets[n], rows)
            key_columns[:, pl.ds(start, rows)] = part[:width, :]
            turned = pltpu.roll(part[...].astype(f32).T, width, 1)
            lane = lax.broadcasted_iota(i32, turned.shape, 1)
            value_rows[pl.ds(start, rows), :] = jnp.where(lane < width, turned, 1.0).astype(bf16)

    for head in range(heads):
        query_rows[head * count : (head + 1) * count] = query[0, head].astype(f32).T.astype(bf16)
    paths[...] = jnp.broadcast_to(path[0], (8, count)).T
    peak[...] = jnp.full_like(peak, masked_score)
    mixed[...] = jnp.zeros_like(mixed)

    def block(number, masked):
        start = pl.multiple_of(number * key_block, key_block)
        scores = dot(query_rows[...], key_columns[:, pl.ds(start, key_block)])
        if masked:
            keys = start + lax.broadcasted_iota(i32, (count, key_block), 1)
            queries = starts[step] + lax.broadcasted_iota(i32, (count, key_block), 0)
            on_path = (paths[:, :1] & key_bits[:, pl.ds(start, key_block)]) != 0
            allowed = on_path & (keys <= queries)
            scores = jnp.where(
                allowed[None], scores.reshape(heads, count, key_block), masked_score
            ).reshape(heads * count, key_block)
        old = peak[...]
        new = jnp.maximum(old, jnp.max(scores, axis=1, keepdims=True))
        weights = jnp.exp(scores - jnp.tile(new, (1, key_block // 128))).astype(bf16)
        mixed[...] = mixed[...] * jnp.exp(old - new) + dot(
            weights, value_rows[pl.ds(start, key_block), :]
        )
        peak[...] = new

    @pl.loop(0, key_blocks)
    def _(number):
        code = codes[step * key_blocks + number]

        @pl.when(code == 1)
        def _():
            block(number, True)

        @pl.when(code == 2)
        def _():
            block(number, False)

    lane = lax.broadcasted_iota(i32, (count, 2 * width), 1)
    for head in range(heads):
        at = slice(head * count, (head + 1) * count)
        sums = mixed[at]
        turned = jnp.where(
            lane < width, sums / pltpu.roll(sums, width, 1), peak[at] + jnp.log(sums)
        ).T
        out[0, head] = turned[:width]
        rounded[0, head] = turned[:width].astype(bf16)
        log_total[0, head] = turned[width : width + 1]


def attend_backward_kernel(
    offsets,
    starts,
    codes,
    query,
    mixed_grad,
    mixed,
    log_total,
    path,
    key_bits,
    *rest,
    parts,
    key_blocks,
    key_block,
):
    kv_parts = rest[:parts]
    query_grad = rest[parts]
    grad_parts = rest[parts + 1 : 2 * parts + 1]
    (kv_rows, key_columns, padded, padded_grad, query_rows, grad_rows, row_terms, query_sum, kv_sum) = (
        rest[2 * parts + 1 :]
    )
    step = pl.program_id(0)
    heads, width, count = query.shape[1:]

    @pl.when(step == 0)
    def _():
        for n, part in enumerate(kv_parts):
            rows = part.shape[1]
            start = pl.multiple_of(offsets[n], rows)
            key_columns[:, pl.ds(start, rows)] = part[:width, :]
            kv_rows[pl.ds(start, rows), :] = part[...].astype(f32).T.astype(bf16)
        padded[...] = jnp.zeros_like(padded)
        padded_grad[...] = jnp.zeros_like(padded_grad)
        kv_sum[...] = jnp.zeros_like(kv_sum)

    for head in range(heads):
        at = slice(head * count, (head + 1) * count)
        padded[:width, at] = query[0, head]
        padded_grad[width:, at] = mixed_grad[0, head]
        row_terms[0:1, at] = log_total[0, head]
        row_terms[1:2, at] = jnp.sum(
            mixed_grad[0, head].astype(f32) * mixed[0, head], axis=0, keepdims=True
        )
    query_rows[...] = padded[...].astype(f32).T.astype(bf16)
    grad_rows[...] = padded_grad[...].astype(f32).T.astype(bf16)
    query_sum[...] = jnp.zeros_like(query_sum)

    def block(number, masked):
        start = pl.multiple_of(number * key_block, key_block)
        rows = kv_rows[pl.ds(start, key_block), :]
        scores = dot(rows, padded[...])
        if masked:
            keys = start + lax.broadcasted_iota(i32, (key_block, count), 0)
            queries = starts[step] + lax.broadcasted_iota(i32, (key_block, count), 1)
            on_path = (path[0] & column_of(key_bits[:, pl.ds(start, key_block)])) != 0
            allowed = on_path & (keys <= queries)
            scores = jnp.where(jnp.concatenate([allowed] * heads, axis=1), scores, masked_score)
        weights = jnp.exp(scores - row_terms[0:1, :])
        weight_grad = dot(rows, padded_grad[...])
        score_grad = (weights * (weight_grad - row_terms[1:2, :])).astype(bf16)
        kv_sum[pl.ds(start, key_block), :] += dot(score_grad, query_rows[...]) + dot(
            weights.astype(bf16), grad_rows[...]
        )
        query_sum[...] += dot(key_columns[:, pl.ds(start, key_block)], score_grad)

    @pl.loop(0, key_blocks)
    def _(number):
        code = codes[step * key_blocks + number]

        @pl.when(code == 1)
        def _():
            block(number, True)

        @pl.when(code == 2)
        def _():
            block(number, False)

    for head in range(heads):
        query_grad[0, head] = score_scale * query_sum[:, head * count : (head + 1) * count]

    @pl.when(step == pl.num_programs(0) - 1)
    def _():
        for n, part in enumerate(grad_parts):
            rows = part.shape[0]
            part[...] = kv_sum[pl.ds(pl.multiple_of(offsets[n], rows), rows), :].astype(part.dtype)


def whole(shape):
    return pl.BlockSpec(shape, lambda *_: (0,) * len(shape), pipeline_mode=pl.Buffered(1))


def attention_specs(heads, rows, block):
    per_group = rows // block

    def four(step, *_):
        return (step // per_group, 0, 0, step % per_group)

    return pl.BlockSpec((1, heads, HD, block), four), pl.BlockSpec((1, heads, 1, block), four)


def attend_forward(offsets, starts, codes, query, path_bits, key_bits, kv_parts):
    groups, heads, _, rows = query.shape
    block = min(QUERY_BLOCK, rows)
    per_group = rows // block
    tokens = key_bits.shape[1]
    key_block = min(KEY_BLOCK, tokens)
    wide, row = attention_specs(heads, rows, block)
    kernel = functools.partial(
        attend_forward_kernel,
        parts=len(kv_parts),
        key_blocks=tokens // key_block,
        key_block=key_block,
    )
    return pl.pallas_call(
        kernel,
        name="attend_forward",
        grid_spec=pltpu.PrefetchScalarGridSpec(
            num_scalar_prefetch=3,
            grid=(groups * per_group,),
            in_specs=[
                wide,
                pl.BlockSpec((1, 1, block), lambda s, *_: (s // per_group, 0, s % per_group)),
                whole(key_bits.shape),
            ]
            + [whole(p.shape) for p in kv_parts],
            out_specs=[wide, wide, row],
            scratch_shapes=[
                pltpu.VMEM((HD, tokens), bf16),
                pltpu.VMEM((tokens, 2 * HD), bf16),
                pltpu.VMEM((heads * block, HD), bf16),
                pltpu.VMEM((heads * block, 2 * HD), f32),
                pltpu.VMEM((heads * block, 2 * HD), f32),
                pltpu.VMEM((block, 8), i32),
            ],
        ),
        out_shape=[
            jax.ShapeDtypeStruct(query.shape, f32),
            jax.ShapeDtypeStruct(query.shape, bf16),
            jax.ShapeDtypeStruct((groups, heads, 1, rows), f32),
        ],
        compiler_params=pltpu.CompilerParams(
            dimension_semantics=("arbitrary",), vmem_limit_bytes=VMEM_LIMIT
        ),
    )(offsets, starts, codes, query, path_bits[:, None, :], key_bits, *kv_parts)


def attend_backward(
    offsets, starts, codes, query, mixed_grad, mixed, log_total, path_bits, key_bits, kv_parts
):
    groups, heads, _, rows = query.shape
    block = min(QUERY_BLOCK, rows)
    per_group = rows // block
    tokens = key_bits.shape[1]
    key_block = min(KEY_BLOCK, tokens)
    wide, row = attention_specs(heads, rows, block)
    grad_shape = (kv_parts[0].shape[1], 2 * HD)
    kernel = functools.partial(
        attend_backward_kernel,
        parts=len(kv_parts),
        key_blocks=tokens // key_block,
        key_block=key_block,
    )
    outs = pl.pallas_call(
        kernel,
        name="attend_backward",
        grid_spec=pltpu.PrefetchScalarGridSpec(
            num_scalar_prefetch=3,
            grid=(groups * per_group,),
            in_specs=[
                wide,
                wide,
                wide,
                row,
                pl.BlockSpec((1, 1, block), lambda s, *_: (s // per_group, 0, s % per_group)),
                whole(key_bits.shape),
            ]
            + [whole(p.shape) for p in kv_parts],
            out_specs=[wide] + [whole(grad_shape) for _ in kv_parts],
            scratch_shapes=[
                pltpu.VMEM((tokens, 2 * HD), bf16),
                pltpu.VMEM((HD, tokens), bf16),
                pltpu.VMEM((2 * HD, heads * block), bf16),
                pltpu.VMEM((2 * HD, heads * block), bf16),
                pltpu.VMEM((heads * block, 2 * HD), bf16),
                pltpu.VMEM((heads * block, 2 * HD), bf16),
                pltpu.VMEM((8, heads * block), f32),
                pltpu.VMEM((HD, heads * block), f32),
                pltpu.VMEM((tokens, 2 * HD), f32),
            ],
        ),
        out_shape=[jax.ShapeDtypeStruct(query.shape, f32)]
        + [jax.ShapeDtypeStruct(grad_shape, bf16) for _ in kv_parts],
        compiler_params=pltpu.CompilerParams(
            dimension_semantics=("arbitrary",), vmem_limit_bytes=VMEM_LIMIT
        ),
    )(
        offsets,
        starts,
        codes,
        query,
        mixed_grad,
        mixed,
        log_total,
        path_bits[:, None, :],
        key_bits,
        *kv_parts,
    )
    return outs[0], outs[1:]


def place_kernel(offsets, *rest):
    parts, out = rest[:-1], rest[-1]
    for n, part in enumerate(parts):
        rows = part.shape[0]
        out[pl.ds(pl.multiple_of(offsets[n], rows), rows), :] = part[...]


def place_rows(offsets, parts):
    rows, width = parts[0].shape
    return pl.pallas_call(
        place_kernel,
        name="place_rows",
        grid_spec=pltpu.PrefetchScalarGridSpec(
            num_scalar_prefetch=1,
            grid=(1,),
            in_specs=[whole(p.shape) for p in parts],
            out_specs=whole((rows * len(parts), width)),
        ),
        out_shape=jax.ShapeDtypeStruct((rows * len(parts), width), parts[0].dtype),
        compiler_params=pltpu.CompilerParams(vmem_limit_bytes=VMEM_LIMIT),
    )(offsets, *parts)


def rank_kernel(first, route_rows, priority_rows, route_columns, priority_columns, out, *, experts):
    rows = route_rows.shape[2]
    never = rows * TOPK
    for e in range(experts):
        expert = first[0] + e
        along = jnp.min(
            jnp.where(route_rows[0] == expert, priority_rows[0], never), axis=0, keepdims=True
        )
        down = jnp.min(
            jnp.where(route_columns[0] == expert, priority_columns[0], never), axis=1, keepdims=True
        )
        count = jnp.zeros((8, rows), i32)
        for begin in range(0, rows, 8):
            count += (down[begin : begin + 8] < along).astype(i32)
        rank = jnp.sum(count, axis=0, keepdims=True)
        out[0, e : e + 1, :] = jnp.where((along < never) & (rank < CAP), rank, -1)
    if out.shape[1] > experts:
        out[0, experts:, :] = jnp.full((out.shape[1] - experts, rows), -1, i32)


def slot_ranks(first, routes, priority, experts):
    groups, rows, _ = routes.shape
    tall = pl.BlockSpec((1, rows, TOPK), lambda g, *_: (g, 0, 0))
    flat = pl.BlockSpec((1, TOPK, rows), lambda g, *_: (g, 0, 0))
    padded = -(-experts // 8) * 8
    return pl.pallas_call(
        functools.partial(rank_kernel, experts=experts),
        name="slot_ranks",
        grid_spec=pltpu.PrefetchScalarGridSpec(
            num_scalar_prefetch=1,
            grid=(groups,),
            in_specs=[flat, flat, tall, tall],
            out_specs=pl.BlockSpec((1, padded, rows), lambda g, *_: (g, 0, 0)),
        ),
        out_shape=jax.ShapeDtypeStruct((groups, padded, rows), i32),
        compiler_params=pltpu.CompilerParams(vmem_limit_bytes=VMEM_LIMIT),
    )(
        first.reshape(1),
        routes.transpose(0, 2, 1),
        priority.transpose(0, 2, 1),
        routes,
        priority,
    )


def expert_kernel(offsets, first, ranks, *rest, parts, groups):
    gates, rest = rest[:groups], rest[groups:]
    tokens, rest = rest[:groups], rest[groups:]
    grads, rest = rest[:groups], rest[groups:]
    weights = rest[:parts]
    weighted_out, token_grad, inputs, slot_grads, hidden, pair_grads, matrices = rest[parts:]
    rows = tokens[0].shape[0]
    e = pl.program_id(0)
    for n, part in enumerate(weights):
        count = part.shape[2]
        for m in range(3):
            matrices[m, pl.ds(pl.multiple_of(offsets[n], count), count), :] = part[m, 0]
    slot = lax.broadcasted_iota(i32, (SLOTS, rows), 0)
    for g in range(groups):
        at = slice(g * SLOTS, (g + 1) * SLOTS)
        inside = slot == ranks[g, pl.ds(e, 1), :]
        pick = inside.astype(bf16)
        gate = gates[g][pl.ds(first[0] + e, 1), :]
        weight = jnp.sum(jnp.where(inside, gate, 0.0), axis=1, keepdims=True)
        picked = dot(pick, tokens[g][...]).astype(bf16)
        inputs[0, at, :] = picked
        gate_pre = dot(picked, matrices[0])
        up_pre = dot(picked, matrices[1])
        sigma = jax.nn.sigmoid(gate_pre)
        silu = gate_pre * sigma
        active = (silu * up_pre).astype(bf16)
        out = dot_dims(active, matrices[2], 1, 1)
        weighted_out[g, 0] = (out * weight).astype(bf16)
        upstream = dot(pick, grads[g][...])
        pair = jnp.sum(upstream * out, axis=1, keepdims=True)
        pair_grads[g, pl.ds(e, 1), :] = jnp.sum(jnp.where(inside, pair, 0.0), axis=0, keepdims=True)
        slot_grad = (weight * upstream).astype(bf16)
        slot_grads[0, at, :] = slot_grad
        act_grad = dot(slot_grad, matrices[2])
        gate_grad = (act_grad * up_pre * sigma * (1.0 + gate_pre * (1.0 - sigma))).astype(bf16)
        up_grad = (act_grad * silu).astype(bf16)
        hidden[0, 0, at, :] = gate_grad
        hidden[0, 1, at, :] = up_grad
        hidden[0, 2, at, :] = active
        token_grad[g, 0] = (
            dot_dims(gate_grad, matrices[0], 1, 1) + dot_dims(up_grad, matrices[1], 1, 1)
        ).astype(bf16)


def run_experts(offsets, first, ranks, gates, tokens, grads, weight_parts):
    groups = len(tokens)
    rows = tokens[0].shape[0]
    _, experts, part_rows, _ = weight_parts[0].shape
    parts = len(weight_parts)
    slots = groups * SLOTS
    by_group = pl.BlockSpec((groups, 1, SLOTS, D), lambda e, *_: (0, e, 0, 0))
    stash = pl.BlockSpec((1, slots, D), lambda e, *_: (e, 0, 0))
    return pl.pallas_call(
        functools.partial(expert_kernel, parts=parts, groups=groups),
        name="experts",
        grid_spec=pltpu.PrefetchScalarGridSpec(
            num_scalar_prefetch=2,
            grid=(experts,),
            in_specs=[whole(ranks.shape)]
            + [whole((EXPERTS, rows)) for _ in range(groups)]
            + [whole((rows, D)) for _ in range(2 * groups)]
            + [pl.BlockSpec((3, 1, part_rows, H), lambda e, *_: (0, e, 0, 0)) for _ in weight_parts],
            out_specs=[
                by_group,
                by_group,
                stash,
                stash,
                pl.BlockSpec((1, 3, slots, H), lambda e, *_: (e, 0, 0, 0)),
                whole(ranks.shape),
            ],
            scratch_shapes=[pltpu.VMEM((3, D, H), bf16)],
        ),
        out_shape=[
            jax.ShapeDtypeStruct((groups, experts, SLOTS, D), bf16),
            jax.ShapeDtypeStruct((groups, experts, SLOTS, D), bf16),
            jax.ShapeDtypeStruct((experts, slots, D), bf16),
            jax.ShapeDtypeStruct((experts, slots, D), bf16),
            jax.ShapeDtypeStruct((experts, 3, slots, H), bf16),
            jax.ShapeDtypeStruct(ranks.shape, f32),
        ],
        compiler_params=pltpu.CompilerParams(
            dimension_semantics=("arbitrary",), vmem_limit_bytes=VMEM_LIMIT
        ),
    )(
        offsets,
        first.reshape(1),
        ranks,
        *gates,
        *tokens,
        *grads,
        *weight_parts,
    )


def expert_grad_kernel(offsets, inputs, slot_grads, hidden, *rest, pieces):
    outs, total = rest[:-1], rest[-1]
    for m in range(3):
        left = inputs if m < 2 else slot_grads
        total[...] = dot_dims(left[0], hidden[0, m], 0, 0)
        for (n, begin), out in zip(pieces, outs):
            if begin <= m < begin + out.shape[0]:
                count = out.shape[2]
                at = pl.ds(pl.multiple_of(offsets[n], count), count)
                out[m - begin, 0] = total[at, :].astype(bf16)


def expert_grads(offsets, inputs, slot_grads, hidden, parts, cut_parts, part_rows):
    experts, slots, _ = inputs.shape
    stash = pl.BlockSpec((1, slots, D), lambda e, *_: (e, 0, 0))
    pieces = []
    for n in range(parts):
        pieces += [(n, 0, 1), (n, 1, 2)] if n in cut_parts else [(n, 0, 3)]
    outs = pl.pallas_call(
        functools.partial(expert_grad_kernel, pieces=[(n, begin) for n, begin, _ in pieces]),
        name="expert_grads",
        grid_spec=pltpu.PrefetchScalarGridSpec(
            num_scalar_prefetch=1,
            grid=(experts,),
            in_specs=[stash, stash, pl.BlockSpec((1, 3, slots, H), lambda e, *_: (e, 0, 0, 0))],
            out_specs=[
                pl.BlockSpec((held, 1, part_rows, H), lambda e, *_: (0, e, 0, 0))
                for _, _, held in pieces
            ],
            scratch_shapes=[pltpu.VMEM((D, H), f32)],
        ),
        out_shape=[
            jax.ShapeDtypeStruct((held, experts, part_rows, H), bf16) for _, _, held in pieces
        ],
        compiler_params=pltpu.CompilerParams(
            dimension_semantics=("arbitrary",), vmem_limit_bytes=VMEM_LIMIT
        ),
    )(offsets, inputs, slot_grads, hidden)
    found = {}
    for (n, _, _), out in zip(pieces, outs):
        found.setdefault(n, []).append(out)
    return [found[n] for n in range(parts)]


def combine_kernel(ranks, rows_in, out, *, experts):
    count = out.shape[0]
    slot = lax.broadcasted_iota(i32, (count, SLOTS), 1)
    pick = jnp.concatenate(
        [(ranks[0, :, e : e + 1] == slot).astype(bf16) for e in range(experts)], axis=1
    )
    out[...] = dot(pick, rows_in[0]).astype(bf16)


def combine(ranks, slot_rows, g):
    groups, rows, columns = ranks.shape
    experts = slot_rows.shape[1]
    block = min(256, rows)
    return pl.pallas_call(
        functools.partial(combine_kernel, experts=experts),
        name="combine",
        grid=(rows // block,),
        in_specs=[
            pl.BlockSpec((1, block, columns), lambda i: (g, i, 0)),
            pl.BlockSpec(
                (1, experts * SLOTS, D), lambda i: (g, 0, 0), pipeline_mode=pl.Buffered(1)
            ),
        ],
        out_specs=pl.BlockSpec((block, D), lambda i: (i, 0)),
        out_shape=jax.ShapeDtypeStruct((rows, D), bf16),
        compiler_params=pltpu.CompilerParams(vmem_limit_bytes=VMEM_LIMIT),
    )(ranks, slot_rows.reshape(groups, experts * SLOTS, D))


def project_kernel(mixed, x, gain, matrix, middle, normed, inverse):
    branch = dot_dims(mixed[...].astype(f32).T.astype(bf16), matrix[:, :D], 1, 1)
    total = x[...].astype(f32) + branch_scale * branch
    scale = lax.rsqrt(jnp.mean(total * total, axis=1, keepdims=True) + epsilon)
    middle[...] = total
    inverse[...] = scale
    normed[...] = (total * scale * gain[...]).astype(bf16)


def project_out(mixed, x, gain, matrix):
    rows = x.shape[0]
    block = min(256, rows)
    tall = pl.BlockSpec((block, D), lambda i: (i, 0))
    return pl.pallas_call(
        project_kernel,
        name="project_out",
        grid=(rows // block,),
        in_specs=[
            pl.BlockSpec((D, block), lambda i: (0, i)),
            tall,
            whole(gain.shape),
            whole(matrix.shape),
        ],
        out_specs=[tall, tall, pl.BlockSpec((block, 1), lambda i: (i, 0))],
        out_shape=[
            jax.ShapeDtypeStruct((rows, D), f32),
            jax.ShapeDtypeStruct((rows, D), bf16),
            jax.ShapeDtypeStruct((rows, 1), f32),
        ],
        compiler_params=pltpu.CompilerParams(
            dimension_semantics=("arbitrary",), vmem_limit_bytes=VMEM_LIMIT
        ),
    )(mixed, x, gain, matrix)


def rotate(values, cosine, sine):
    first = values[..., : HD // 2, :]
    second = values[..., HD // 2 :, :]
    return jnp.concatenate([first * cosine - second * sine, second * cosine + first * sine], axis=-2)


def rotate_back(values, cosine, sine):
    first = values[..., : HD // 2, :]
    second = values[..., HD // 2 :, :]
    return jnp.concatenate([first * cosine + second * sine, second * cosine - first * sine], axis=-2)


def tree_tables(ancestry, own_all, token_starts, query_block, key_block):
    groups, rows, _ = ancestry.shape
    tokens = own_all.shape[0]
    segments = jnp.arange(SEGS, dtype=i32)
    index = jnp.arange(tokens, dtype=i32)
    member = own_all[None, :] == segments[:, None]
    begin = jnp.min(jnp.where(member, index[None, :], tokens), axis=1)
    length = jnp.sum(member.astype(i32), axis=1)
    on_path = jnp.any(ancestry[:, :, :, None] == segments, axis=2)
    at = token_starts[:, None] + jnp.arange(rows, dtype=i32)[None, :]
    before = jnp.clip(at[:, :, None] - begin, 0, length)
    position = jnp.sum(jnp.where(on_path, before, 0), axis=2)
    bits = jnp.sum(on_path.astype(i32) << segments, axis=2)
    blocked = on_path.reshape(groups * rows // query_block, query_block, SEGS)
    path_any = jnp.any(blocked, axis=1)
    path_all = jnp.all(blocked, axis=1)
    keys = jnp.any(member.reshape(SEGS, tokens // key_block, key_block), axis=2).T
    some = jnp.any(path_any[:, None, :] & keys[None, :, :], axis=2)
    every = jnp.all(path_all[:, None, :] | ~keys[None, :, :], axis=2)
    query_start = at.reshape(-1, query_block)[:, 0]
    key_start = jnp.arange(tokens // key_block, dtype=i32) * key_block
    some &= key_start[None, :] < query_start[:, None] + query_block
    every &= key_start[None, :] + key_block <= query_start[:, None] + 1
    codes = jnp.where(some, jnp.where(every, 2, 1), 0).astype(i32)
    return position, bits, query_start, codes.reshape(-1)


def body(
    layer_input,
    cotangent,
    gain_attention,
    gain_mixture,
    w_query,
    w_key,
    w_value,
    w_out,
    w_router,
    w_gate,
    w_up,
    w_down,
    routes,
    priority,
    ancestry,
):
    chips, share, columns = lax.axis_size("chip"), lax.axis_size("core"), lax.axis_size("col")
    chip, core, column = lax.axis_index("chip"), lax.axis_index("core"), lax.axis_index("col")
    row_axes = ("chip", "core")
    rows, width = layer_input.shape
    weight_rows = w_query.shape[0]
    query_heads = w_query.shape[1] // HD
    key_heads = w_key.shape[1] // HD
    group = query_heads // key_heads
    own_heads = key_heads // share
    experts = w_gate.shape[1] // share
    tokens_all = rows * chips * share
    query_block = min(QUERY_BLOCK, rows)
    key_block = min(KEY_BLOCK, tokens_all)
    token_block = rows // columns

    places = [(chip ^ j) * share + (core ^ h) for j in range(chips) for h in range(share)]
    token_offsets = jnp.stack([p * rows for p in places]).astype(i32)
    feature_offsets = jnp.stack([p * weight_rows for p in places]).astype(i32)

    def groups_of(values):
        return [values] + ([swap_core(values)] if share == 2 else [])

    x_full = lax.all_gather(layer_input, "col", axis=1, tiled=True)
    x_full, w_out_here = tie(x_full, w_out)
    out_columns = jnp.zeros((weight_rows, D), bf16)
    for c, part in [(column, w_out_here)] + column_shifts(lambda _: w_out_here):
        out_columns = lax.dynamic_update_slice_in_dim(out_columns, part, c * part.shape[1], 1)
    cotangent_here, out_columns = tie(cotangent, out_columns)
    cotangent_full = lax.all_gather(cotangent_here, "col", axis=1, tiled=True)
    index_groups = groups_of(jnp.concatenate([routes, priority, ancestry], axis=1))
    index_arrays = jnp.stack(index_groups)

    own_all = lax.all_gather(ancestry[:, 0], row_axes, axis=0, tiled=True)
    project_part = jnp.concatenate([w_query, w_key, w_value], axis=1)
    own_all, project_part = tie(own_all, project_part)
    levels_here = range(len(chip_bits(chips)))
    project_parts = [project_part]
    for level in levels_here:
        project_parts = shared_level(project_parts, level)

    stacked = jnp.stack([m.transpose(1, 0, 2) for m in (w_gate, w_up, w_down)])
    stacked = stacked.reshape(3, share, experts, weight_rows, H).transpose(1, 0, 2, 3, 4)
    own_weights, other_weights = own_and_other(stacked, core, share)
    starts = [own_weights] + ([swap_core(other_weights)] if share == 2 else [])
    project_parts, starts, index_arrays = tie(project_parts, starts, index_arrays)
    all_routes = index_arrays[:, :, :TOPK]
    all_priority = index_arrays[:, :, TOPK : 2 * TOPK]
    all_ancestry = index_arrays[:, :, 2 * TOPK :]
    project = shared_rows(project_parts)
    rounds = gather_rounds(chips, share)
    weights_held = run_gather({(h, 0): v for h, v in enumerate(starts)}, rounds[:1])
    gains = column_rows(jnp.concatenate([gain_attention, gain_mixture])[None, :])
    gains = gains.reshape(columns, 2, width).transpose(1, 0, 2).reshape(2, D)

    token_starts = jnp.stack([(chip * share + (core ^ g)) * rows for g in range(share)]).astype(i32)
    position, path_bits, query_starts, codes = tree_tables(
        all_ancestry, own_all, token_starts, query_block, key_block
    )
    frequency = rope_base ** (-(jnp.arange(HD // 2, dtype=f32) * 2.0) / HD)
    angle = position.astype(f32)[:, None, :] * frequency[None, :, None]
    by_rows = Layout(major_to_minor=(0, 1, 2))
    cosine = with_layout_constraint(jnp.cos(angle), by_rows)
    sine = with_layout_constraint(jnp.sin(angle), by_rows)
    first_expert = (column * (experts * share) + core * experts).astype(i32)
    ranks = slot_ranks(first_expert, all_routes, all_priority, experts)
    rank_columns = ranks.transpose(0, 2, 1)
    expert_ids = jnp.arange(EXPERTS, dtype=i32)
    chosen = jnp.any(all_routes[:, None, :, :] == expert_ids[None, :, None, None], axis=3)

    key_bits = (jnp.int32(1) << own_all)[None, :]
    tables = (ranks, rank_columns, cosine, sine, path_bits, codes, chosen, key_bits, project, gains)
    out_parts = [jnp.concatenate([out_columns, w_router], axis=1)]
    out_parts = shared_level(out_parts, 0)
    x_full, weights_held, tables, out_parts = tie(x_full, weights_held, tables, out_parts)
    ranks, rank_columns, cosine, sine, path_bits, codes, chosen, key_bits, project, gains = tables
    x_wide = x_full.astype(f32)
    inverse_one = lax.rsqrt(jnp.mean(x_wide * x_wide, axis=1, keepdims=True) + epsilon)
    h_one = (x_wide * inverse_one * gains[0][None, :]).astype(bf16)
    projected = dot_dims(project, h_one, 0, 1)
    query_width, key_width = query_heads * HD, key_heads * HD
    query = rotate(
        projected[:query_width].reshape(share, own_heads, group, HD, rows), cosine[0], sine[0]
    )
    query = (query.astype(bf16).astype(f32) * score_scale).astype(bf16)
    keys = rotate(
        projected[query_width : query_width + key_width].reshape(share, own_heads, HD, rows),
        cosine[0],
        sine[0],
    ).astype(bf16)
    values = projected[query_width + key_width :].reshape(share, own_heads, HD, rows).astype(bf16)
    sent = jnp.concatenate([keys[:, :, None], values[:, :, None], query], axis=2)
    own_sent, other_sent = own_and_other(sent, core, share)
    received = [own_sent] + ([swap_core(other_sent)] if share == 2 else [])
    query_groups = jnp.stack([r[:, 2:] for r in received], axis=1)
    pairs = [r[:, :2].reshape(own_heads, 2 * HD, rows) for r in received]
    for level in levels_here[1:]:
        out_parts = shared_level(out_parts, level)
    pairs, weights_held, out_parts = tie(pairs, weights_held, out_parts)
    kv_parts = gather_parts(pairs, chips)
    kv_parts, weights_held = tie(kv_parts, weights_held)
    weights_held = run_gather(weights_held, rounds[1 : len(rounds) - 1])

    attend_outs = [
        attend_forward(
            token_offsets,
            query_starts,
            codes,
            query_groups[head],
            path_bits,
            key_bits,
            [p[head] for p in kv_parts],
        )
        for head in range(own_heads)
    ]
    mixed_b = jnp.stack([o[1] for o in attend_outs])
    mixed_b, weights_held, cotangent_full, out_parts = tie(
        mixed_b, weights_held, cotangent_full, out_parts
    )
    out_router = shared_rows(out_parts)
    weights_held = run_gather(weights_held, rounds[len(rounds) - 1 :])
    mixed_other = swap_core(mixed_b[:, 1]) if share == 2 else None
    mixed = in_core_order(mixed_b[:, 0], mixed_other, core).reshape(query_width, rows)
    mixed_full = lax.all_gather(mixed, "col", axis=0, tiled=True)
    mixed_full, weights_held, out_router = tie(mixed_full, weights_held, out_router)
    mix_grads = groups_of((branch_scale * cotangent_full.astype(f32)).astype(bf16))
    x_middle, h_two, inverse_two = project_out(
        mixed_full, x_full, gains[1:2], out_router
    )
    full_router = out_router[:, D:]
    h_two_groups = groups_of(h_two)

    def gates_of(tokens, picks):
        logits = dot_dims(full_router, tokens, 0, 1)
        shown = jnp.where(picks, logits, masked_score)
        raised = jnp.where(picks, jnp.exp(logits - jnp.max(shown, axis=0, keepdims=True)), 0.0)
        return raised / jnp.sum(raised, axis=0, keepdims=True)

    gates = [gates_of(h_two_groups[g], chosen[g]) for g in range(share)]
    weighted_out, slot_token_grads, inputs, slot_grads, hidden, pair_rows = run_experts(
        feature_offsets,
        first_expert,
        ranks,
        gates,
        h_two_groups,
        mix_grads,
        listed(weights_held, chips),
    )

    def combine_groups(slot_rows):
        if share == 1:
            return combine(rank_columns, slot_rows, 0)
        received = swap_core(combine(rank_columns, slot_rows, 1))
        own = combine(rank_columns, slot_rows, 0)
        return (own.astype(f32) + received.astype(f32)).astype(bf16)

    token_sum = combine_groups(slot_token_grads)
    token_grads = lax.psum_scatter(token_sum, "col", scatter_dimension=0, tiled=True)
    pair_other = swap_core(pair_rows[1, :experts]) if share == 2 else None
    pair_columns = in_core_order(pair_rows[0, :experts], pair_other, core)
    pair_columns = pair_columns.reshape(share * experts, rows)
    pair_grad = column_rows(pair_columns)
    picked_grad = gates[0] * (pair_grad - jnp.sum(gates[0] * pair_grad, axis=0, keepdims=True))
    logit_grad = picked_grad.astype(bf16)
    mix_sum = combine_groups(weighted_out)

    levels = reduce_levels(chips, share)
    first = [[m for m in moves if m[1]] for moves in levels[0]]
    last = [[m for m in moves if not m[1]] for moves in levels[0]]
    sent = {(h, j ^ bit) for moves in first for h, j, bit in moves}
    last_sent = {(h, j ^ bit) for moves in last for h, j, bit in moves}
    parts = expert_grads(
        feature_offsets,
        inputs,
        slot_grads,
        hidden,
        chips * share,
        {j * share + h for h, j in sent | last_sent},
        weight_rows,
    )
    sums_held = {(h, j): parts[j * share + h] for j in range(chips) for h in range(share)}

    def take_piece(rounds_here, held):
        taken = {}
        for moves in rounds_here:
            taken.update(take(held, moves))
        return taken

    first_taken = take_piece(first, {k: sums_held[k][0] for k in sent})
    staying = [sums_held[h, 0][0] for h in range(share)]
    token_grads, staying, mix_sum, logit_grad, first_taken = tie(
        token_grads, staying, mix_sum, logit_grad, first_taken
    )
    token_grads = token_grads.astype(f32)
    second_taken = take_piece(first, {k: sums_held[k][1] for k in sent})

    token_start = column * token_block

    def own_tokens(array):
        return lax.dynamic_slice_in_dim(array, token_start, token_block, 0)

    h_two_grad = token_grads + dot_dims(
        lax.dynamic_slice_in_dim(logit_grad, token_start, token_block, 1), full_router, 0, 1
    )
    x_part, inverse_part = own_tokens(x_middle), own_tokens(inverse_two)
    scaled_two = h_two_grad * gains[1][None, :]
    inner_two = jnp.sum(scaled_two * x_part, axis=1, keepdims=True)
    x_middle_grad = (
        own_tokens(cotangent_full).astype(f32)
        + inverse_part * scaled_two
        - x_part * inverse_part**3 * inner_two / D
    )
    gain_mixture_part = jnp.sum(h_two_grad * x_part * inverse_part, axis=0)
    branch_part = (branch_scale * x_middle_grad).astype(bf16)
    mixed_parts = dot(branch_part, out_router[:, :D]).astype(bf16)
    mixed_parts = mixed_parts.reshape(token_block, columns, query_width).transpose(1, 0, 2)
    mixed_grad = lax.all_to_all(mixed_parts, "col", split_axis=0, concat_axis=0, tiled=True)
    mixed_grad, branch_part, mix_sum, second_taken = tie(
        mixed_grad, branch_part, mix_sum, second_taken
    )
    branch_grad = lax.all_gather(branch_part, "col", axis=0, tiled=True)
    sums_here = {}
    for k, part in first_taken.items():
        taken = jnp.concatenate([part, second_taken[k]])
        sums_here[k] = (sums_held[k][0].astype(f32) + taken.astype(f32)).astype(bf16)

    mixed_grad = mixed_grad.reshape(rows, query_width).T
    mixed_grad, sums_here = tie(mixed_grad, sums_here)
    own_grad, other_grad = own_and_other(
        mixed_grad.reshape(share, own_heads, group, HD, rows), core, share
    )
    arrived = [[part] for part in staying]
    for rounds_here in levels[1:]:
        passed = {}
        for moves in rounds_here:
            passed.update(take(sums_here, moves))
        for h in range(share):
            if (h, 0) in passed:
                arrived[h].append(passed.pop((h, 0)))
        sums_here = add_taken(sums_here, passed)
    last_begin = {k: sums_held[k][0] for k in last_sent}
    last_rest = {k: sums_held[k][1] for k in last_sent}
    last_rest, own_grad = tie(last_rest, own_grad)
    last_rest = take_piece(last, last_rest)
    grad_groups = jnp.stack(
        [own_grad] + ([swap_core(other_grad)] if share == 2 else []), axis=1
    )
    backward_outs = [
        attend_backward(
            token_offsets,
            query_starts,
            codes,
            query_groups[head],
            grad_groups[head],
            attend_outs[head][0],
            attend_outs[head][2],
            path_bits,
            key_bits,
            [p[head] for p in kv_parts],
        )
        for head in range(own_heads)
    ]
    mix_slice = lax.psum_scatter(mix_sum, "col", scatter_dimension=1, tiled=True).astype(f32)
    feature_start = column * width
    x_middle_slice = lax.dynamic_slice_in_dim(x_middle, feature_start, width, 1)
    result = (x_middle_slice + branch_scale * mix_slice).astype(bf16)
    backward_outs, arrived, branch_later, last_rest = tie(
        backward_outs, arrived, branch_grad, last_rest
    )
    query_grad = jnp.stack([o[0] for o in backward_outs])
    query_grad = rotate_back(query_grad, cosine[None, :, None], sine[None, :, None]).astype(bf16)
    query_other = swap_core(query_grad[:, 1]) if share == 2 else None
    query_pre_grad = in_core_order(query_grad[:, 0], query_other, core).reshape(query_width, rows)
    kv_sums = reduce_parts(
        [jnp.stack([o[1][n] for o in backward_outs]) for n in range(chips * share)], chips, share
    )
    kv_other = swap_core(kv_sums[1]) if share == 2 else None
    kv_grad = in_core_order(kv_sums[0], kv_other, core).astype(f32)
    kv_grad, last_begin = tie(kv_grad, last_begin)
    last_begin = take_piece(last, last_begin)
    for h in range(share):
        for k in last_rest:
            if k[0] == h:
                arrived[h].append(jnp.concatenate([last_begin[k], last_rest[k]]))
    kv_grad = kv_grad.transpose(0, 1, 3, 2).reshape(key_heads, 2 * HD, rows)
    key_pre_grad = (
        rotate_back(kv_grad[:, :HD], cosine[0], sine[0]).astype(bf16).reshape(key_width, rows)
    )
    value_pre_grad = kv_grad[:, HD:].astype(bf16).reshape(key_width, rows)
    project_grad = jnp.concatenate([query_pre_grad, key_pre_grad, value_pre_grad], axis=0)

    (project_grad,) = tie(project_grad)
    h_one_part = dot(project, project_grad).astype(bf16)
    h_one_part, project_grad = tie(h_one_part, project_grad)
    h_one_grad = lax.psum_scatter(h_one_part, "col", scatter_dimension=0, tiled=True)
    inner_one = column_sum(jnp.sum(project_grad.astype(f32) * projected, axis=0))[:, None]
    sums = [functools.reduce(jnp.add, [p.astype(f32) for p in own]).astype(bf16) for own in arrived]
    returned = swap_core(sums[1]) if share == 2 else None
    late = dot_dims(h_one, project_grad, 0, 1)
    early = [dot_dims(branch_later, mixed, 0, 1), dot_dims(h_two, logit_grad, 0, 1)]
    small_grads = jnp.concatenate([late] + early, axis=1).astype(bf16)
    gain_attention_part = jnp.sum(late * project.astype(f32), axis=1) / gains[0]
    gain_parts = jnp.stack([gain_attention_part, gain_mixture_part])

    def own_features(array, c):
        return lax.dynamic_slice_in_dim(array, c * width, width, 1)

    gain_sums = own_features(gain_parts, column)
    for _, other in column_shifts(lambda c: own_features(gain_parts, c)):
        gain_sums = gain_sums + other
    small_sum = shared_reduce(small_grads, weight_rows)
    gain_sums = row_sum(gain_sums)
    matrix_grads = [
        in_core_order(sums[0][m], None if returned is None else returned[m], core)
        .astype(f32)
        .reshape(share * experts, weight_rows, H)
        .transpose(1, 0, 2)
        for m in range(3)
    ]
    h_one_grad, matrix_grads, small_sum, gain_sums, inner_one = tie(
        h_one_grad, matrix_grads, small_sum, gain_sums, inner_one
    )
    x_slice = layer_input.astype(f32)
    middle_slice = lax.dynamic_slice_in_dim(branch_grad, feature_start, width, 1).astype(f32)
    input_grad = (
        middle_slice * (1.0 / branch_scale)
        + inverse_one * h_one_grad.astype(f32).T * gain_attention[None, :]
        - x_slice * inverse_one**2 * inner_one / D
    )
    kv_width = query_width + 2 * key_width
    return (
        result,
        input_grad,
        gain_sums[0],
        gain_sums[1],
        small_sum[:, :query_width],
        small_sum[:, query_width : query_width + key_width],
        small_sum[:, query_width + key_width : kv_width],
        small_sum[:, kv_width : kv_width + query_width],
        small_sum[:, kv_width + query_width :],
        *matrix_grads,
    )


def solution(mesh):
    rows, columns = mesh.shape["row"], mesh.shape["col"]
    halves = rows % 2 == 0 and EXPERTS // columns % 2 == 0 and KVH // columns % 2 == 0
    share = 2 if halves else 1
    split = Mesh(mesh.devices.reshape(rows // share, share, columns), ("chip", "core", "col"))
    row = ("chip", "core")
    return jax.shard_map(
        body,
        mesh=split,
        in_specs=(
            P(row, "col"),
            P(row, "col"),
            P("col"),
            P("col"),
            P(row, "col"),
            P(row, "col"),
            P(row, "col"),
            P(row, "col"),
            P(row, None),
            P(row, "col", None),
            P(row, "col", None),
            P(row, "col", None),
            P(row, None),
            P(row, None),
            P(row, None),
        ),
        out_specs=(
            P(row, "col"),
            P(row, "col"),
            P("col"),
            P("col"),
            P(row, "col"),
            P(row, "col"),
            P(row, "col"),
            P(row, "col"),
            P(row, None),
            P(row, "col", None),
            P(row, "col", None),
            P(row, "col", None),
        ),
        check_vma=False,
    )
```

```python
import functools

import jax
import jax.numpy as jnp
from jax import lax
from jax.experimental.layout import Layout, with_layout_constraint
from jax.experimental import pallas as pl
from jax.experimental.pallas import tpu as pltpu
from jax.sharding import Mesh
from jax.sharding import PartitionSpec as P

D = 1536
HD = 64
H = 512
KVH = 8
EXPERTS = 40
TOPK = 8
SEGS = 13
CAP = 230
SLOTS = 256

epsilon = 1e-06
branch_scale = 0.22
score_scale = 0.015625
rope_base = 10000.0
masked_score = -1e30

bf16 = jnp.bfloat16
f32 = jnp.float32
i32 = jnp.int32

QUERY_BLOCK = 512
KEY_BLOCK = 512
VMEM_LIMIT = 60 * 1024 * 1024


def dot(left, right):
    return jnp.dot(left, right, preferred_element_type=f32)


def dot_dims(left, right, left_dim, right_dim):
    return lax.dot_general(
        left, right, (((left_dim,), (right_dim,)), ((), ())), preferred_element_type=f32
    )


def swap(values, axis, bit):
    size = lax.axis_size(axis)
    return lax.ppermute(values, axis, [(i, i ^ bit) for i in range(size)])


def swap_core(values):
    return swap(values, "core", 1)


def chip_bits(chips):
    return [1 << b for b in range(chips.bit_length() - 1)]


def half_bits(chips, half):
    bits = chip_bits(chips)
    return bits if half == 0 else bits[::-1]


def gather_rounds(chips, halves):
    rounds = []
    for level in range(len(chip_bits(chips))):
        moves = []
        for half in range(halves):
            bits = half_bits(chips, half)
            held = [0]
            for bit in bits[:level]:
                held += [j ^ bit for j in held]
            moves.append([(half, j, bits[level]) for j in sorted(held)])
        rounds += [list(r) for r in zip(*moves)]
    return rounds


def run_gather(held, rounds):
    held = dict(held)
    for moves in rounds:
        for half, j, bit in moves:
            held[half, j ^ bit] = swap(held[half, j], "chip", bit)
    return held


def gather_parts(values, chips):
    held = run_gather(
        {(h, 0): v for h, v in enumerate(values)}, gather_rounds(chips, len(values))
    )
    return listed(held, chips)


def listed(held, chips):
    halves = len(held) // chips
    return [held[h, j] for j in range(chips) for h in range(halves)]


def reduce_levels(chips, halves):
    levels = []
    for level in range(len(chip_bits(chips))):
        moves = []
        for half in range(halves):
            bits = half_bits(chips, half)
            done = sum(bits[: level + 1])
            moves.append([(half, j, bits[level]) for j in range(chips) if not j & done])
        levels.append([list(r) for r in zip(*moves)])
    return levels


def take(held, moves):
    return {(h, j): swap(held[h, j ^ bit], "chip", bit) for h, j, bit in moves}


def add_taken(held, taken):
    sums = {k: (held[k].astype(f32) + v.astype(f32)).astype(v.dtype) for k, v in taken.items()}
    return {**held, **sums}


def reduce_parts(parts, chips, share):
    held = {(h, j): parts[j * share + h] for j in range(chips) for h in range(share)}
    for rounds in reduce_levels(chips, share):
        taken = {}
        for moves in rounds:
            taken.update(take(held, moves))
        held = add_taken(held, taken)
    return [held[h, 0] for h in range(share)]


def pick(core, values):
    return jnp.where(core == 0, values[0], values[-1])


def shared_places(chips, share, core):
    chip = lax.axis_index("chip")
    places = []
    for p in range(chips):
        jumps = [
            sum(b for t, b in enumerate(half_bits(chips, k)) if p >> t & 1) for k in range(share)
        ]
        places.append((chip ^ pick(core, jumps)) * share + core)
    return places


def shared_swap(values, level):
    chips, share = lax.axis_size("chip"), lax.axis_size("core")
    pairs = [
        (c * share + k, (c ^ half_bits(chips, k)[level]) * share + k)
        for c in range(chips)
        for k in range(share)
    ]
    return lax.ppermute(values, ("chip", "core"), pairs)


def shared_level(blocks, level):
    return blocks + [shared_swap(b, level) for b in blocks]


def shared_rows(blocks):
    chips, share, core = lax.axis_size("chip"), lax.axis_size("core"), lax.axis_index("core")
    places = shared_places(chips, share, core)
    parts = list(blocks)
    if share == 2:
        parts += [swap_core(b) for b in blocks]
        places = places + shared_places(chips, share, 1 - core)
    rows = blocks[0].shape[0]
    return place_rows(jnp.stack([p * rows for p in places]).astype(i32), parts)


def shared_reduce(held, other):
    def add(left, right):
        return (left.astype(f32) + right.astype(f32)).astype(left.dtype)

    if other is not None:
        held = add(held, swap_core(other))
    for level in reversed(range(len(chip_bits(lax.axis_size("chip"))))):
        half = 1 << level
        held = add(held[:half], shared_swap(held[half:], level))
    return held[0].astype(f32)


def column_shifts(values_for):
    size = lax.axis_size("col")
    me = lax.axis_index("col")
    return [
        (
            (me - d) % size,
            lax.ppermute(values_for((me + d) % size), "col", [(i, (i + d) % size) for i in range(size)]),
        )
        for d in range(1, size)
    ]


def column_sum(values):
    for _, other in column_shifts(lambda _: values):
        values = values + other
    return values


def column_rows(values):
    rows = values.shape[0]
    size = lax.axis_size("col")
    out = jnp.zeros((size * rows,) + values.shape[1:], values.dtype)
    for c, part in [(lax.axis_index("col"), values)] + column_shifts(lambda _: values):
        out = lax.dynamic_update_slice_in_dim(out, part, c * rows, 0)
    return out


def row_sum(values):
    for axis in ("core", "chip"):
        for bit in chip_bits(lax.axis_size(axis)):
            values = values + swap(values, axis, bit)
    return values


def tie(*trees):
    return lax.optimization_barrier(trees)


def own_and_other(values, core, share):
    if share == 1:
        return values[0], None
    mine = lax.dynamic_index_in_dim(values, core, 0, keepdims=False)
    other = lax.dynamic_index_in_dim(values, 1 - core, 0, keepdims=False)
    return mine, other


def in_core_order(mine, other, core):
    if other is None:
        return mine[None]
    first = core == 0
    return jnp.stack([jnp.where(first, mine, other), jnp.where(first, other, mine)])


def column_of(row):
    return jnp.broadcast_to(row, (8, row.shape[1])).T[:, :1]


def attend_forward_kernel(
    offsets, starts, codes, query, path, key_bits, *rest, parts, key_blocks, key_block
):
    kv_parts = rest[:parts]
    out, rounded, log_total, key_columns, value_rows, query_rows, peak, mixed, paths = rest[parts:]
    step = pl.program_id(0)
    heads, width, count = query.shape[1:]

    @pl.when(step == 0)
    def _():
        for n, part in enumerate(kv_parts):
            rows = part.shape[1]
            start = pl.multiple_of(offsets[n], rows)
            key_columns[:, pl.ds(start, rows)] = part[:width, :]
            turned = pltpu.roll(part[...].astype(f32).T, width, 1)
            lane = lax.broadcasted_iota(i32, turned.shape, 1)
            value_rows[pl.ds(start, rows), :] = jnp.where(lane < width, turned, 1.0).astype(bf16)

    for head in range(heads):
        query_rows[head * count : (head + 1) * count] = query[0, head].astype(f32).T.astype(bf16)
    paths[...] = jnp.broadcast_to(path[0], (8, count)).T
    peak[...] = jnp.full_like(peak, masked_score)
    mixed[...] = jnp.zeros_like(mixed)

    def block(number, masked):
        start = pl.multiple_of(number * key_block, key_block)
        scores = dot(query_rows[...], key_columns[:, pl.ds(start, key_block)])
        if masked:
            keys = start + lax.broadcasted_iota(i32, (count, key_block), 1)
            queries = starts[step] + lax.broadcasted_iota(i32, (count, key_block), 0)
            on_path = (paths[:, :1] & key_bits[:, pl.ds(start, key_block)]) != 0
            allowed = on_path & (keys <= queries)
            scores = jnp.where(
                allowed[None], scores.reshape(heads, count, key_block), masked_score
            ).reshape(heads * count, key_block)
        old = peak[...]
        new = jnp.maximum(old, jnp.max(scores, axis=1, keepdims=True))
        weights = jnp.exp(scores - jnp.tile(new, (1, key_block // 128))).astype(bf16)
        mixed[...] = mixed[...] * jnp.exp(old - new) + dot(
            weights, value_rows[pl.ds(start, key_block), :]
        )
        peak[...] = new

    @pl.loop(0, key_blocks)
    def _(number):
        code = codes[step * key_blocks + number]

        @pl.when(code == 1)
        def _():
            block(number, True)

        @pl.when(code == 2)
        def _():
            block(number, False)

    lane = lax.broadcasted_iota(i32, (count, 2 * width), 1)
    for head in range(heads):
        at = slice(head * count, (head + 1) * count)
        sums = mixed[at]
        turned = jnp.where(
            lane < width, sums / pltpu.roll(sums, width, 1), peak[at] + jnp.log(sums)
        ).T
        out[0, head] = turned[:width]
        rounded[0, head] = turned[:width].astype(bf16)
        log_total[0, head] = turned[width : width + 1]


def attend_backward_kernel(
    offsets,
    starts,
    codes,
    query,
    mixed_grad,
    mixed,
    log_total,
    path,
    key_bits,
    *rest,
    parts,
    key_blocks,
    key_block,
):
    kv_parts = rest[:parts]
    query_grad = rest[parts]
    grad_parts = rest[parts + 1 : 2 * parts + 1]
    (kv_rows, key_columns, padded, padded_grad, query_rows, grad_rows, row_terms, query_sum, kv_sum) = (
        rest[2 * parts + 1 :]
    )
    step = pl.program_id(0)
    heads, width, count = query.shape[1:]

    @pl.when(step == 0)
    def _():
        for n, part in enumerate(kv_parts):
            rows = part.shape[1]
            start = pl.multiple_of(offsets[n], rows)
            key_columns[:, pl.ds(start, rows)] = part[:width, :]
            kv_rows[pl.ds(start, rows), :] = part[...].astype(f32).T.astype(bf16)
        padded[...] = jnp.zeros_like(padded)
        padded_grad[...] = jnp.zeros_like(padded_grad)
        kv_sum[...] = jnp.zeros_like(kv_sum)

    for head in range(heads):
        at = slice(head * count, (head + 1) * count)
        padded[:width, at] = query[0, head]
        padded_grad[width:, at] = mixed_grad[0, head]
        row_terms[0:1, at] = log_total[0, head]
        row_terms[1:2, at] = jnp.sum(
            mixed_grad[0, head].astype(f32) * mixed[0, head], axis=0, keepdims=True
        )
    query_rows[...] = padded[...].astype(f32).T.astype(bf16)
    grad_rows[...] = padded_grad[...].astype(f32).T.astype(bf16)
    query_sum[...] = jnp.zeros_like(query_sum)

    def block(number, masked):
        start = pl.multiple_of(number * key_block, key_block)
        rows = kv_rows[pl.ds(start, key_block), :]
        scores = dot(rows, padded[...])
        if masked:
            keys = start + lax.broadcasted_iota(i32, (key_block, count), 0)
            queries = starts[step] + lax.broadcasted_iota(i32, (key_block, count), 1)
            on_path = (path[0] & column_of(key_bits[:, pl.ds(start, key_block)])) != 0
            allowed = on_path & (keys <= queries)
            scores = jnp.where(jnp.concatenate([allowed] * heads, axis=1), scores, masked_score)
        weights = jnp.exp(scores - row_terms[0:1, :])
        weight_grad = dot(rows, padded_grad[...])
        score_grad = (weights * (weight_grad - row_terms[1:2, :])).astype(bf16)
        kv_sum[pl.ds(start, key_block), :] += dot(score_grad, query_rows[...]) + dot(
            weights.astype(bf16), grad_rows[...]
        )
        query_sum[...] += dot(key_columns[:, pl.ds(start, key_block)], score_grad)

    @pl.loop(0, key_blocks)
    def _(number):
        code = codes[step * key_blocks + number]

        @pl.when(code == 1)
        def _():
            block(number, True)

        @pl.when(code == 2)
        def _():
            block(number, False)

    for head in range(heads):
        query_grad[0, head] = score_scale * query_sum[:, head * count : (head + 1) * count]

    @pl.when(step == pl.num_programs(0) - 1)
    def _():
        for n, part in enumerate(grad_parts):
            rows = part.shape[0]
            part[...] = kv_sum[pl.ds(pl.multiple_of(offsets[n], rows), rows), :].astype(part.dtype)


def whole(shape):
    return pl.BlockSpec(shape, lambda *_: (0,) * len(shape), pipeline_mode=pl.Buffered(1))


def attention_specs(heads, rows, block):
    per_group = rows // block

    def four(step, *_):
        return (step // per_group, 0, 0, step % per_group)

    return pl.BlockSpec((1, heads, HD, block), four), pl.BlockSpec((1, heads, 1, block), four)


def attend_forward(offsets, starts, codes, query, path_bits, key_bits, kv_parts):
    groups, heads, _, rows = query.shape
    block = min(QUERY_BLOCK, rows)
    per_group = rows // block
    tokens = key_bits.shape[1]
    key_block = min(KEY_BLOCK, tokens)
    wide, row = attention_specs(heads, rows, block)
    kernel = functools.partial(
        attend_forward_kernel,
        parts=len(kv_parts),
        key_blocks=tokens // key_block,
        key_block=key_block,
    )
    return pl.pallas_call(
        kernel,
        name="attend_forward",
        grid_spec=pltpu.PrefetchScalarGridSpec(
            num_scalar_prefetch=3,
            grid=(groups * per_group,),
            in_specs=[
                wide,
                pl.BlockSpec((1, 1, block), lambda s, *_: (s // per_group, 0, s % per_group)),
                whole(key_bits.shape),
            ]
            + [whole(p.shape) for p in kv_parts],
            out_specs=[wide, wide, row],
            scratch_shapes=[
                pltpu.VMEM((HD, tokens), bf16),
                pltpu.VMEM((tokens, 2 * HD), bf16),
                pltpu.VMEM((heads * block, HD), bf16),
                pltpu.VMEM((heads * block, 2 * HD), f32),
                pltpu.VMEM((heads * block, 2 * HD), f32),
                pltpu.VMEM((block, 8), i32),
            ],
        ),
        out_shape=[
            jax.ShapeDtypeStruct(query.shape, f32),
            jax.ShapeDtypeStruct(query.shape, bf16),
            jax.ShapeDtypeStruct((groups, heads, 1, rows), f32),
        ],
        compiler_params=pltpu.CompilerParams(
            dimension_semantics=("arbitrary",), vmem_limit_bytes=VMEM_LIMIT
        ),
    )(offsets, starts, codes, query, path_bits[:, None, :], key_bits, *kv_parts)


def attend_backward(
    offsets, starts, codes, query, mixed_grad, mixed, log_total, path_bits, key_bits, kv_parts
):
    groups, heads, _, rows = query.shape
    block = min(QUERY_BLOCK, rows)
    per_group = rows // block
    tokens = key_bits.shape[1]
    key_block = min(KEY_BLOCK, tokens)
    wide, row = attention_specs(heads, rows, block)
    grad_shape = (kv_parts[0].shape[1], 2 * HD)
    kernel = functools.partial(
        attend_backward_kernel,
        parts=len(kv_parts),
        key_blocks=tokens // key_block,
        key_block=key_block,
    )
    outs = pl.pallas_call(
        kernel,
        name="attend_backward",
        grid_spec=pltpu.PrefetchScalarGridSpec(
            num_scalar_prefetch=3,
            grid=(groups * per_group,),
            in_specs=[
                wide,
                wide,
                wide,
                row,
                pl.BlockSpec((1, 1, block), lambda s, *_: (s // per_group, 0, s % per_group)),
                whole(key_bits.shape),
            ]
            + [whole(p.shape) for p in kv_parts],
            out_specs=[wide] + [whole(grad_shape) for _ in kv_parts],
            scratch_shapes=[
                pltpu.VMEM((tokens, 2 * HD), bf16),
                pltpu.VMEM((HD, tokens), bf16),
                pltpu.VMEM((2 * HD, heads * block), bf16),
                pltpu.VMEM((2 * HD, heads * block), bf16),
                pltpu.VMEM((heads * block, 2 * HD), bf16),
                pltpu.VMEM((heads * block, 2 * HD), bf16),
                pltpu.VMEM((8, heads * block), f32),
                pltpu.VMEM((HD, heads * block), f32),
                pltpu.VMEM((tokens, 2 * HD), f32),
            ],
        ),
        out_shape=[jax.ShapeDtypeStruct(query.shape, f32)]
        + [jax.ShapeDtypeStruct(grad_shape, bf16) for _ in kv_parts],
        compiler_params=pltpu.CompilerParams(
            dimension_semantics=("arbitrary",), vmem_limit_bytes=VMEM_LIMIT
        ),
    )(
        offsets,
        starts,
        codes,
        query,
        mixed_grad,
        mixed,
        log_total,
        path_bits[:, None, :],
        key_bits,
        *kv_parts,
    )
    return outs[0], outs[1:]


def place_kernel(offsets, *rest):
    parts, out = rest[:-1], rest[-1]
    for n, part in enumerate(parts):
        rows = part.shape[0]
        out[pl.ds(pl.multiple_of(offsets[n], rows), rows), :] = part[...]


def place_rows(offsets, parts):
    rows, width = parts[0].shape
    return pl.pallas_call(
        place_kernel,
        name="place_rows",
        grid_spec=pltpu.PrefetchScalarGridSpec(
            num_scalar_prefetch=1,
            grid=(1,),
            in_specs=[whole(p.shape) for p in parts],
            out_specs=whole((rows * len(parts), width)),
        ),
        out_shape=jax.ShapeDtypeStruct((rows * len(parts), width), parts[0].dtype),
        compiler_params=pltpu.CompilerParams(vmem_limit_bytes=VMEM_LIMIT),
    )(offsets, *parts)


def rank_kernel(first, route_rows, priority_rows, route_columns, priority_columns, out, *, experts):
    rows = route_rows.shape[2]
    never = rows * TOPK
    for e in range(experts):
        expert = first[0] + e
        along = jnp.min(
            jnp.where(route_rows[0] == expert, priority_rows[0], never), axis=0, keepdims=True
        )
        down = jnp.min(
            jnp.where(route_columns[0] == expert, priority_columns[0], never), axis=1, keepdims=True
        )
        count = jnp.zeros((8, rows), i32)
        for begin in range(0, rows, 8):
            count += (down[begin : begin + 8] < along).astype(i32)
        rank = jnp.sum(count, axis=0, keepdims=True)
        out[0, e : e + 1, :] = jnp.where((along < never) & (rank < CAP), rank, -1)
    if out.shape[1] > experts:
        out[0, experts:, :] = jnp.full((out.shape[1] - experts, rows), -1, i32)


def slot_ranks(first, routes, priority, experts):
    groups, rows, _ = routes.shape
    tall = pl.BlockSpec((1, rows, TOPK), lambda g, *_: (g, 0, 0))
    flat = pl.BlockSpec((1, TOPK, rows), lambda g, *_: (g, 0, 0))
    padded = -(-experts // 8) * 8
    return pl.pallas_call(
        functools.partial(rank_kernel, experts=experts),
        name="slot_ranks",
        grid_spec=pltpu.PrefetchScalarGridSpec(
            num_scalar_prefetch=1,
            grid=(groups,),
            in_specs=[flat, flat, tall, tall],
            out_specs=pl.BlockSpec((1, padded, rows), lambda g, *_: (g, 0, 0)),
        ),
        out_shape=jax.ShapeDtypeStruct((groups, padded, rows), i32),
        compiler_params=pltpu.CompilerParams(vmem_limit_bytes=VMEM_LIMIT),
    )(
        first.reshape(1),
        routes.transpose(0, 2, 1),
        priority.transpose(0, 2, 1),
        routes,
        priority,
    )


def expert_kernel(offsets, first, ranks, *rest, parts, groups):
    gates, rest = rest[:groups], rest[groups:]
    tokens, rest = rest[:groups], rest[groups:]
    grads, rest = rest[:groups], rest[groups:]
    weights = rest[:parts]
    weighted_out, token_grad, inputs, slot_grads, hidden, pair_grads, matrices = rest[parts:]
    rows = tokens[0].shape[0]
    e = pl.program_id(0)
    for n, part in enumerate(weights):
        count = part.shape[2]
        for m in range(3):
            matrices[m, pl.ds(pl.multiple_of(offsets[n], count), count), :] = part[m, 0]
    slot = lax.broadcasted_iota(i32, (SLOTS, rows), 0)
    for g in range(groups):
        at = slice(g * SLOTS, (g + 1) * SLOTS)
        inside = slot == ranks[g, pl.ds(e, 1), :]
        pick = inside.astype(bf16)
        gate = gates[g][pl.ds(first[0] + e, 1), :]
        weight = jnp.sum(jnp.where(inside, gate, 0.0), axis=1, keepdims=True)
        picked = dot(pick, tokens[g][...]).astype(bf16)
        inputs[0, at, :] = picked
        gate_pre = dot(picked, matrices[0])
        up_pre = dot(picked, matrices[1])
        sigma = jax.nn.sigmoid(gate_pre)
        silu = gate_pre * sigma
        active = (silu * up_pre).astype(bf16)
        out = dot_dims(active, matrices[2], 1, 1)
        weighted_out[g, 0] = (out * weight).astype(bf16)
        upstream = dot(pick, grads[g][...])
        pair = jnp.sum(upstream * out, axis=1, keepdims=True)
        pair_grads[g, pl.ds(e, 1), :] = jnp.sum(jnp.where(inside, pair, 0.0), axis=0, keepdims=True)
        slot_grad = (weight * upstream).astype(bf16)
        slot_grads[0, at, :] = slot_grad
        act_grad = dot(slot_grad, matrices[2])
        gate_grad = (act_grad * up_pre * sigma * (1.0 + gate_pre * (1.0 - sigma))).astype(bf16)
        up_grad = (act_grad * silu).astype(bf16)
        hidden[0, 0, at, :] = gate_grad
        hidden[0, 1, at, :] = up_grad
        hidden[0, 2, at, :] = active
        token_grad[g, 0] = (
            dot_dims(gate_grad, matrices[0], 1, 1) + dot_dims(up_grad, matrices[1], 1, 1)
        ).astype(bf16)


def run_experts(offsets, first, ranks, gates, tokens, grads, weight_parts):
    groups = len(tokens)
    rows = tokens[0].shape[0]
    _, experts, part_rows, _ = weight_parts[0].shape
    parts = len(weight_parts)
    slots = groups * SLOTS
    by_group = pl.BlockSpec((groups, 1, SLOTS, D), lambda e, *_: (0, e, 0, 0))
    stash = pl.BlockSpec((1, slots, D), lambda e, *_: (e, 0, 0))
    return pl.pallas_call(
        functools.partial(expert_kernel, parts=parts, groups=groups),
        name="experts",
        grid_spec=pltpu.PrefetchScalarGridSpec(
            num_scalar_prefetch=2,
            grid=(experts,),
            in_specs=[whole(ranks.shape)]
            + [whole((EXPERTS, rows)) for _ in range(groups)]
            + [whole((rows, D)) for _ in range(2 * groups)]
            + [pl.BlockSpec((3, 1, part_rows, H), lambda e, *_: (0, e, 0, 0)) for _ in weight_parts],
            out_specs=[
                by_group,
                by_group,
                stash,
                stash,
                pl.BlockSpec((1, 3, slots, H), lambda e, *_: (e, 0, 0, 0)),
                whole(ranks.shape),
            ],
            scratch_shapes=[pltpu.VMEM((3, D, H), bf16)],
        ),
        out_shape=[
            jax.ShapeDtypeStruct((groups, experts, SLOTS, D), bf16),
            jax.ShapeDtypeStruct((groups, experts, SLOTS, D), bf16),
            jax.ShapeDtypeStruct((experts, slots, D), bf16),
            jax.ShapeDtypeStruct((experts, slots, D), bf16),
            jax.ShapeDtypeStruct((experts, 3, slots, H), bf16),
            jax.ShapeDtypeStruct(ranks.shape, f32),
        ],
        compiler_params=pltpu.CompilerParams(
            dimension_semantics=("arbitrary",), vmem_limit_bytes=VMEM_LIMIT
        ),
    )(
        offsets,
        first.reshape(1),
        ranks,
        *gates,
        *tokens,
        *grads,
        *weight_parts,
    )


def expert_grad_kernel(offsets, inputs, slot_grads, hidden, *rest, pieces):
    outs, total = rest[:-1], rest[-1]
    for m in range(3):
        left = inputs if m < 2 else slot_grads
        total[...] = dot_dims(left[0], hidden[0, m], 0, 0)
        for (n, begin), out in zip(pieces, outs):
            if begin <= m < begin + out.shape[0]:
                count = out.shape[2]
                at = pl.ds(pl.multiple_of(offsets[n], count), count)
                out[m - begin, 0] = total[at, :].astype(bf16)


def expert_grads(offsets, inputs, slot_grads, hidden, parts, cut_parts, part_rows):
    experts, slots, _ = inputs.shape
    stash = pl.BlockSpec((1, slots, D), lambda e, *_: (e, 0, 0))
    pieces = []
    for n in range(parts):
        pieces += [(n, 0, 1), (n, 1, 2)] if n in cut_parts else [(n, 0, 3)]
    outs = pl.pallas_call(
        functools.partial(expert_grad_kernel, pieces=[(n, begin) for n, begin, _ in pieces]),
        name="expert_grads",
        grid_spec=pltpu.PrefetchScalarGridSpec(
            num_scalar_prefetch=1,
            grid=(experts,),
            in_specs=[stash, stash, pl.BlockSpec((1, 3, slots, H), lambda e, *_: (e, 0, 0, 0))],
            out_specs=[
                pl.BlockSpec((held, 1, part_rows, H), lambda e, *_: (0, e, 0, 0))
                for _, _, held in pieces
            ],
            scratch_shapes=[pltpu.VMEM((D, H), f32)],
        ),
        out_shape=[
            jax.ShapeDtypeStruct((held, experts, part_rows, H), bf16) for _, _, held in pieces
        ],
        compiler_params=pltpu.CompilerParams(
            dimension_semantics=("arbitrary",), vmem_limit_bytes=VMEM_LIMIT
        ),
    )(offsets, inputs, slot_grads, hidden)
    found = {}
    for (n, _, _), out in zip(pieces, outs):
        found.setdefault(n, []).append(out)
    return [found[n] for n in range(parts)]


def combine_kernel(ranks, rows_in, out, *, experts):
    count = out.shape[0]
    slot = lax.broadcasted_iota(i32, (count, SLOTS), 1)
    pick = jnp.concatenate(
        [(ranks[0, :, e : e + 1] == slot).astype(bf16) for e in range(experts)], axis=1
    )
    out[...] = dot(pick, rows_in[0]).astype(bf16)


def combine(ranks, slot_rows, g):
    groups, rows, columns = ranks.shape
    experts = slot_rows.shape[1]
    block = min(256, rows)
    return pl.pallas_call(
        functools.partial(combine_kernel, experts=experts),
        name="combine",
        grid=(rows // block,),
        in_specs=[
            pl.BlockSpec((1, block, columns), lambda i: (g, i, 0)),
            pl.BlockSpec(
                (1, experts * SLOTS, D), lambda i: (g, 0, 0), pipeline_mode=pl.Buffered(1)
            ),
        ],
        out_specs=pl.BlockSpec((block, D), lambda i: (i, 0)),
        out_shape=jax.ShapeDtypeStruct((rows, D), bf16),
        compiler_params=pltpu.CompilerParams(vmem_limit_bytes=VMEM_LIMIT),
    )(ranks, slot_rows.reshape(groups, experts * SLOTS, D))


def project_kernel(mixed, x, gain, matrix, middle, normed, inverse):
    branch = dot_dims(mixed[...].astype(f32).T.astype(bf16), matrix[:, :D], 1, 1)
    total = x[...].astype(f32) + branch_scale * branch
    scale = lax.rsqrt(jnp.mean(total * total, axis=1, keepdims=True) + epsilon)
    middle[...] = total
    inverse[...] = scale
    normed[...] = (total * scale * gain[...]).astype(bf16)


def project_out(mixed, x, gain, matrix):
    rows = x.shape[0]
    block = min(256, rows)
    tall = pl.BlockSpec((block, D), lambda i: (i, 0))
    return pl.pallas_call(
        project_kernel,
        name="project_out",
        grid=(rows // block,),
        in_specs=[
            pl.BlockSpec((D, block), lambda i: (0, i)),
            tall,
            whole(gain.shape),
            whole(matrix.shape),
        ],
        out_specs=[tall, tall, pl.BlockSpec((block, 1), lambda i: (i, 0))],
        out_shape=[
            jax.ShapeDtypeStruct((rows, D), f32),
            jax.ShapeDtypeStruct((rows, D), bf16),
            jax.ShapeDtypeStruct((rows, 1), f32),
        ],
        compiler_params=pltpu.CompilerParams(
            dimension_semantics=("arbitrary",), vmem_limit_bytes=VMEM_LIMIT
        ),
    )(mixed, x, gain, matrix)


def rows_of(columns):
    return columns[...].astype(f32).T.astype(bf16)


def matrix_grad_kernel(
    offsets, h_one, project_grad, branch_grad, mixed, h_two, logit_grad, project, *rest
):
    outs, gain, total = rest[:-2], rest[-2], rest[-1]
    wide = project_grad.shape[0]
    end = wide + mixed.shape[0]
    late = dot_dims(h_one[...], rows_of(project_grad), 0, 0)
    gain[...] = jnp.sum(late * project[...].astype(f32), axis=1, keepdims=True)
    total[:, :wide] = late
    total[:, wide:end] = dot_dims(branch_grad[...], rows_of(mixed), 0, 0)
    total[:, end:] = dot_dims(h_two[...], rows_of(logit_grad), 0, 0)
    for k, out in enumerate(outs):
        count, rows, _ = out.shape
        for p in range(count):
            at = pl.ds(pl.multiple_of(offsets[k * count + p], rows), rows)
            out[p] = total[at, :].astype(bf16)


def matrix_grads_of(offsets, share, arrays):
    width = sum(a.shape[0] for a in (arrays[1], arrays[3], arrays[5]))
    count = offsets.shape[0] // share
    out = jax.ShapeDtypeStruct((count, D // (count * share), width), bf16)
    return pl.pallas_call(
        matrix_grad_kernel,
        name="matrix_grads",
        grid_spec=pltpu.PrefetchScalarGridSpec(
            num_scalar_prefetch=1,
            grid=(1,),
            in_specs=[whole(a.shape) for a in arrays],
            out_specs=[whole(out.shape)] * share + [whole((D, 1))],
            scratch_shapes=[pltpu.VMEM((D, width), f32)],
        ),
        out_shape=[out] * share + [jax.ShapeDtypeStruct((D, 1), f32)],
        compiler_params=pltpu.CompilerParams(vmem_limit_bytes=VMEM_LIMIT),
    )(offsets, *arrays)


def rotate(values, cosine, sine):
    first = values[..., : HD // 2, :]
    second = values[..., HD // 2 :, :]
    return jnp.concatenate([first * cosine - second * sine, second * cosine + first * sine], axis=-2)


def rotate_back(values, cosine, sine):
    first = values[..., : HD // 2, :]
    second = values[..., HD // 2 :, :]
    return jnp.concatenate([first * cosine + second * sine, second * cosine - first * sine], axis=-2)


def tree_tables(ancestry, own_all, token_starts, query_block, key_block):
    groups, rows, _ = ancestry.shape
    tokens = own_all.shape[0]
    segments = jnp.arange(SEGS, dtype=i32)
    index = jnp.arange(tokens, dtype=i32)
    member = own_all[None, :] == segments[:, None]
    begin = jnp.min(jnp.where(member, index[None, :], tokens), axis=1)
    length = jnp.sum(member.astype(i32), axis=1)
    on_path = jnp.any(ancestry[:, :, :, None] == segments, axis=2)
    at = token_starts[:, None] + jnp.arange(rows, dtype=i32)[None, :]
    before = jnp.clip(at[:, :, None] - begin, 0, length)
    position = jnp.sum(jnp.where(on_path, before, 0), axis=2)
    bits = jnp.sum(on_path.astype(i32) << segments, axis=2)
    blocked = on_path.reshape(groups * rows // query_block, query_block, SEGS)
    path_any = jnp.any(blocked, axis=1)
    path_all = jnp.all(blocked, axis=1)
    keys = jnp.any(member.reshape(SEGS, tokens // key_block, key_block), axis=2).T
    some = jnp.any(path_any[:, None, :] & keys[None, :, :], axis=2)
    every = jnp.all(path_all[:, None, :] | ~keys[None, :, :], axis=2)
    query_start = at.reshape(-1, query_block)[:, 0]
    key_start = jnp.arange(tokens // key_block, dtype=i32) * key_block
    some &= key_start[None, :] < query_start[:, None] + query_block
    every &= key_start[None, :] + key_block <= query_start[:, None] + 1
    codes = jnp.where(some, jnp.where(every, 2, 1), 0).astype(i32)
    return position, bits, query_start, codes.reshape(-1)


def body(
    layer_input,
    cotangent,
    gain_attention,
    gain_mixture,
    w_query,
    w_key,
    w_value,
    w_out,
    w_router,
    w_gate,
    w_up,
    w_down,
    routes,
    priority,
    ancestry,
):
    chips, share, columns = lax.axis_size("chip"), lax.axis_size("core"), lax.axis_size("col")
    chip, core, column = lax.axis_index("chip"), lax.axis_index("core"), lax.axis_index("col")
    row_axes = ("chip", "core")
    rows, width = layer_input.shape
    weight_rows = w_query.shape[0]
    query_heads = w_query.shape[1] // HD
    key_heads = w_key.shape[1] // HD
    group = query_heads // key_heads
    own_heads = key_heads // share
    experts = w_gate.shape[1] // share
    tokens_all = rows * chips * share
    query_block = min(QUERY_BLOCK, rows)
    key_block = min(KEY_BLOCK, tokens_all)
    token_block = rows // columns

    places = [(chip ^ j) * share + (core ^ h) for j in range(chips) for h in range(share)]
    token_offsets = jnp.stack([p * rows for p in places]).astype(i32)
    feature_offsets = jnp.stack([p * weight_rows for p in places]).astype(i32)

    def groups_of(values):
        return [values] + ([swap_core(values)] if share == 2 else [])

    x_full = lax.all_gather(layer_input, "col", axis=1, tiled=True)
    index_groups = groups_of(jnp.concatenate([routes, priority, ancestry], axis=1))
    index_arrays = jnp.stack(index_groups)

    own_all = lax.all_gather(ancestry[:, 0], row_axes, axis=0, tiled=True)
    project_part = jnp.concatenate([w_query, w_key, w_value], axis=1)
    own_all, project_part = tie(own_all, project_part)
    levels_here = range(len(chip_bits(chips)))
    project_parts = [project_part]
    for level in levels_here:
        project_parts = shared_level(project_parts, level)

    stacked = jnp.stack([m.transpose(1, 0, 2) for m in (w_gate, w_up, w_down)])
    stacked = stacked.reshape(3, share, experts, weight_rows, H).transpose(1, 0, 2, 3, 4)
    own_weights, other_weights = own_and_other(stacked, core, share)
    starts = [own_weights] + ([swap_core(other_weights)] if share == 2 else [])
    project_parts, starts, index_arrays = tie(project_parts, starts, index_arrays)
    all_routes = index_arrays[:, :, :TOPK]
    all_priority = index_arrays[:, :, TOPK : 2 * TOPK]
    all_ancestry = index_arrays[:, :, 2 * TOPK :]
    project = shared_rows(project_parts)
    rounds = gather_rounds(chips, share)
    weights_held = run_gather({(h, 0): v for h, v in enumerate(starts)}, rounds[:1])
    gains = column_rows(jnp.concatenate([gain_attention, gain_mixture])[None, :])
    gains = gains.reshape(columns, 2, width).transpose(1, 0, 2).reshape(2, D)

    token_starts = jnp.stack([(chip * share + (core ^ g)) * rows for g in range(share)]).astype(i32)
    position, path_bits, query_starts, codes = tree_tables(
        all_ancestry, own_all, token_starts, query_block, key_block
    )
    frequency = rope_base ** (-(jnp.arange(HD // 2, dtype=f32) * 2.0) / HD)
    angle = position.astype(f32)[:, None, :] * frequency[None, :, None]
    by_rows = Layout(major_to_minor=(0, 1, 2))
    cosine = with_layout_constraint(jnp.cos(angle), by_rows)
    sine = with_layout_constraint(jnp.sin(angle), by_rows)
    first_expert = (column * (experts * share) + core * experts).astype(i32)
    ranks = slot_ranks(first_expert, all_routes, all_priority, experts)
    rank_columns = ranks.transpose(0, 2, 1)
    expert_ids = jnp.arange(EXPERTS, dtype=i32)
    chosen = jnp.any(all_routes[:, None, :, :] == expert_ids[None, :, None, None], axis=3)

    key_bits = (jnp.int32(1) << own_all)[None, :]
    early_tables = (ranks, rank_columns, codes, path_bits, chosen, cosine, sine, project)
    x_full, w_out_here, early_tables = tie(x_full, w_out, early_tables)
    ranks, rank_columns, codes, path_bits, chosen, cosine, sine, project = early_tables
    out_columns = jnp.zeros((weight_rows, D), bf16)
    for c, part in [(column, w_out_here)] + column_shifts(lambda _: w_out_here):
        out_columns = lax.dynamic_update_slice_in_dim(out_columns, part, c * part.shape[1], 1)
    cotangent_here, out_columns = tie(cotangent, out_columns)
    cotangent_full = lax.all_gather(cotangent_here, "col", axis=1, tiled=True)
    tables = (ranks, rank_columns, cosine, sine, path_bits, codes, chosen, key_bits, project, gains)
    out_parts = [jnp.concatenate([out_columns, w_router], axis=1)]
    x_full, weights_held, tables = tie(x_full, weights_held, tables)
    ranks, rank_columns, cosine, sine, path_bits, codes, chosen, key_bits, project, gains = tables
    x_wide = x_full.astype(f32)
    inverse_one = lax.rsqrt(jnp.mean(x_wide * x_wide, axis=1, keepdims=True) + epsilon)
    h_one = (x_wide * inverse_one * gains[0][None, :]).astype(bf16)
    projected = dot_dims(project, h_one, 0, 1)
    query_width, key_width = query_heads * HD, key_heads * HD
    query = rotate(
        projected[:query_width].reshape(share, own_heads, group, HD, rows), cosine[0], sine[0]
    )
    query = (query.astype(bf16).astype(f32) * score_scale).astype(bf16)
    keys = rotate(
        projected[query_width : query_width + key_width].reshape(share, own_heads, HD, rows),
        cosine[0],
        sine[0],
    ).astype(bf16)
    values = projected[query_width + key_width :].reshape(share, own_heads, HD, rows).astype(bf16)
    sent = jnp.concatenate([keys[:, :, None], values[:, :, None], query], axis=2)
    own_sent, other_sent = own_and_other(sent, core, share)
    received = [own_sent] + ([swap_core(other_sent)] if share == 2 else [])
    query_groups = jnp.stack([r[:, 2:] for r in received], axis=1)
    pairs = [r[:, :2].reshape(own_heads, 2 * HD, rows) for r in received]
    for level in levels_here:
        out_parts = shared_level(out_parts, level)
    pairs, weights_held, out_parts = tie(pairs, weights_held, out_parts)
    kv_parts = gather_parts(pairs, chips)
    kv_parts, weights_held = tie(kv_parts, weights_held)
    weights_held = run_gather(weights_held, rounds[1 : len(rounds) - 1])

    attend_outs = [
        attend_forward(
            token_offsets,
            query_starts,
            codes,
            query_groups[head],
            path_bits,
            key_bits,
            [p[head] for p in kv_parts],
        )
        for head in range(own_heads)
    ]
    mixed_b = jnp.stack([o[1] for o in attend_outs])
    mixed_b, weights_held, cotangent_full, out_parts = tie(
        mixed_b, weights_held, cotangent_full, out_parts
    )
    out_router = shared_rows(out_parts)
    weights_held = run_gather(weights_held, rounds[len(rounds) - 1 :])
    mixed_other = swap_core(mixed_b[:, 1]) if share == 2 else None
    mixed = in_core_order(mixed_b[:, 0], mixed_other, core).reshape(query_width, rows)
    mixed_full = lax.all_gather(mixed, "col", axis=0, tiled=True)
    mixed_full, weights_held, out_router = tie(mixed_full, weights_held, out_router)
    mix_grads = groups_of((branch_scale * cotangent_full.astype(f32)).astype(bf16))
    x_middle, h_two, inverse_two = project_out(
        mixed_full, x_full, gains[1:2], out_router
    )
    full_router = out_router[:, D:]
    h_two_groups = groups_of(h_two)

    def gates_of(tokens, picks):
        logits = dot_dims(full_router, tokens, 0, 1)
        shown = jnp.where(picks, logits, masked_score)
        raised = jnp.where(picks, jnp.exp(logits - jnp.max(shown, axis=0, keepdims=True)), 0.0)
        return raised / jnp.sum(raised, axis=0, keepdims=True)

    gates = [gates_of(h_two_groups[g], chosen[g]) for g in range(share)]
    weighted_out, slot_token_grads, inputs, slot_grads, hidden, pair_rows = run_experts(
        feature_offsets,
        first_expert,
        ranks,
        gates,
        h_two_groups,
        mix_grads,
        listed(weights_held, chips),
    )

    def combine_groups(slot_rows):
        if share == 1:
            return combine(rank_columns, slot_rows, 0)
        received = swap_core(combine(rank_columns, slot_rows, 1))
        own = combine(rank_columns, slot_rows, 0)
        return (own.astype(f32) + received.astype(f32)).astype(bf16)

    token_sum = combine_groups(slot_token_grads)
    token_grads = lax.psum_scatter(token_sum, "col", scatter_dimension=0, tiled=True)
    pair_other = swap_core(pair_rows[1, :experts]) if share == 2 else None
    pair_columns = in_core_order(pair_rows[0, :experts], pair_other, core)
    pair_columns = pair_columns.reshape(share * experts, rows)
    pair_grad = column_rows(pair_columns)
    picked_grad = gates[0] * (pair_grad - jnp.sum(gates[0] * pair_grad, axis=0, keepdims=True))
    logit_grad = picked_grad.astype(bf16)
    mix_sum = combine_groups(weighted_out)

    levels = reduce_levels(chips, share)
    first = [[m for m in moves if m[1]] for moves in levels[0]]
    last = [[m for m in moves if not m[1]] for moves in levels[0]]
    sent = {(h, j ^ bit) for moves in first for h, j, bit in moves}
    last_sent = {(h, j ^ bit) for moves in last for h, j, bit in moves}
    parts = expert_grads(
        feature_offsets,
        inputs,
        slot_grads,
        hidden,
        chips * share,
        {j * share + h for h, j in sent | last_sent},
        weight_rows,
    )
    sums_held = {(h, j): parts[j * share + h] for j in range(chips) for h in range(share)}

    def take_piece(rounds_here, held):
        taken = {}
        for moves in rounds_here:
            taken.update(take(held, moves))
        return taken

    first_taken = take_piece(first, {k: sums_held[k][0] for k in sent})
    staying = [sums_held[h, 0][0] for h in range(share)]
    token_grads, staying, mix_sum, logit_grad, first_taken = tie(
        token_grads, staying, mix_sum, logit_grad, first_taken
    )
    token_grads = token_grads.astype(f32)
    second_taken = take_piece(first, {k: sums_held[k][1] for k in sent})

    token_start = column * token_block

    def own_tokens(array):
        return lax.dynamic_slice_in_dim(array, token_start, token_block, 0)

    h_two_grad = token_grads + dot_dims(
        lax.dynamic_slice_in_dim(logit_grad, token_start, token_block, 1), full_router, 0, 1
    )
    x_part, inverse_part = own_tokens(x_middle), own_tokens(inverse_two)
    scaled_two = h_two_grad * gains[1][None, :]
    inner_two = jnp.sum(scaled_two * x_part, axis=1, keepdims=True)
    x_middle_grad = (
        own_tokens(cotangent_full).astype(f32)
        + inverse_part * scaled_two
        - x_part * inverse_part**3 * inner_two / D
    )
    gain_mixture_part = jnp.sum(h_two_grad * x_part * inverse_part, axis=0)
    branch_part = (branch_scale * x_middle_grad).astype(bf16)
    mixed_parts = dot(branch_part, out_router[:, :D]).astype(bf16)
    mixed_parts = mixed_parts.reshape(token_block, columns, query_width).transpose(1, 0, 2)
    mixed_grad = lax.all_to_all(mixed_parts, "col", split_axis=0, concat_axis=0, tiled=True)
    mixed_grad, branch_part, mix_sum, second_taken = tie(
        mixed_grad, branch_part, mix_sum, second_taken
    )
    branch_grad = lax.all_gather(branch_part, "col", axis=0, tiled=True)
    sums_here = {}
    for k, part in first_taken.items():
        taken = jnp.concatenate([part, second_taken[k]])
        sums_here[k] = (sums_held[k][0].astype(f32) + taken.astype(f32)).astype(bf16)

    mixed_grad = mixed_grad.reshape(rows, query_width).T
    mixed_grad, sums_here = tie(mixed_grad, sums_here)
    own_grad, other_grad = own_and_other(
        mixed_grad.reshape(share, own_heads, group, HD, rows), core, share
    )
    arrived = [[part] for part in staying]
    for rounds_here in levels[1:]:
        passed = {}
        for moves in rounds_here:
            passed.update(take(sums_here, moves))
        for h in range(share):
            if (h, 0) in passed:
                arrived[h].append(passed.pop((h, 0)))
        sums_here = add_taken(sums_here, passed)
    last_begin = {k: sums_held[k][0] for k in last_sent}
    last_rest = {k: sums_held[k][1] for k in last_sent}
    last_rest, own_grad = tie(last_rest, own_grad)
    last_rest = take_piece(last, last_rest)
    grad_groups = jnp.stack(
        [own_grad] + ([swap_core(other_grad)] if share == 2 else []), axis=1
    )
    backward_outs = [
        attend_backward(
            token_offsets,
            query_starts,
            codes,
            query_groups[head],
            grad_groups[head],
            attend_outs[head][0],
            attend_outs[head][2],
            path_bits,
            key_bits,
            [p[head] for p in kv_parts],
        )
        for head in range(own_heads)
    ]
    mix_slice = lax.psum_scatter(mix_sum, "col", scatter_dimension=1, tiled=True).astype(f32)
    feature_start = column * width
    x_middle_slice = lax.dynamic_slice_in_dim(x_middle, feature_start, width, 1)
    result = (x_middle_slice + branch_scale * mix_slice).astype(bf16)
    backward_outs, arrived, branch_later, last_rest = tie(
        backward_outs, arrived, branch_grad, last_rest
    )
    query_grad = jnp.stack([o[0] for o in backward_outs])
    query_grad = rotate_back(query_grad, cosine[None, :, None], sine[None, :, None]).astype(bf16)
    query_other = swap_core(query_grad[:, 1]) if share == 2 else None
    query_pre_grad = in_core_order(query_grad[:, 0], query_other, core).reshape(query_width, rows)
    kv_sums = reduce_parts(
        [jnp.stack([o[1][n] for o in backward_outs]) for n in range(chips * share)], chips, share
    )
    kv_other = swap_core(kv_sums[1]) if share == 2 else None
    kv_grad = in_core_order(kv_sums[0], kv_other, core).astype(f32)
    kv_grad, last_begin = tie(kv_grad, last_begin)
    last_begin = take_piece(last, last_begin)
    for h in range(share):
        for k in last_rest:
            if k[0] == h:
                arrived[h].append(jnp.concatenate([last_begin[k], last_rest[k]]))
    kv_grad = kv_grad.transpose(0, 1, 3, 2).reshape(key_heads, 2 * HD, rows)
    key_pre_grad = (
        rotate_back(kv_grad[:, :HD], cosine[0], sine[0]).astype(bf16).reshape(key_width, rows)
    )
    value_pre_grad = kv_grad[:, HD:].astype(bf16).reshape(key_width, rows)
    project_grad = jnp.concatenate([query_pre_grad, key_pre_grad, value_pre_grad], axis=0)

    (project_grad,) = tie(project_grad)
    h_one_part = dot(project, project_grad).astype(bf16)
    h_one_part, project_grad = tie(h_one_part, project_grad)
    h_one_grad = lax.psum_scatter(h_one_part, "col", scatter_dimension=0, tiled=True)
    inner_one = column_sum(jnp.sum(project_grad.astype(f32) * projected, axis=0))[:, None]
    sums = [functools.reduce(jnp.add, [p.astype(f32) for p in own]).astype(bf16) for own in arrived]
    small_places = shared_places(chips, share, core)
    if share == 2:
        small_places = small_places + shared_places(chips, share, 1 - core)
    *small_parts, gain_column = matrix_grads_of(
        jnp.stack([p * weight_rows for p in small_places]).astype(i32),
        share,
        (h_one, project_grad, branch_later, mixed, h_two, logit_grad, project),
    )
    gain_attention_part = gain_column[:, 0] / gains[0]
    gain_parts = jnp.stack([gain_attention_part, gain_mixture_part])

    def own_features(array, c):
        return lax.dynamic_slice_in_dim(array, c * width, width, 1)

    gain_sums = own_features(gain_parts, column)
    for _, other in column_shifts(lambda c: own_features(gain_parts, c)):
        gain_sums = gain_sums + other
    small_parts, sums = tie(small_parts, sums)
    returned = swap_core(sums[1]) if share == 2 else None
    small_sum = shared_reduce(small_parts[0], small_parts[1] if share == 2 else None)
    gain_sums = row_sum(gain_sums)
    matrix_grads = [
        in_core_order(sums[0][m], None if returned is None else returned[m], core)
        .astype(f32)
        .reshape(share * experts, weight_rows, H)
        .transpose(1, 0, 2)
        for m in range(3)
    ]
    h_one_grad, matrix_grads, small_sum, gain_sums, inner_one = tie(
        h_one_grad, matrix_grads, small_sum, gain_sums, inner_one
    )
    x_slice = layer_input.astype(f32)
    middle_slice = lax.dynamic_slice_in_dim(branch_grad, feature_start, width, 1).astype(f32)
    input_grad = (
        middle_slice * (1.0 / branch_scale)
        + inverse_one * h_one_grad.astype(f32).T * gain_attention[None, :]
        - x_slice * inverse_one**2 * inner_one / D
    )
    kv_width = query_width + 2 * key_width
    return (
        result,
        input_grad,
        gain_sums[0],
        gain_sums[1],
        small_sum[:, :query_width],
        small_sum[:, query_width : query_width + key_width],
        small_sum[:, query_width + key_width : kv_width],
        small_sum[:, kv_width : kv_width + query_width],
        small_sum[:, kv_width + query_width :],
        *matrix_grads,
    )


def solution(mesh):
    rows, columns = mesh.shape["row"], mesh.shape["col"]
    halves = rows % 2 == 0 and EXPERTS // columns % 2 == 0 and KVH // columns % 2 == 0
    share = 2 if halves else 1
    split = Mesh(mesh.devices.reshape(rows // share, share, columns), ("chip", "core", "col"))
    row = ("chip", "core")
    return jax.shard_map(
        body,
        mesh=split,
        in_specs=(
            P(row, "col"),
            P(row, "col"),
            P("col"),
            P("col"),
            P(row, "col"),
            P(row, "col"),
            P(row, "col"),
            P(row, "col"),
            P(row, None),
            P(row, "col", None),
            P(row, "col", None),
            P(row, "col", None),
            P(row, None),
            P(row, None),
            P(row, None),
        ),
        out_specs=(
            P(row, "col"),
            P(row, "col"),
            P("col"),
            P("col"),
            P(row, "col"),
            P(row, "col"),
            P(row, "col"),
            P(row, "col"),
            P(row, None),
            P(row, "col", None),
            P(row, "col", None),
            P(row, "col", None),
        ),
        check_vma=False,
    )
```

```python
import functools

import jax
import jax.numpy as jnp
from jax import lax
from jax.experimental.layout import Layout, with_layout_constraint
from jax.experimental import pallas as pl
from jax.experimental.pallas import tpu as pltpu
from jax.sharding import Mesh
from jax.sharding import PartitionSpec as P

D = 1536
HD = 64
H = 512
KVH = 8
EXPERTS = 40
TOPK = 8
SEGS = 13
CAP = 230
SLOTS = 256

epsilon = 1e-06
branch_scale = 0.22
score_scale = 0.015625
rope_base = 10000.0
masked_score = -1e30

bf16 = jnp.bfloat16
f32 = jnp.float32
i32 = jnp.int32

QUERY_BLOCK = 512
KEY_BLOCK = 512
VMEM_LIMIT = 60 * 1024 * 1024


def dot(left, right):
    return jnp.dot(left, right, preferred_element_type=f32)


def dot_dims(left, right, left_dim, right_dim):
    return lax.dot_general(
        left, right, (((left_dim,), (right_dim,)), ((), ())), preferred_element_type=f32
    )


def swap(values, axis, bit):
    size = lax.axis_size(axis)
    return lax.ppermute(values, axis, [(i, i ^ bit) for i in range(size)])


def swap_core(values):
    return swap(values, "core", 1)


def chip_bits(chips):
    return [1 << b for b in range(chips.bit_length() - 1)]


def half_bits(chips, half):
    bits = chip_bits(chips)
    return bits if half == 0 else bits[::-1]


def gather_rounds(chips, halves):
    rounds = []
    for level in range(len(chip_bits(chips))):
        moves = []
        for half in range(halves):
            bits = half_bits(chips, half)
            held = [0]
            for bit in bits[:level]:
                held += [j ^ bit for j in held]
            moves.append([(half, j, bits[level]) for j in sorted(held)])
        rounds += [list(r) for r in zip(*moves)]
    return rounds


def run_gather(held, rounds):
    held = dict(held)
    for moves in rounds:
        for half, j, bit in moves:
            held[half, j ^ bit] = swap(held[half, j], "chip", bit)
    return held


def gather_parts(values, chips):
    held = run_gather(
        {(h, 0): v for h, v in enumerate(values)}, gather_rounds(chips, len(values))
    )
    return listed(held, chips)


def listed(held, chips):
    halves = len(held) // chips
    return [held[h, j] for j in range(chips) for h in range(halves)]


def reduce_levels(chips, halves):
    levels = []
    for level in range(len(chip_bits(chips))):
        moves = []
        for half in range(halves):
            bits = half_bits(chips, half)
            done = sum(bits[: level + 1])
            moves.append([(half, j, bits[level]) for j in range(chips) if not j & done])
        levels.append([list(r) for r in zip(*moves)])
    return levels


def take(held, moves):
    return {(h, j): swap(held[h, j ^ bit], "chip", bit) for h, j, bit in moves}


def add_taken(held, taken):
    sums = {k: (held[k].astype(f32) + v.astype(f32)).astype(v.dtype) for k, v in taken.items()}
    return {**held, **sums}


def reduce_parts(parts, chips, share):
    held = {(h, j): parts[j * share + h] for j in range(chips) for h in range(share)}
    for rounds in reduce_levels(chips, share):
        taken = {}
        for moves in rounds:
            taken.update(take(held, moves))
        held = add_taken(held, taken)
    return [held[h, 0] for h in range(share)]


def pick(core, values):
    return jnp.where(core == 0, values[0], values[-1])


def shared_places(chips, share, core):
    chip = lax.axis_index("chip")
    places = []
    for p in range(chips):
        jumps = [
            sum(b for t, b in enumerate(half_bits(chips, k)) if p >> t & 1) for k in range(share)
        ]
        places.append((chip ^ pick(core, jumps)) * share + core)
    return places


def shared_swap(values, level):
    chips, share = lax.axis_size("chip"), lax.axis_size("core")
    pairs = [
        (c * share + k, (c ^ half_bits(chips, k)[level]) * share + k)
        for c in range(chips)
        for k in range(share)
    ]
    return lax.ppermute(values, ("chip", "core"), pairs)


def shared_level(blocks, level):
    return blocks + [shared_swap(b, level) for b in blocks]


def shared_rows(blocks):
    chips, share, core = lax.axis_size("chip"), lax.axis_size("core"), lax.axis_index("core")
    places = shared_places(chips, share, core)
    parts = list(blocks)
    if share == 2:
        parts += [swap_core(b) for b in blocks]
        places = places + shared_places(chips, share, 1 - core)
    rows = blocks[0].shape[0]
    return place_rows(jnp.stack([p * rows for p in places]).astype(i32), parts)


def shared_reduce(held, other):
    def add(left, right):
        return (left.astype(f32) + right.astype(f32)).astype(left.dtype)

    if other is not None:
        held = add(held, swap_core(other))
    for level in reversed(range(len(chip_bits(lax.axis_size("chip"))))):
        half = 1 << level
        held = add(held[:half], shared_swap(held[half:], level))
    return held[0].astype(f32)


def column_shifts(values_for):
    size = lax.axis_size("col")
    me = lax.axis_index("col")
    return [
        (
            (me - d) % size,
            lax.ppermute(values_for((me + d) % size), "col", [(i, (i + d) % size) for i in range(size)]),
        )
        for d in range(1, size)
    ]


def column_sum(values):
    for _, other in column_shifts(lambda _: values):
        values = values + other
    return values


def column_rows(values):
    rows = values.shape[0]
    size = lax.axis_size("col")
    out = jnp.zeros((size * rows,) + values.shape[1:], values.dtype)
    for c, part in [(lax.axis_index("col"), values)] + column_shifts(lambda _: values):
        out = lax.dynamic_update_slice_in_dim(out, part, c * rows, 0)
    return out


def row_sum(values):
    for axis in ("core", "chip"):
        for bit in chip_bits(lax.axis_size(axis)):
            values = values + swap(values, axis, bit)
    return values


def tie(*trees):
    return lax.optimization_barrier(trees)


def own_and_other(values, core, share):
    if share == 1:
        return values[0], None
    mine = lax.dynamic_index_in_dim(values, core, 0, keepdims=False)
    other = lax.dynamic_index_in_dim(values, 1 - core, 0, keepdims=False)
    return mine, other


def in_core_order(mine, other, core):
    if other is None:
        return mine[None]
    first = core == 0
    return jnp.stack([jnp.where(first, mine, other), jnp.where(first, other, mine)])


def column_of(row):
    return jnp.broadcast_to(row, (8, row.shape[1])).T[:, :1]


def attend_forward_kernel(
    offsets, starts, codes, query, path, key_bits, *rest, parts, key_blocks, key_block
):
    kv_parts = rest[:parts]
    out, rounded, log_total, key_columns, value_rows, query_rows, peak, mixed, paths = rest[parts:]
    step = pl.program_id(0)
    heads, width, count = query.shape[1:]

    @pl.when(step == 0)
    def _():
        for n, part in enumerate(kv_parts):
            rows = part.shape[1]
            start = pl.multiple_of(offsets[n], rows)
            key_columns[:, pl.ds(start, rows)] = part[:width, :]
            turned = pltpu.roll(part[...].astype(f32).T, width, 1)
            lane = lax.broadcasted_iota(i32, turned.shape, 1)
            value_rows[pl.ds(start, rows), :] = jnp.where(lane < width, turned, 1.0).astype(bf16)

    for head in range(heads):
        query_rows[head * count : (head + 1) * count] = query[0, head].astype(f32).T.astype(bf16)
    paths[...] = jnp.broadcast_to(path[0], (8, count)).T
    peak[...] = jnp.full_like(peak, masked_score)
    mixed[...] = jnp.zeros_like(mixed)

    def block(number, masked):
        start = pl.multiple_of(number * key_block, key_block)
        scores = dot(query_rows[...], key_columns[:, pl.ds(start, key_block)])
        if masked:
            keys = start + lax.broadcasted_iota(i32, (count, key_block), 1)
            queries = starts[step] + lax.broadcasted_iota(i32, (count, key_block), 0)
            on_path = (paths[:, :1] & key_bits[:, pl.ds(start, key_block)]) != 0
            allowed = on_path & (keys <= queries)
            scores = jnp.where(
                allowed[None], scores.reshape(heads, count, key_block), masked_score
            ).reshape(heads * count, key_block)
        old = peak[...]
        new = jnp.maximum(old, jnp.max(scores, axis=1, keepdims=True))
        weights = jnp.exp(scores - jnp.tile(new, (1, key_block // 128))).astype(bf16)
        mixed[...] = mixed[...] * jnp.exp(old - new) + dot(
            weights, value_rows[pl.ds(start, key_block), :]
        )
        peak[...] = new

    @pl.loop(0, key_blocks)
    def _(number):
        code = codes[step * key_blocks + number]

        @pl.when(code == 1)
        def _():
            block(number, True)

        @pl.when(code == 2)
        def _():
            block(number, False)

    lane = lax.broadcasted_iota(i32, (count, 2 * width), 1)
    for head in range(heads):
        at = slice(head * count, (head + 1) * count)
        sums = mixed[at]
        turned = jnp.where(
            lane < width, sums / pltpu.roll(sums, width, 1), peak[at] + jnp.log(sums)
        ).T
        out[0, head] = turned[:width]
        rounded[0, head] = turned[:width].astype(bf16)
        log_total[0, head] = turned[width : width + 1]


def attend_backward_kernel(
    offsets,
    starts,
    codes,
    query,
    mixed_grad,
    mixed,
    log_total,
    path,
    key_bits,
    *rest,
    parts,
    key_blocks,
    key_block,
):
    kv_parts = rest[:parts]
    query_grad = rest[parts]
    grad_parts = rest[parts + 1 : 2 * parts + 1]
    (kv_rows, key_columns, padded, padded_grad, query_rows, grad_rows, row_terms, query_sum, kv_sum) = (
        rest[2 * parts + 1 :]
    )
    step = pl.program_id(0)
    heads, width, count = query.shape[1:]

    @pl.when(step == 0)
    def _():
        for n, part in enumerate(kv_parts):
            rows = part.shape[1]
            start = pl.multiple_of(offsets[n], rows)
            key_columns[:, pl.ds(start, rows)] = part[:width, :]
            kv_rows[pl.ds(start, rows), :] = part[...].astype(f32).T.astype(bf16)
        padded[...] = jnp.zeros_like(padded)
        padded_grad[...] = jnp.zeros_like(padded_grad)
        kv_sum[...] = jnp.zeros_like(kv_sum)

    for head in range(heads):
        at = slice(head * count, (head + 1) * count)
        padded[:width, at] = query[0, head]
        padded_grad[width:, at] = mixed_grad[0, head]
        row_terms[0:1, at] = log_total[0, head]
        row_terms[1:2, at] = jnp.sum(
            mixed_grad[0, head].astype(f32) * mixed[0, head], axis=0, keepdims=True
        )
    query_rows[...] = padded[...].astype(f32).T.astype(bf16)
    grad_rows[...] = padded_grad[...].astype(f32).T.astype(bf16)
    query_sum[...] = jnp.zeros_like(query_sum)

    def block(number, masked):
        start = pl.multiple_of(number * key_block, key_block)
        rows = kv_rows[pl.ds(start, key_block), :]
        scores = dot(rows, padded[...])
        if masked:
            keys = start + lax.broadcasted_iota(i32, (key_block, count), 0)
            queries = starts[step] + lax.broadcasted_iota(i32, (key_block, count), 1)
            on_path = (path[0] & column_of(key_bits[:, pl.ds(start, key_block)])) != 0
            allowed = on_path & (keys <= queries)
            scores = jnp.where(jnp.concatenate([allowed] * heads, axis=1), scores, masked_score)
        weights = jnp.exp(scores - row_terms[0:1, :])
        weight_grad = dot(rows, padded_grad[...])
        score_grad = (weights * (weight_grad - row_terms[1:2, :])).astype(bf16)
        kv_sum[pl.ds(start, key_block), :] += dot(score_grad, query_rows[...]) + dot(
            weights.astype(bf16), grad_rows[...]
        )
        query_sum[...] += dot(key_columns[:, pl.ds(start, key_block)], score_grad)

    @pl.loop(0, key_blocks)
    def _(number):
        code = codes[step * key_blocks + number]

        @pl.when(code == 1)
        def _():
            block(number, True)

        @pl.when(code == 2)
        def _():
            block(number, False)

    for head in range(heads):
        query_grad[0, head] = score_scale * query_sum[:, head * count : (head + 1) * count]

    @pl.when(step == pl.num_programs(0) - 1)
    def _():
        for n, part in enumerate(grad_parts):
            rows = part.shape[0]
            part[...] = kv_sum[pl.ds(pl.multiple_of(offsets[n], rows), rows), :].astype(part.dtype)


def whole(shape):
    return pl.BlockSpec(shape, lambda *_: (0,) * len(shape), pipeline_mode=pl.Buffered(1))


def attention_specs(heads, rows, block):
    per_group = rows // block

    def four(step, *_):
        return (step // per_group, 0, 0, step % per_group)

    return pl.BlockSpec((1, heads, HD, block), four), pl.BlockSpec((1, heads, 1, block), four)


def attend_forward(offsets, starts, codes, query, path_bits, key_bits, kv_parts):
    groups, heads, _, rows = query.shape
    block = min(QUERY_BLOCK, rows)
    per_group = rows // block
    tokens = key_bits.shape[1]
    key_block = min(KEY_BLOCK, tokens)
    wide, row = attention_specs(heads, rows, block)
    kernel = functools.partial(
        attend_forward_kernel,
        parts=len(kv_parts),
        key_blocks=tokens // key_block,
        key_block=key_block,
    )
    return pl.pallas_call(
        kernel,
        name="attend_forward",
        grid_spec=pltpu.PrefetchScalarGridSpec(
            num_scalar_prefetch=3,
            grid=(groups * per_group,),
            in_specs=[
                wide,
                pl.BlockSpec((1, 1, block), lambda s, *_: (s // per_group, 0, s % per_group)),
                whole(key_bits.shape),
            ]
            + [whole(p.shape) for p in kv_parts],
            out_specs=[wide, wide, row],
            scratch_shapes=[
                pltpu.VMEM((HD, tokens), bf16),
                pltpu.VMEM((tokens, 2 * HD), bf16),
                pltpu.VMEM((heads * block, HD), bf16),
                pltpu.VMEM((heads * block, 2 * HD), f32),
                pltpu.VMEM((heads * block, 2 * HD), f32),
                pltpu.VMEM((block, 8), i32),
            ],
        ),
        out_shape=[
            jax.ShapeDtypeStruct(query.shape, f32),
            jax.ShapeDtypeStruct(query.shape, bf16),
            jax.ShapeDtypeStruct((groups, heads, 1, rows), f32),
        ],
        compiler_params=pltpu.CompilerParams(
            dimension_semantics=("arbitrary",), vmem_limit_bytes=VMEM_LIMIT
        ),
    )(offsets, starts, codes, query, path_bits[:, None, :], key_bits, *kv_parts)


def attend_backward(
    offsets, starts, codes, query, mixed_grad, mixed, log_total, path_bits, key_bits, kv_parts
):
    groups, heads, _, rows = query.shape
    block = min(QUERY_BLOCK, rows)
    per_group = rows // block
    tokens = key_bits.shape[1]
    key_block = min(KEY_BLOCK, tokens)
    wide, row = attention_specs(heads, rows, block)
    grad_shape = (kv_parts[0].shape[1], 2 * HD)
    kernel = functools.partial(
        attend_backward_kernel,
        parts=len(kv_parts),
        key_blocks=tokens // key_block,
        key_block=key_block,
    )
    outs = pl.pallas_call(
        kernel,
        name="attend_backward",
        grid_spec=pltpu.PrefetchScalarGridSpec(
            num_scalar_prefetch=3,
            grid=(groups * per_group,),
            in_specs=[
                wide,
                wide,
                wide,
                row,
                pl.BlockSpec((1, 1, block), lambda s, *_: (s // per_group, 0, s % per_group)),
                whole(key_bits.shape),
            ]
            + [whole(p.shape) for p in kv_parts],
            out_specs=[wide] + [whole(grad_shape) for _ in kv_parts],
            scratch_shapes=[
                pltpu.VMEM((tokens, 2 * HD), bf16),
                pltpu.VMEM((HD, tokens), bf16),
                pltpu.VMEM((2 * HD, heads * block), bf16),
                pltpu.VMEM((2 * HD, heads * block), bf16),
                pltpu.VMEM((heads * block, 2 * HD), bf16),
                pltpu.VMEM((heads * block, 2 * HD), bf16),
                pltpu.VMEM((8, heads * block), f32),
                pltpu.VMEM((HD, heads * block), f32),
                pltpu.VMEM((tokens, 2 * HD), f32),
            ],
        ),
        out_shape=[jax.ShapeDtypeStruct(query.shape, f32)]
        + [jax.ShapeDtypeStruct(grad_shape, bf16) for _ in kv_parts],
        compiler_params=pltpu.CompilerParams(
            dimension_semantics=("arbitrary",), vmem_limit_bytes=VMEM_LIMIT
        ),
    )(
        offsets,
        starts,
        codes,
        query,
        mixed_grad,
        mixed,
        log_total,
        path_bits[:, None, :],
        key_bits,
        *kv_parts,
    )
    return outs[0], outs[1:]


def place_kernel(offsets, *rest):
    parts, out = rest[:-1], rest[-1]
    for n, part in enumerate(parts):
        rows = part.shape[0]
        out[pl.ds(pl.multiple_of(offsets[n], rows), rows), :] = part[...]


def place_rows(offsets, parts):
    rows, width = parts[0].shape
    return pl.pallas_call(
        place_kernel,
        name="place_rows",
        grid_spec=pltpu.PrefetchScalarGridSpec(
            num_scalar_prefetch=1,
            grid=(1,),
            in_specs=[whole(p.shape) for p in parts],
            out_specs=whole((rows * len(parts), width)),
        ),
        out_shape=jax.ShapeDtypeStruct((rows * len(parts), width), parts[0].dtype),
        compiler_params=pltpu.CompilerParams(vmem_limit_bytes=VMEM_LIMIT),
    )(offsets, *parts)


def rank_kernel(first, route_rows, priority_rows, route_columns, priority_columns, out, *, experts):
    rows = route_rows.shape[2]
    never = rows * TOPK
    for e in range(experts):
        expert = first[0] + e
        along = jnp.min(
            jnp.where(route_rows[0] == expert, priority_rows[0], never), axis=0, keepdims=True
        )
        down = jnp.min(
            jnp.where(route_columns[0] == expert, priority_columns[0], never), axis=1, keepdims=True
        )
        count = jnp.zeros((8, rows), i32)
        for begin in range(0, rows, 8):
            count += (down[begin : begin + 8] < along).astype(i32)
        rank = jnp.sum(count, axis=0, keepdims=True)
        out[0, e : e + 1, :] = jnp.where((along < never) & (rank < CAP), rank, -1)
    if out.shape[1] > experts:
        out[0, experts:, :] = jnp.full((out.shape[1] - experts, rows), -1, i32)


def slot_ranks(first, routes, priority, experts):
    groups, rows, _ = routes.shape
    tall = pl.BlockSpec((1, rows, TOPK), lambda g, *_: (g, 0, 0))
    flat = pl.BlockSpec((1, TOPK, rows), lambda g, *_: (g, 0, 0))
    padded = -(-experts // 8) * 8
    return pl.pallas_call(
        functools.partial(rank_kernel, experts=experts),
        name="slot_ranks",
        grid_spec=pltpu.PrefetchScalarGridSpec(
            num_scalar_prefetch=1,
            grid=(groups,),
            in_specs=[flat, flat, tall, tall],
            out_specs=pl.BlockSpec((1, padded, rows), lambda g, *_: (g, 0, 0)),
        ),
        out_shape=jax.ShapeDtypeStruct((groups, padded, rows), i32),
        compiler_params=pltpu.CompilerParams(vmem_limit_bytes=VMEM_LIMIT),
    )(
        first.reshape(1),
        routes.transpose(0, 2, 1),
        priority.transpose(0, 2, 1),
        routes,
        priority,
    )


def expert_kernel(offsets, first, ranks, *rest, parts, groups):
    gates, rest = rest[:groups], rest[groups:]
    tokens, rest = rest[:groups], rest[groups:]
    grads, rest = rest[:groups], rest[groups:]
    weights = rest[:parts]
    weighted_out, token_grad, inputs, slot_grads, hidden, pair_grads, matrices = rest[parts:]
    rows = tokens[0].shape[0]
    e = pl.program_id(0)
    for n, part in enumerate(weights):
        count = part.shape[2]
        for m in range(3):
            matrices[m, pl.ds(pl.multiple_of(offsets[n], count), count), :] = part[m, 0]
    slot = lax.broadcasted_iota(i32, (SLOTS, rows), 0)
    for g in range(groups):
        at = slice(g * SLOTS, (g + 1) * SLOTS)
        inside = slot == ranks[g, pl.ds(e, 1), :]
        pick = inside.astype(bf16)
        gate = gates[g][pl.ds(first[0] + e, 1), :]
        weight = jnp.sum(jnp.where(inside, gate, 0.0), axis=1, keepdims=True)
        picked = dot(pick, tokens[g][...]).astype(bf16)
        inputs[0, at, :] = picked
        gate_pre = dot(picked, matrices[0])
        up_pre = dot(picked, matrices[1])
        sigma = jax.nn.sigmoid(gate_pre)
        silu = gate_pre * sigma
        active = (silu * up_pre).astype(bf16)
        out = dot_dims(active, matrices[2], 1, 1)
        weighted_out[g, 0] = (out * weight).astype(bf16)
        upstream = dot(pick, grads[g][...])
        pair = jnp.sum(upstream * out, axis=1, keepdims=True)
        pair_grads[g, pl.ds(e, 1), :] = jnp.sum(jnp.where(inside, pair, 0.0), axis=0, keepdims=True)
        slot_grad = (weight * upstream).astype(bf16)
        slot_grads[0, at, :] = slot_grad
        act_grad = dot(slot_grad, matrices[2])
        gate_grad = (act_grad * up_pre * sigma * (1.0 + gate_pre * (1.0 - sigma))).astype(bf16)
        up_grad = (act_grad * silu).astype(bf16)
        hidden[0, 0, at, :] = gate_grad
        hidden[0, 1, at, :] = up_grad
        hidden[0, 2, at, :] = active
        token_grad[g, 0] = (
            dot_dims(gate_grad, matrices[0], 1, 1) + dot_dims(up_grad, matrices[1], 1, 1)
        ).astype(bf16)


def run_experts(offsets, first, ranks, gates, tokens, grads, weight_parts):
    groups = len(tokens)
    rows = tokens[0].shape[0]
    _, experts, part_rows, _ = weight_parts[0].shape
    parts = len(weight_parts)
    slots = groups * SLOTS
    by_group = pl.BlockSpec((groups, 1, SLOTS, D), lambda e, *_: (0, e, 0, 0))
    stash = pl.BlockSpec((1, slots, D), lambda e, *_: (e, 0, 0))
    return pl.pallas_call(
        functools.partial(expert_kernel, parts=parts, groups=groups),
        name="experts",
        grid_spec=pltpu.PrefetchScalarGridSpec(
            num_scalar_prefetch=2,
            grid=(experts,),
            in_specs=[whole(ranks.shape)]
            + [whole((EXPERTS, rows)) for _ in range(groups)]
            + [whole((rows, D)) for _ in range(2 * groups)]
            + [pl.BlockSpec((3, 1, part_rows, H), lambda e, *_: (0, e, 0, 0)) for _ in weight_parts],
            out_specs=[
                by_group,
                by_group,
                stash,
                stash,
                pl.BlockSpec((1, 3, slots, H), lambda e, *_: (e, 0, 0, 0)),
                whole(ranks.shape),
            ],
            scratch_shapes=[pltpu.VMEM((3, D, H), bf16)],
        ),
        out_shape=[
            jax.ShapeDtypeStruct((groups, experts, SLOTS, D), bf16),
            jax.ShapeDtypeStruct((groups, experts, SLOTS, D), bf16),
            jax.ShapeDtypeStruct((experts, slots, D), bf16),
            jax.ShapeDtypeStruct((experts, slots, D), bf16),
            jax.ShapeDtypeStruct((experts, 3, slots, H), bf16),
            jax.ShapeDtypeStruct(ranks.shape, f32),
        ],
        compiler_params=pltpu.CompilerParams(
            dimension_semantics=("arbitrary",), vmem_limit_bytes=VMEM_LIMIT
        ),
    )(
        offsets,
        first.reshape(1),
        ranks,
        *gates,
        *tokens,
        *grads,
        *weight_parts,
    )


def expert_grad_kernel(offsets, inputs, slot_grads, hidden, *rest, pieces):
    outs, total = rest[:-1], rest[-1]
    for m in range(3):
        left = inputs if m < 2 else slot_grads
        total[...] = dot_dims(left[0], hidden[0, m], 0, 0)
        for (n, begin), out in zip(pieces, outs):
            if begin <= m < begin + out.shape[0]:
                count = out.shape[2]
                at = pl.ds(pl.multiple_of(offsets[n], count), count)
                out[m - begin, 0] = total[at, :].astype(bf16)


def expert_grads(offsets, inputs, slot_grads, hidden, parts, cut_parts, part_rows):
    experts, slots, _ = inputs.shape
    stash = pl.BlockSpec((1, slots, D), lambda e, *_: (e, 0, 0))
    pieces = []
    for n in range(parts):
        pieces += [(n, 0, 1), (n, 1, 2)] if n in cut_parts else [(n, 0, 3)]
    outs = pl.pallas_call(
        functools.partial(expert_grad_kernel, pieces=[(n, begin) for n, begin, _ in pieces]),
        name="expert_grads",
        grid_spec=pltpu.PrefetchScalarGridSpec(
            num_scalar_prefetch=1,
            grid=(experts,),
            in_specs=[stash, stash, pl.BlockSpec((1, 3, slots, H), lambda e, *_: (e, 0, 0, 0))],
            out_specs=[
                pl.BlockSpec((held, 1, part_rows, H), lambda e, *_: (0, e, 0, 0))
                for _, _, held in pieces
            ],
            scratch_shapes=[pltpu.VMEM((D, H), f32)],
        ),
        out_shape=[
            jax.ShapeDtypeStruct((held, experts, part_rows, H), bf16) for _, _, held in pieces
        ],
        compiler_params=pltpu.CompilerParams(
            dimension_semantics=("arbitrary",), vmem_limit_bytes=VMEM_LIMIT
        ),
    )(offsets, inputs, slot_grads, hidden)
    found = {}
    for (n, _, _), out in zip(pieces, outs):
        found.setdefault(n, []).append(out)
    return [found[n] for n in range(parts)]


def combine_kernel(ranks, rows_in, out, *, experts, turned):
    count = ranks.shape[1]
    slot = lax.broadcasted_iota(i32, (count, SLOTS), 1)
    pick = jnp.concatenate(
        [(ranks[0, :, e : e + 1] == slot).astype(bf16) for e in range(experts)], axis=1
    )
    total = dot(pick, rows_in[0])
    out[...] = (total.T if turned else total).astype(bf16)


def combine(ranks, slot_rows, g, turned):
    groups, rows, columns = ranks.shape
    experts = slot_rows.shape[1]
    block = min(256, rows)
    return pl.pallas_call(
        functools.partial(combine_kernel, experts=experts, turned=turned),
        name="combine",
        grid=(rows // block,),
        in_specs=[
            pl.BlockSpec((1, block, columns), lambda i: (g, i, 0)),
            pl.BlockSpec(
                (1, experts * SLOTS, D), lambda i: (g, 0, 0), pipeline_mode=pl.Buffered(1)
            ),
        ],
        out_specs=(
            pl.BlockSpec((D, block), lambda i: (0, i))
            if turned
            else pl.BlockSpec((block, D), lambda i: (i, 0))
        ),
        out_shape=jax.ShapeDtypeStruct((D, rows) if turned else (rows, D), bf16),
        compiler_params=pltpu.CompilerParams(vmem_limit_bytes=VMEM_LIMIT),
    )(ranks, slot_rows.reshape(groups, experts * SLOTS, D))


def project_kernel(mixed, x, gain, matrix, middle, normed, inverse):
    branch = dot_dims(mixed[...].astype(f32).T.astype(bf16), matrix[:, :D], 1, 1)
    total = x[...].astype(f32) + branch_scale * branch
    scale = lax.rsqrt(jnp.mean(total * total, axis=1, keepdims=True) + epsilon)
    middle[...] = total
    inverse[...] = scale
    normed[...] = (total * scale * gain[...]).astype(bf16)


def project_out(mixed, x, gain, matrix):
    rows = x.shape[0]
    block = min(256, rows)
    tall = pl.BlockSpec((block, D), lambda i: (i, 0))
    return pl.pallas_call(
        project_kernel,
        name="project_out",
        grid=(rows // block,),
        in_specs=[
            pl.BlockSpec((D, block), lambda i: (0, i)),
            tall,
            whole(gain.shape),
            whole(matrix.shape),
        ],
        out_specs=[tall, tall, pl.BlockSpec((block, 1), lambda i: (i, 0))],
        out_shape=[
            jax.ShapeDtypeStruct((rows, D), f32),
            jax.ShapeDtypeStruct((rows, D), bf16),
            jax.ShapeDtypeStruct((rows, 1), f32),
        ],
        compiler_params=pltpu.CompilerParams(
            dimension_semantics=("arbitrary",), vmem_limit_bytes=VMEM_LIMIT
        ),
    )(mixed, x, gain, matrix)


def rows_of(columns):
    return columns[...].astype(f32).T.astype(bf16)


def matrix_grad_kernel(
    offsets, h_one, project_grad, branch_grad, mixed, h_two, logit_grad, project, *rest
):
    outs, gain, total = rest[:-2], rest[-2], rest[-1]
    wide = project_grad.shape[0]
    end = wide + mixed.shape[0]
    late = dot_dims(h_one[...], rows_of(project_grad), 0, 0)
    gain[...] = jnp.sum(late * project[...].astype(f32), axis=1, keepdims=True)
    total[:, :wide] = late
    total[:, wide:end] = dot_dims(branch_grad[...], rows_of(mixed), 0, 0)
    total[:, end:] = dot_dims(h_two[...], rows_of(logit_grad), 0, 0)
    for k, out in enumerate(outs):
        count, rows, _ = out.shape
        for p in range(count):
            at = pl.ds(pl.multiple_of(offsets[k * count + p], rows), rows)
            out[p] = total[at, :].astype(bf16)


def matrix_grads_of(offsets, share, arrays):
    width = sum(a.shape[0] for a in (arrays[1], arrays[3], arrays[5]))
    count = offsets.shape[0] // share
    out = jax.ShapeDtypeStruct((count, D // (count * share), width), bf16)
    return pl.pallas_call(
        matrix_grad_kernel,
        name="matrix_grads",
        grid_spec=pltpu.PrefetchScalarGridSpec(
            num_scalar_prefetch=1,
            grid=(1,),
            in_specs=[whole(a.shape) for a in arrays],
            out_specs=[whole(out.shape)] * share + [whole((D, 1))],
            scratch_shapes=[pltpu.VMEM((D, width), f32)],
        ),
        out_shape=[out] * share + [jax.ShapeDtypeStruct((D, 1), f32)],
        compiler_params=pltpu.CompilerParams(vmem_limit_bytes=VMEM_LIMIT),
    )(offsets, *arrays)


def rotate(values, cosine, sine):
    first = values[..., : HD // 2, :]
    second = values[..., HD // 2 :, :]
    return jnp.concatenate([first * cosine - second * sine, second * cosine + first * sine], axis=-2)


def rotate_back(values, cosine, sine):
    first = values[..., : HD // 2, :]
    second = values[..., HD // 2 :, :]
    return jnp.concatenate([first * cosine + second * sine, second * cosine - first * sine], axis=-2)


def tree_tables(ancestry, own_all, token_starts, query_block, key_block):
    groups, rows, _ = ancestry.shape
    tokens = own_all.shape[0]
    segments = jnp.arange(SEGS, dtype=i32)
    index = jnp.arange(tokens, dtype=i32)
    member = own_all[None, :] == segments[:, None]
    begin = jnp.min(jnp.where(member, index[None, :], tokens), axis=1)
    length = jnp.sum(member.astype(i32), axis=1)
    on_path = jnp.any(ancestry[:, :, :, None] == segments, axis=2)
    at = token_starts[:, None] + jnp.arange(rows, dtype=i32)[None, :]
    before = jnp.clip(at[:, :, None] - begin, 0, length)
    position = jnp.sum(jnp.where(on_path, before, 0), axis=2)
    bits = jnp.sum(on_path.astype(i32) << segments, axis=2)
    blocked = on_path.reshape(groups * rows // query_block, query_block, SEGS)
    path_any = jnp.any(blocked, axis=1)
    path_all = jnp.all(blocked, axis=1)
    keys = jnp.any(member.reshape(SEGS, tokens // key_block, key_block), axis=2).T
    some = jnp.any(path_any[:, None, :] & keys[None, :, :], axis=2)
    every = jnp.all(path_all[:, None, :] | ~keys[None, :, :], axis=2)
    query_start = at.reshape(-1, query_block)[:, 0]
    key_start = jnp.arange(tokens // key_block, dtype=i32) * key_block
    some &= key_start[None, :] < query_start[:, None] + query_block
    every &= key_start[None, :] + key_block <= query_start[:, None] + 1
    codes = jnp.where(some, jnp.where(every, 2, 1), 0).astype(i32)
    return position, bits, query_start, codes.reshape(-1)


def body(
    layer_input,
    cotangent,
    gain_attention,
    gain_mixture,
    w_query,
    w_key,
    w_value,
    w_out,
    w_router,
    w_gate,
    w_up,
    w_down,
    routes,
    priority,
    ancestry,
):
    chips, share, columns = lax.axis_size("chip"), lax.axis_size("core"), lax.axis_size("col")
    chip, core, column = lax.axis_index("chip"), lax.axis_index("core"), lax.axis_index("col")
    row_axes = ("chip", "core")
    rows, width = layer_input.shape
    weight_rows = w_query.shape[0]
    query_heads = w_query.shape[1] // HD
    key_heads = w_key.shape[1] // HD
    group = query_heads // key_heads
    own_heads = key_heads // share
    experts = w_gate.shape[1] // share
    tokens_all = rows * chips * share
    query_block = min(QUERY_BLOCK, rows)
    key_block = min(KEY_BLOCK, tokens_all)
    token_block = rows // columns

    places = [(chip ^ j) * share + (core ^ h) for j in range(chips) for h in range(share)]
    token_offsets = jnp.stack([p * rows for p in places]).astype(i32)
    feature_offsets = jnp.stack([p * weight_rows for p in places]).astype(i32)

    def groups_of(values):
        return [values] + ([swap_core(values)] if share == 2 else [])

    x_full = lax.all_gather(layer_input, "col", axis=1, tiled=True)
    index_groups = groups_of(jnp.concatenate([routes, priority, ancestry], axis=1))
    index_arrays = jnp.stack(index_groups)

    own_all = lax.all_gather(ancestry[:, 0], row_axes, axis=0, tiled=True)
    project_part = jnp.concatenate([w_query, w_key, w_value], axis=1)
    levels_here = range(len(chip_bits(chips)))
    project_parts = shared_level([project_part], 0)
    own_all, project_parts = tie(own_all, project_parts)
    for level in levels_here[1:]:
        project_parts = shared_level(project_parts, level)

    stacked = jnp.stack([m.transpose(1, 0, 2) for m in (w_gate, w_up, w_down)])
    stacked = stacked.reshape(3, share, experts, weight_rows, H).transpose(1, 0, 2, 3, 4)
    own_weights, other_weights = own_and_other(stacked, core, share)
    starts = [own_weights] + ([swap_core(other_weights)] if share == 2 else [])
    project_parts, starts, index_arrays = tie(project_parts, starts, index_arrays)
    all_routes = index_arrays[:, :, :TOPK]
    all_priority = index_arrays[:, :, TOPK : 2 * TOPK]
    all_ancestry = index_arrays[:, :, 2 * TOPK :]
    project = shared_rows(project_parts)
    rounds = gather_rounds(chips, share)
    weights_held = run_gather({(h, 0): v for h, v in enumerate(starts)}, rounds[:1])
    gains = column_rows(jnp.concatenate([gain_attention, gain_mixture])[None, :])
    gains = gains.reshape(columns, 2, width).transpose(1, 0, 2).reshape(2, D)

    token_starts = jnp.stack([(chip * share + (core ^ g)) * rows for g in range(share)]).astype(i32)
    position, path_bits, query_starts, codes = tree_tables(
        all_ancestry, own_all, token_starts, query_block, key_block
    )
    frequency = rope_base ** (-(jnp.arange(HD // 2, dtype=f32) * 2.0) / HD)
    angle = position.astype(f32)[:, None, :] * frequency[None, :, None]
    by_rows = Layout(major_to_minor=(0, 1, 2))
    cosine = with_layout_constraint(jnp.cos(angle), by_rows)
    sine = with_layout_constraint(jnp.sin(angle), by_rows)
    first_expert = (column * (experts * share) + core * experts).astype(i32)
    ranks = slot_ranks(first_expert, all_routes, all_priority, experts)
    rank_columns = ranks.transpose(0, 2, 1)
    expert_ids = jnp.arange(EXPERTS, dtype=i32)
    chosen = jnp.any(all_routes[:, None, :, :] == expert_ids[None, :, None, None], axis=3)

    key_bits = (jnp.int32(1) << own_all)[None, :]
    early_tables = (ranks, rank_columns, codes, path_bits, chosen, cosine, sine, project)
    x_full, w_out_here, early_tables = tie(x_full, w_out, early_tables)
    ranks, rank_columns, codes, path_bits, chosen, cosine, sine, project = early_tables
    out_columns = jnp.zeros((weight_rows, D), bf16)
    for c, part in [(column, w_out_here)] + column_shifts(lambda _: w_out_here):
        out_columns = lax.dynamic_update_slice_in_dim(out_columns, part, c * part.shape[1], 1)
    cotangent_here, out_columns = tie(cotangent, out_columns)
    cotangent_full = lax.all_gather(cotangent_here, "col", axis=1, tiled=True)
    tables = (ranks, rank_columns, cosine, sine, path_bits, codes, chosen, key_bits, project, gains)
    out_parts = [jnp.concatenate([out_columns, w_router], axis=1)]
    x_full, weights_held, tables = tie(x_full, weights_held, tables)
    ranks, rank_columns, cosine, sine, path_bits, codes, chosen, key_bits, project, gains = tables
    x_wide = x_full.astype(f32)
    inverse_one = lax.rsqrt(jnp.mean(x_wide * x_wide, axis=1, keepdims=True) + epsilon)
    h_one = (x_wide * inverse_one * gains[0][None, :]).astype(bf16)
    projected = dot_dims(project, h_one, 0, 1)
    query_width, key_width = query_heads * HD, key_heads * HD
    query = rotate(
        projected[:query_width].reshape(share, own_heads, group, HD, rows), cosine[0], sine[0]
    )
    query = (query.astype(bf16).astype(f32) * score_scale).astype(bf16)
    keys = rotate(
        projected[query_width : query_width + key_width].reshape(share, own_heads, HD, rows),
        cosine[0],
        sine[0],
    ).astype(bf16)
    values = projected[query_width + key_width :].reshape(share, own_heads, HD, rows).astype(bf16)
    sent = jnp.concatenate([keys[:, :, None], values[:, :, None], query], axis=2)
    own_sent, other_sent = own_and_other(sent, core, share)
    received = [own_sent] + ([swap_core(other_sent)] if share == 2 else [])
    query_groups = jnp.stack([r[:, 2:] for r in received], axis=1)
    pairs = [r[:, :2].reshape(own_heads, 2 * HD, rows) for r in received]
    for level in levels_here:
        out_parts = shared_level(out_parts, level)
    pairs, weights_held, out_parts = tie(pairs, weights_held, out_parts)
    kv_parts = gather_parts(pairs, chips)
    kv_parts, weights_held = tie(kv_parts, weights_held)
    weights_held = run_gather(weights_held, rounds[1 : len(rounds) - 1])

    attend_outs = [
        attend_forward(
            token_offsets,
            query_starts,
            codes,
            query_groups[head],
            path_bits,
            key_bits,
            [p[head] for p in kv_parts],
        )
        for head in range(own_heads)
    ]
    mixed_b = jnp.stack([o[1] for o in attend_outs])
    mixed_b, weights_held, cotangent_full, out_parts = tie(
        mixed_b, weights_held, cotangent_full, out_parts
    )
    out_router = shared_rows(out_parts)
    weights_held = run_gather(weights_held, rounds[len(rounds) - 1 :])
    mixed_other = swap_core(mixed_b[:, 1]) if share == 2 else None
    mixed = in_core_order(mixed_b[:, 0], mixed_other, core).reshape(query_width, rows)
    mixed_full = lax.all_gather(mixed, "col", axis=0, tiled=True)
    mixed_full, weights_held, out_router = tie(mixed_full, weights_held, out_router)
    mix_grads = groups_of((branch_scale * cotangent_full.astype(f32)).astype(bf16))
    x_middle, h_two, inverse_two = project_out(
        mixed_full, x_full, gains[1:2], out_router
    )
    full_router = out_router[:, D:]
    h_two_groups = groups_of(h_two)

    def gates_of(tokens, picks):
        logits = dot_dims(full_router, tokens, 0, 1)
        shown = jnp.where(picks, logits, masked_score)
        raised = jnp.where(picks, jnp.exp(logits - jnp.max(shown, axis=0, keepdims=True)), 0.0)
        return raised / jnp.sum(raised, axis=0, keepdims=True)

    gates = [gates_of(h_two_groups[g], chosen[g]) for g in range(share)]
    weighted_out, slot_token_grads, inputs, slot_grads, hidden, pair_rows = run_experts(
        feature_offsets,
        first_expert,
        ranks,
        gates,
        h_two_groups,
        mix_grads,
        listed(weights_held, chips),
    )

    def combine_groups(slot_rows, turned):
        if share == 1:
            return combine(rank_columns, slot_rows, 0, turned)
        received = swap_core(combine(rank_columns, slot_rows, 1, turned))
        own = combine(rank_columns, slot_rows, 0, turned)
        return (own.astype(f32) + received.astype(f32)).astype(bf16)

    token_sum = combine_groups(slot_token_grads, False)
    token_grads = lax.psum_scatter(token_sum, "col", scatter_dimension=0, tiled=True)
    pair_other = swap_core(pair_rows[1, :experts]) if share == 2 else None
    pair_columns = in_core_order(pair_rows[0, :experts], pair_other, core)
    pair_columns = pair_columns.reshape(share * experts, rows)
    pair_grad = column_rows(pair_columns)
    picked_grad = gates[0] * (pair_grad - jnp.sum(gates[0] * pair_grad, axis=0, keepdims=True))
    logit_grad = picked_grad.astype(bf16)
    mix_sum = combine_groups(weighted_out, True)

    levels = reduce_levels(chips, share)
    first = [[m for m in moves if m[1]] for moves in levels[0]]
    last = [[m for m in moves if not m[1]] for moves in levels[0]]
    sent = {(h, j ^ bit) for moves in first for h, j, bit in moves}
    last_sent = {(h, j ^ bit) for moves in last for h, j, bit in moves}
    parts = expert_grads(
        feature_offsets,
        inputs,
        slot_grads,
        hidden,
        chips * share,
        {j * share + h for h, j in sent | last_sent},
        weight_rows,
    )
    sums_held = {(h, j): parts[j * share + h] for j in range(chips) for h in range(share)}

    def take_piece(rounds_here, held):
        taken = {}
        for moves in rounds_here:
            taken.update(take(held, moves))
        return taken

    first_taken = take_piece(first, {k: sums_held[k][0] for k in sent})
    staying = [sums_held[h, 0][0] for h in range(share)]
    token_grads, staying, mix_sum, logit_grad, first_taken = tie(
        token_grads, staying, mix_sum, logit_grad, first_taken
    )
    token_grads = token_grads.astype(f32)
    second_taken = take_piece(first, {k: sums_held[k][1] for k in sent})

    token_start = column * token_block

    def own_tokens(array):
        return lax.dynamic_slice_in_dim(array, token_start, token_block, 0)

    h_two_grad = token_grads + dot_dims(
        lax.dynamic_slice_in_dim(logit_grad, token_start, token_block, 1), full_router, 0, 1
    )
    x_part, inverse_part = own_tokens(x_middle), own_tokens(inverse_two)
    scaled_two = h_two_grad * gains[1][None, :]
    inner_two = jnp.sum(scaled_two * x_part, axis=1, keepdims=True)
    x_middle_grad = (
        own_tokens(cotangent_full).astype(f32)
        + inverse_part * scaled_two
        - x_part * inverse_part**3 * inner_two / D
    )
    gain_mixture_part = jnp.sum(h_two_grad * x_part * inverse_part, axis=0)
    branch_part = (branch_scale * x_middle_grad).astype(bf16)
    mixed_parts = dot(branch_part, out_router[:, :D]).astype(bf16)
    mixed_parts = mixed_parts.reshape(token_block, columns, query_width).transpose(1, 0, 2)
    mixed_grad = lax.all_to_all(mixed_parts, "col", split_axis=0, concat_axis=0, tiled=True)
    mixed_grad, branch_part, mix_sum, second_taken = tie(
        mixed_grad, branch_part, mix_sum, second_taken
    )
    branch_grad = lax.all_gather(branch_part, "col", axis=0, tiled=True)
    sums_here = {}
    for k, part in first_taken.items():
        taken = jnp.concatenate([part, second_taken[k]])
        sums_here[k] = (sums_held[k][0].astype(f32) + taken.astype(f32)).astype(bf16)

    mixed_grad = mixed_grad.reshape(rows, query_width).T
    mixed_grad, sums_here = tie(mixed_grad, sums_here)
    own_grad, other_grad = own_and_other(
        mixed_grad.reshape(share, own_heads, group, HD, rows), core, share
    )
    arrived = [[part] for part in staying]
    for rounds_here in levels[1:]:
        passed = {}
        for moves in rounds_here:
            passed.update(take(sums_here, moves))
        for h in range(share):
            if (h, 0) in passed:
                arrived[h].append(passed.pop((h, 0)))
        sums_here = add_taken(sums_here, passed)
    last_begin = {k: sums_held[k][0] for k in last_sent}
    last_rest = {k: sums_held[k][1] for k in last_sent}
    last_rest, own_grad = tie(last_rest, own_grad)
    last_rest = take_piece(last, last_rest)
    grad_groups = jnp.stack(
        [own_grad] + ([swap_core(other_grad)] if share == 2 else []), axis=1
    )
    backward_outs = [
        attend_backward(
            token_offsets,
            query_starts,
            codes,
            query_groups[head],
            grad_groups[head],
            attend_outs[head][0],
            attend_outs[head][2],
            path_bits,
            key_bits,
            [p[head] for p in kv_parts],
        )
        for head in range(own_heads)
    ]
    mix_slice = lax.psum_scatter(mix_sum, "col", scatter_dimension=0, tiled=True).astype(f32).T
    feature_start = column * width
    x_middle_slice = lax.dynamic_slice_in_dim(x_middle, feature_start, width, 1)
    result = (x_middle_slice + branch_scale * mix_slice).astype(bf16)
    backward_outs, arrived, branch_later, last_rest = tie(
        backward_outs, arrived, branch_grad, last_rest
    )
    query_grad = jnp.stack([o[0] for o in backward_outs])
    query_grad = rotate_back(query_grad, cosine[None, :, None], sine[None, :, None]).astype(bf16)
    query_other = swap_core(query_grad[:, 1]) if share == 2 else None
    query_pre_grad = in_core_order(query_grad[:, 0], query_other, core).reshape(query_width, rows)
    kv_sums = reduce_parts(
        [jnp.stack([o[1][n] for o in backward_outs]) for n in range(chips * share)], chips, share
    )
    kv_other = swap_core(kv_sums[1]) if share == 2 else None
    kv_grad = in_core_order(kv_sums[0], kv_other, core).astype(f32)
    kv_grad, last_begin = tie(kv_grad, last_begin)
    last_begin = take_piece(last, last_begin)
    for h in range(share):
        for k in last_rest:
            if k[0] == h:
                arrived[h].append(jnp.concatenate([last_begin[k], last_rest[k]]))
    kv_grad = kv_grad.transpose(0, 1, 3, 2).reshape(key_heads, 2 * HD, rows)
    key_pre_grad = (
        rotate_back(kv_grad[:, :HD], cosine[0], sine[0]).astype(bf16).reshape(key_width, rows)
    )
    value_pre_grad = kv_grad[:, HD:].astype(bf16).reshape(key_width, rows)
    project_grad = jnp.concatenate([query_pre_grad, key_pre_grad, value_pre_grad], axis=0)

    (project_grad,) = tie(project_grad)
    h_one_part = dot(project, project_grad).astype(bf16)
    h_one_part, project_grad = tie(h_one_part, project_grad)
    h_one_grad = lax.psum_scatter(h_one_part, "col", scatter_dimension=0, tiled=True)
    inner_one = column_sum(jnp.sum(project_grad.astype(f32) * projected, axis=0))[:, None]
    sums = [functools.reduce(jnp.add, [p.astype(f32) for p in own]).astype(bf16) for own in arrived]
    small_places = shared_places(chips, share, core)
    if share == 2:
        small_places = small_places + shared_places(chips, share, 1 - core)
    *small_parts, gain_column = matrix_grads_of(
        jnp.stack([p * weight_rows for p in small_places]).astype(i32),
        share,
        (h_one, project_grad, branch_later, mixed, h_two, logit_grad, project),
    )
    gain_attention_part = gain_column[:, 0] / gains[0]
    gain_parts = jnp.stack([gain_attention_part, gain_mixture_part])

    def own_features(array, c):
        return lax.dynamic_slice_in_dim(array, c * width, width, 1)

    gain_sums = own_features(gain_parts, column)
    for _, other in column_shifts(lambda c: own_features(gain_parts, c)):
        gain_sums = gain_sums + other
    small_parts, sums = tie(small_parts, sums)
    returned = swap_core(sums[1]) if share == 2 else None
    small_sum = shared_reduce(small_parts[0], small_parts[1] if share == 2 else None)
    gain_sums = row_sum(gain_sums)
    matrix_grads = [
        in_core_order(sums[0][m], None if returned is None else returned[m], core)
        .astype(f32)
        .reshape(share * experts, weight_rows, H)
        .transpose(1, 0, 2)
        for m in range(3)
    ]
    h_one_grad, matrix_grads, small_sum, gain_sums, inner_one = tie(
        h_one_grad, matrix_grads, small_sum, gain_sums, inner_one
    )
    x_slice = layer_input.astype(f32)
    middle_slice = lax.dynamic_slice_in_dim(branch_grad, feature_start, width, 1).astype(f32)
    input_grad = (
        middle_slice * (1.0 / branch_scale)
        + inverse_one * h_one_grad.astype(f32).T * gain_attention[None, :]
        - x_slice * inverse_one**2 * inner_one / D
    )
    kv_width = query_width + 2 * key_width
    return (
        result,
        input_grad,
        gain_sums[0],
        gain_sums[1],
        small_sum[:, :query_width],
        small_sum[:, query_width : query_width + key_width],
        small_sum[:, query_width + key_width : kv_width],
        small_sum[:, kv_width : kv_width + query_width],
        small_sum[:, kv_width + query_width :],
        *matrix_grads,
    )


def solution(mesh):
    rows, columns = mesh.shape["row"], mesh.shape["col"]
    halves = rows % 2 == 0 and EXPERTS // columns % 2 == 0 and KVH // columns % 2 == 0
    share = 2 if halves else 1
    split = Mesh(mesh.devices.reshape(rows // share, share, columns), ("chip", "core", "col"))
    row = ("chip", "core")
    return jax.shard_map(
        body,
        mesh=split,
        in_specs=(
            P(row, "col"),
            P(row, "col"),
            P("col"),
            P("col"),
            P(row, "col"),
            P(row, "col"),
            P(row, "col"),
            P(row, "col"),
            P(row, None),
            P(row, "col", None),
            P(row, "col", None),
            P(row, "col", None),
            P(row, None),
            P(row, None),
            P(row, None),
        ),
        out_specs=(
            P(row, "col"),
            P(row, "col"),
            P("col"),
            P("col"),
            P(row, "col"),
            P(row, "col"),
            P(row, "col"),
            P(row, "col"),
            P(row, None),
            P(row, "col", None),
            P(row, "col", None),
            P(row, "col", None),
        ),
        check_vma=False,
    )
```

```python
import functools

import jax
import jax.numpy as jnp
from jax import lax
from jax.experimental.layout import Layout, with_layout_constraint
from jax.experimental import pallas as pl
from jax.experimental.pallas import tpu as pltpu
from jax.sharding import Mesh
from jax.sharding import PartitionSpec as P

D = 1536
HD = 64
H = 512
KVH = 8
EXPERTS = 40
TOPK = 8
SEGS = 13
CAP = 230
SLOTS = 256

epsilon = 1e-06
branch_scale = 0.22
score_scale = 0.015625
rope_base = 10000.0
masked_score = -1e30

bf16 = jnp.bfloat16
f32 = jnp.float32
i32 = jnp.int32

QUERY_BLOCK = 512
KEY_BLOCK = 512
VMEM_LIMIT = 60 * 1024 * 1024


def dot(left, right):
    return jnp.dot(left, right, preferred_element_type=f32)


def dot_dims(left, right, left_dim, right_dim):
    return lax.dot_general(
        left, right, (((left_dim,), (right_dim,)), ((), ())), preferred_element_type=f32
    )


def swap(values, axis, bit):
    size = lax.axis_size(axis)
    return lax.ppermute(values, axis, [(i, i ^ bit) for i in range(size)])


def swap_core(values):
    return swap(values, "core", 1)


def chip_bits(chips):
    return [1 << b for b in range(chips.bit_length() - 1)]


def half_bits(chips, half):
    bits = chip_bits(chips)
    return bits if half == 0 else bits[::-1]


def gather_rounds(chips, halves):
    rounds = []
    for level in range(len(chip_bits(chips))):
        moves = []
        for half in range(halves):
            bits = half_bits(chips, half)
            held = [0]
            for bit in bits[:level]:
                held += [j ^ bit for j in held]
            moves.append([(half, j, bits[level]) for j in sorted(held)])
        rounds += [list(r) for r in zip(*moves)]
    return rounds


def run_gather(held, rounds):
    held = dict(held)
    for moves in rounds:
        for half, j, bit in moves:
            held[half, j ^ bit] = swap(held[half, j], "chip", bit)
    return held


def gather_parts(values, chips):
    held = run_gather(
        {(h, 0): v for h, v in enumerate(values)}, gather_rounds(chips, len(values))
    )
    return listed(held, chips)


def listed(held, chips):
    halves = len(held) // chips
    return [held[h, j] for j in range(chips) for h in range(halves)]


def reduce_levels(chips, halves):
    levels = []
    for level in range(len(chip_bits(chips))):
        moves = []
        for half in range(halves):
            bits = half_bits(chips, half)
            done = sum(bits[: level + 1])
            moves.append([(half, j, bits[level]) for j in range(chips) if not j & done])
        levels.append([list(r) for r in zip(*moves)])
    return levels


def take(held, moves):
    return {(h, j): swap(held[h, j ^ bit], "chip", bit) for h, j, bit in moves}


def add_taken(held, taken):
    sums = {k: (held[k].astype(f32) + v.astype(f32)).astype(v.dtype) for k, v in taken.items()}
    return {**held, **sums}


def reduce_parts(parts, chips, share):
    held = {(h, j): parts[j * share + h] for j in range(chips) for h in range(share)}
    for rounds in reduce_levels(chips, share):
        taken = {}
        for moves in rounds:
            taken.update(take(held, moves))
        held = add_taken(held, taken)
    return [held[h, 0] for h in range(share)]


def pick(core, values):
    return jnp.where(core == 0, values[0], values[-1])


def shared_places(chips, share, core):
    chip = lax.axis_index("chip")
    places = []
    for p in range(chips):
        jumps = [
            sum(b for t, b in enumerate(half_bits(chips, k)) if p >> t & 1) for k in range(share)
        ]
        places.append((chip ^ pick(core, jumps)) * share + core)
    return places


def shared_swap(values, level):
    chips, share = lax.axis_size("chip"), lax.axis_size("core")
    pairs = [
        (c * share + k, (c ^ half_bits(chips, k)[level]) * share + k)
        for c in range(chips)
        for k in range(share)
    ]
    return lax.ppermute(values, ("chip", "core"), pairs)


def shared_level(blocks, level):
    return blocks + [shared_swap(b, level) for b in blocks]


def shared_rows(blocks):
    chips, share, core = lax.axis_size("chip"), lax.axis_size("core"), lax.axis_index("core")
    places = shared_places(chips, share, core)
    parts = list(blocks)
    if share == 2:
        parts += [swap_core(b) for b in blocks]
        places = places + shared_places(chips, share, 1 - core)
    rows = blocks[0].shape[0]
    return place_rows(jnp.stack([p * rows for p in places]).astype(i32), parts)


def shared_reduce(held, other):
    def add(left, right):
        return (left.astype(f32) + right.astype(f32)).astype(left.dtype)

    if other is not None:
        held = add(held, swap_core(other))
    for level in reversed(range(len(chip_bits(lax.axis_size("chip"))))):
        half = 1 << level
        held = add(held[:half], shared_swap(held[half:], level))
    return held[0].astype(f32)


def column_shifts(values_for):
    size = lax.axis_size("col")
    me = lax.axis_index("col")
    return [
        (
            (me - d) % size,
            lax.ppermute(values_for((me + d) % size), "col", [(i, (i + d) % size) for i in range(size)]),
        )
        for d in range(1, size)
    ]


def column_sum(values):
    for _, other in column_shifts(lambda _: values):
        values = values + other
    return values


def column_rows(values):
    rows = values.shape[0]
    size = lax.axis_size("col")
    out = jnp.zeros((size * rows,) + values.shape[1:], values.dtype)
    for c, part in [(lax.axis_index("col"), values)] + column_shifts(lambda _: values):
        out = lax.dynamic_update_slice_in_dim(out, part, c * rows, 0)
    return out


def row_sum(values):
    for axis in ("core", "chip"):
        for bit in chip_bits(lax.axis_size(axis)):
            values = values + swap(values, axis, bit)
    return values


def tie(*trees):
    return lax.optimization_barrier(trees)


def own_and_other(values, core, share):
    if share == 1:
        return values[0], None
    mine = lax.dynamic_index_in_dim(values, core, 0, keepdims=False)
    other = lax.dynamic_index_in_dim(values, 1 - core, 0, keepdims=False)
    return mine, other


def in_core_order(mine, other, core):
    if other is None:
        return mine[None]
    first = core == 0
    return jnp.stack([jnp.where(first, mine, other), jnp.where(first, other, mine)])


def column_of(row):
    return jnp.broadcast_to(row, (8, row.shape[1])).T[:, :1]


def attend_forward_kernel(
    offsets, starts, codes, query, path, key_bits, *rest, parts, key_blocks, key_block
):
    kv_parts = rest[:parts]
    out, rounded, log_total, key_columns, value_rows, query_rows, peak, mixed, paths = rest[parts:]
    step = pl.program_id(0)
    heads, width, count = query.shape[1:]

    @pl.when(step == 0)
    def _():
        for n, part in enumerate(kv_parts):
            rows = part.shape[1]
            start = pl.multiple_of(offsets[n], rows)
            key_columns[:, pl.ds(start, rows)] = part[:width, :]
            turned = pltpu.roll(part[...].astype(f32).T, width, 1)
            lane = lax.broadcasted_iota(i32, turned.shape, 1)
            value_rows[pl.ds(start, rows), :] = jnp.where(lane < width, turned, 1.0).astype(bf16)

    for head in range(heads):
        query_rows[head * count : (head + 1) * count] = query[0, head].astype(f32).T.astype(bf16)
    paths[...] = jnp.broadcast_to(path[0], (8, count)).T
    peak[...] = jnp.full_like(peak, masked_score)
    mixed[...] = jnp.zeros_like(mixed)

    def block(number, masked):
        start = pl.multiple_of(number * key_block, key_block)
        scores = dot(query_rows[...], key_columns[:, pl.ds(start, key_block)])
        if masked:
            keys = start + lax.broadcasted_iota(i32, (count, key_block), 1)
            queries = starts[step] + lax.broadcasted_iota(i32, (count, key_block), 0)
            on_path = (paths[:, :1] & key_bits[:, pl.ds(start, key_block)]) != 0
            allowed = on_path & (keys <= queries)
            scores = jnp.where(
                allowed[None], scores.reshape(heads, count, key_block), masked_score
            ).reshape(heads * count, key_block)
        old = peak[...]
        new = jnp.maximum(old, jnp.max(scores, axis=1, keepdims=True))
        weights = jnp.exp(scores - jnp.tile(new, (1, key_block // 128))).astype(bf16)
        mixed[...] = mixed[...] * jnp.exp(old - new) + dot(
            weights, value_rows[pl.ds(start, key_block), :]
        )
        peak[...] = new

    @pl.loop(0, key_blocks)
    def _(number):
        code = codes[step * key_blocks + number]

        @pl.when(code == 1)
        def _():
            block(number, True)

        @pl.when(code == 2)
        def _():
            block(number, False)

    lane = lax.broadcasted_iota(i32, (count, 2 * width), 1)
    for head in range(heads):
        at = slice(head * count, (head + 1) * count)
        sums = mixed[at]
        turned = jnp.where(
            lane < width, sums / pltpu.roll(sums, width, 1), peak[at] + jnp.log(sums)
        ).T
        out[0, head] = turned[:width]
        rounded[0, head] = turned[:width].astype(bf16)
        log_total[0, head] = turned[width : width + 1]


def attend_backward_kernel(
    offsets,
    starts,
    codes,
    query,
    mixed_grad,
    mixed,
    log_total,
    path,
    key_bits,
    *rest,
    parts,
    key_blocks,
    key_block,
):
    kv_parts = rest[:parts]
    query_grad = rest[parts]
    grad_parts = rest[parts + 1 : 2 * parts + 1]
    (kv_rows, key_columns, padded, padded_grad, query_rows, grad_rows, row_terms, query_sum, kv_sum) = (
        rest[2 * parts + 1 :]
    )
    step = pl.program_id(0)
    heads, width, count = query.shape[1:]

    @pl.when(step == 0)
    def _():
        for n, part in enumerate(kv_parts):
            rows = part.shape[1]
            start = pl.multiple_of(offsets[n], rows)
            key_columns[:, pl.ds(start, rows)] = part[:width, :]
            kv_rows[pl.ds(start, rows), :] = part[...].astype(f32).T.astype(bf16)
        padded[...] = jnp.zeros_like(padded)
        padded_grad[...] = jnp.zeros_like(padded_grad)
        kv_sum[...] = jnp.zeros_like(kv_sum)

    for head in range(heads):
        at = slice(head * count, (head + 1) * count)
        padded[:width, at] = query[0, head]
        padded_grad[width:, at] = mixed_grad[0, head]
        row_terms[0:1, at] = log_total[0, head]
        row_terms[1:2, at] = jnp.sum(
            mixed_grad[0, head].astype(f32) * mixed[0, head], axis=0, keepdims=True
        )
    query_rows[...] = padded[...].astype(f32).T.astype(bf16)
    grad_rows[...] = padded_grad[...].astype(f32).T.astype(bf16)
    query_sum[...] = jnp.zeros_like(query_sum)

    def block(number, masked):
        start = pl.multiple_of(number * key_block, key_block)
        rows = kv_rows[pl.ds(start, key_block), :]
        scores = dot(rows, padded[...])
        if masked:
            keys = start + lax.broadcasted_iota(i32, (key_block, count), 0)
            queries = starts[step] + lax.broadcasted_iota(i32, (key_block, count), 1)
            on_path = (path[0] & column_of(key_bits[:, pl.ds(start, key_block)])) != 0
            allowed = on_path & (keys <= queries)
            scores = jnp.where(jnp.concatenate([allowed] * heads, axis=1), scores, masked_score)
        weights = jnp.exp(scores - row_terms[0:1, :])
        weight_grad = dot(rows, padded_grad[...])
        score_grad = (weights * (weight_grad - row_terms[1:2, :])).astype(bf16)
        kv_sum[pl.ds(start, key_block), :] += dot(score_grad, query_rows[...]) + dot(
            weights.astype(bf16), grad_rows[...]
        )
        query_sum[...] += dot(key_columns[:, pl.ds(start, key_block)], score_grad)

    @pl.loop(0, key_blocks)
    def _(number):
        code = codes[step * key_blocks + number]

        @pl.when(code == 1)
        def _():
            block(number, True)

        @pl.when(code == 2)
        def _():
            block(number, False)

    for head in range(heads):
        query_grad[0, head] = score_scale * query_sum[:, head * count : (head + 1) * count]

    @pl.when(step == pl.num_programs(0) - 1)
    def _():
        for n, part in enumerate(grad_parts):
            rows = part.shape[0]
            part[...] = kv_sum[pl.ds(pl.multiple_of(offsets[n], rows), rows), :].astype(part.dtype)


def whole(shape):
    return pl.BlockSpec(shape, lambda *_: (0,) * len(shape), pipeline_mode=pl.Buffered(1))


def attention_specs(heads, rows, block):
    per_group = rows // block

    def four(step, *_):
        return (step // per_group, 0, 0, step % per_group)

    return pl.BlockSpec((1, heads, HD, block), four), pl.BlockSpec((1, heads, 1, block), four)


def attend_forward(offsets, starts, codes, query, path_bits, key_bits, kv_parts):
    groups, heads, _, rows = query.shape
    block = min(QUERY_BLOCK, rows)
    per_group = rows // block
    tokens = key_bits.shape[1]
    key_block = min(KEY_BLOCK, tokens)
    wide, row = attention_specs(heads, rows, block)
    kernel = functools.partial(
        attend_forward_kernel,
        parts=len(kv_parts),
        key_blocks=tokens // key_block,
        key_block=key_block,
    )
    return pl.pallas_call(
        kernel,
        name="attend_forward",
        grid_spec=pltpu.PrefetchScalarGridSpec(
            num_scalar_prefetch=3,
            grid=(groups * per_group,),
            in_specs=[
                wide,
                pl.BlockSpec((1, 1, block), lambda s, *_: (s // per_group, 0, s % per_group)),
                whole(key_bits.shape),
            ]
            + [whole(p.shape) for p in kv_parts],
            out_specs=[wide, wide, row],
            scratch_shapes=[
                pltpu.VMEM((HD, tokens), bf16),
                pltpu.VMEM((tokens, 2 * HD), bf16),
                pltpu.VMEM((heads * block, HD), bf16),
                pltpu.VMEM((heads * block, 2 * HD), f32),
                pltpu.VMEM((heads * block, 2 * HD), f32),
                pltpu.VMEM((block, 8), i32),
            ],
        ),
        out_shape=[
            jax.ShapeDtypeStruct(query.shape, f32),
            jax.ShapeDtypeStruct(query.shape, bf16),
            jax.ShapeDtypeStruct((groups, heads, 1, rows), f32),
        ],
        compiler_params=pltpu.CompilerParams(
            dimension_semantics=("arbitrary",), vmem_limit_bytes=VMEM_LIMIT
        ),
    )(offsets, starts, codes, query, path_bits[:, None, :], key_bits, *kv_parts)


def attend_backward(
    offsets, starts, codes, query, mixed_grad, mixed, log_total, path_bits, key_bits, kv_parts
):
    groups, heads, _, rows = query.shape
    block = min(QUERY_BLOCK, rows)
    per_group = rows // block
    tokens = key_bits.shape[1]
    key_block = min(KEY_BLOCK, tokens)
    wide, row = attention_specs(heads, rows, block)
    grad_shape = (kv_parts[0].shape[1], 2 * HD)
    kernel = functools.partial(
        attend_backward_kernel,
        parts=len(kv_parts),
        key_blocks=tokens // key_block,
        key_block=key_block,
    )
    outs = pl.pallas_call(
        kernel,
        name="attend_backward",
        grid_spec=pltpu.PrefetchScalarGridSpec(
            num_scalar_prefetch=3,
            grid=(groups * per_group,),
            in_specs=[
                wide,
                wide,
                wide,
                row,
                pl.BlockSpec((1, 1, block), lambda s, *_: (s // per_group, 0, s % per_group)),
                whole(key_bits.shape),
            ]
            + [whole(p.shape) for p in kv_parts],
            out_specs=[wide] + [whole(grad_shape) for _ in kv_parts],
            scratch_shapes=[
                pltpu.VMEM((tokens, 2 * HD), bf16),
                pltpu.VMEM((HD, tokens), bf16),
                pltpu.VMEM((2 * HD, heads * block), bf16),
                pltpu.VMEM((2 * HD, heads * block), bf16),
                pltpu.VMEM((heads * block, 2 * HD), bf16),
                pltpu.VMEM((heads * block, 2 * HD), bf16),
                pltpu.VMEM((8, heads * block), f32),
                pltpu.VMEM((HD, heads * block), f32),
                pltpu.VMEM((tokens, 2 * HD), f32),
            ],
        ),
        out_shape=[jax.ShapeDtypeStruct(query.shape, f32)]
        + [jax.ShapeDtypeStruct(grad_shape, bf16) for _ in kv_parts],
        compiler_params=pltpu.CompilerParams(
            dimension_semantics=("arbitrary",), vmem_limit_bytes=VMEM_LIMIT
        ),
    )(
        offsets,
        starts,
        codes,
        query,
        mixed_grad,
        mixed,
        log_total,
        path_bits[:, None, :],
        key_bits,
        *kv_parts,
    )
    return outs[0], outs[1:]


def place_kernel(offsets, *rest):
    parts, out = rest[:-1], rest[-1]
    for n, part in enumerate(parts):
        rows = part.shape[0]
        out[pl.ds(pl.multiple_of(offsets[n], rows), rows), :] = part[...]


def place_rows(offsets, parts):
    rows, width = parts[0].shape
    return pl.pallas_call(
        place_kernel,
        name="place_rows",
        grid_spec=pltpu.PrefetchScalarGridSpec(
            num_scalar_prefetch=1,
            grid=(1,),
            in_specs=[whole(p.shape) for p in parts],
            out_specs=whole((rows * len(parts), width)),
        ),
        out_shape=jax.ShapeDtypeStruct((rows * len(parts), width), parts[0].dtype),
        compiler_params=pltpu.CompilerParams(vmem_limit_bytes=VMEM_LIMIT),
    )(offsets, *parts)


def rank_kernel(first, route_rows, priority_rows, route_columns, priority_columns, out, *, experts):
    rows = route_rows.shape[2]
    never = rows * TOPK
    for e in range(experts):
        expert = first[0] + e
        along = jnp.min(
            jnp.where(route_rows[0] == expert, priority_rows[0], never), axis=0, keepdims=True
        )
        down = jnp.min(
            jnp.where(route_columns[0] == expert, priority_columns[0], never), axis=1, keepdims=True
        )
        count = jnp.zeros((8, rows), i32)
        for begin in range(0, rows, 8):
            count += (down[begin : begin + 8] < along).astype(i32)
        rank = jnp.sum(count, axis=0, keepdims=True)
        out[0, e : e + 1, :] = jnp.where((along < never) & (rank < CAP), rank, -1)
    if out.shape[1] > experts:
        out[0, experts:, :] = jnp.full((out.shape[1] - experts, rows), -1, i32)


def slot_ranks(first, routes, priority, experts):
    groups, rows, _ = routes.shape
    tall = pl.BlockSpec((1, rows, TOPK), lambda g, *_: (g, 0, 0))
    flat = pl.BlockSpec((1, TOPK, rows), lambda g, *_: (g, 0, 0))
    padded = -(-experts // 8) * 8
    return pl.pallas_call(
        functools.partial(rank_kernel, experts=experts),
        name="slot_ranks",
        grid_spec=pltpu.PrefetchScalarGridSpec(
            num_scalar_prefetch=1,
            grid=(groups,),
            in_specs=[flat, flat, tall, tall],
            out_specs=pl.BlockSpec((1, padded, rows), lambda g, *_: (g, 0, 0)),
        ),
        out_shape=jax.ShapeDtypeStruct((groups, padded, rows), i32),
        compiler_params=pltpu.CompilerParams(vmem_limit_bytes=VMEM_LIMIT),
    )(
        first.reshape(1),
        routes.transpose(0, 2, 1),
        priority.transpose(0, 2, 1),
        routes,
        priority,
    )


def expert_kernel(offsets, first, ranks, *rest, parts, groups):
    gates, rest = rest[:groups], rest[groups:]
    tokens, rest = rest[:groups], rest[groups:]
    grads, rest = rest[:groups], rest[groups:]
    weights = rest[:parts]
    weighted_out, token_grad, inputs, slot_grads, hidden, pair_grads, matrices = rest[parts:]
    rows = tokens[0].shape[0]
    e = pl.program_id(0)
    for n, part in enumerate(weights):
        count = part.shape[2]
        for m in range(3):
            matrices[m, pl.ds(pl.multiple_of(offsets[n], count), count), :] = part[m, 0]
    slot = lax.broadcasted_iota(i32, (SLOTS, rows), 0)
    for g in range(groups):
        at = slice(g * SLOTS, (g + 1) * SLOTS)
        inside = slot == ranks[g, pl.ds(e, 1), :]
        pick = inside.astype(bf16)
        gate = gates[g][pl.ds(first[0] + e, 1), :]
        weight = jnp.sum(jnp.where(inside, gate, 0.0), axis=1, keepdims=True)
        picked = dot(pick, tokens[g][...]).astype(bf16)
        inputs[0, at, :] = picked
        gate_pre = dot(picked, matrices[0])
        up_pre = dot(picked, matrices[1])
        sigma = jax.nn.sigmoid(gate_pre)
        silu = gate_pre * sigma
        active = (silu * up_pre).astype(bf16)
        out = dot_dims(active, matrices[2], 1, 1)
        weighted_out[g, 0] = (out * weight).astype(bf16)
        upstream = dot(pick, grads[g][...])
        pair = jnp.sum(upstream * out, axis=1, keepdims=True)
        pair_grads[g, pl.ds(e, 1), :] = jnp.sum(jnp.where(inside, pair, 0.0), axis=0, keepdims=True)
        slot_grad = (weight * upstream).astype(bf16)
        slot_grads[0, at, :] = slot_grad
        act_grad = dot(slot_grad, matrices[2])
        gate_grad = (act_grad * up_pre * sigma * (1.0 + gate_pre * (1.0 - sigma))).astype(bf16)
        up_grad = (act_grad * silu).astype(bf16)
        hidden[0, 0, at, :] = gate_grad
        hidden[0, 1, at, :] = up_grad
        hidden[0, 2, at, :] = active
        token_grad[g, 0] = (
            dot_dims(gate_grad, matrices[0], 1, 1) + dot_dims(up_grad, matrices[1], 1, 1)
        ).astype(bf16)


def run_experts(offsets, first, ranks, gates, tokens, grads, weight_parts):
    groups = len(tokens)
    rows = tokens[0].shape[0]
    _, experts, part_rows, _ = weight_parts[0].shape
    parts = len(weight_parts)
    slots = groups * SLOTS
    by_group = pl.BlockSpec((groups, 1, SLOTS, D), lambda e, *_: (0, e, 0, 0))
    stash = pl.BlockSpec((1, slots, D), lambda e, *_: (e, 0, 0))
    return pl.pallas_call(
        functools.partial(expert_kernel, parts=parts, groups=groups),
        name="experts",
        grid_spec=pltpu.PrefetchScalarGridSpec(
            num_scalar_prefetch=2,
            grid=(experts,),
            in_specs=[whole(ranks.shape)]
            + [whole((EXPERTS, rows)) for _ in range(groups)]
            + [whole((rows, D)) for _ in range(2 * groups)]
            + [pl.BlockSpec((3, 1, part_rows, H), lambda e, *_: (0, e, 0, 0)) for _ in weight_parts],
            out_specs=[
                by_group,
                by_group,
                stash,
                stash,
                pl.BlockSpec((1, 3, slots, H), lambda e, *_: (e, 0, 0, 0)),
                whole(ranks.shape),
            ],
            scratch_shapes=[pltpu.VMEM((3, D, H), bf16)],
        ),
        out_shape=[
            jax.ShapeDtypeStruct((groups, experts, SLOTS, D), bf16),
            jax.ShapeDtypeStruct((groups, experts, SLOTS, D), bf16),
            jax.ShapeDtypeStruct((experts, slots, D), bf16),
            jax.ShapeDtypeStruct((experts, slots, D), bf16),
            jax.ShapeDtypeStruct((experts, 3, slots, H), bf16),
            jax.ShapeDtypeStruct(ranks.shape, f32),
        ],
        compiler_params=pltpu.CompilerParams(
            dimension_semantics=("arbitrary",), vmem_limit_bytes=VMEM_LIMIT
        ),
    )(
        offsets,
        first.reshape(1),
        ranks,
        *gates,
        *tokens,
        *grads,
        *weight_parts,
    )


def expert_grad_kernel(offsets, inputs, slot_grads, hidden, *rest, pieces):
    outs, total = rest[:-1], rest[-1]
    for m in range(3):
        left = inputs if m < 2 else slot_grads
        total[...] = dot_dims(left[0], hidden[0, m], 0, 0)
        for (n, begin), out in zip(pieces, outs):
            if begin <= m < begin + out.shape[0]:
                count = out.shape[2]
                at = pl.ds(pl.multiple_of(offsets[n], count), count)
                out[m - begin, 0] = total[at, :].astype(bf16)


def expert_grads(offsets, inputs, slot_grads, hidden, parts, cut_parts, part_rows):
    experts, slots, _ = inputs.shape
    stash = pl.BlockSpec((1, slots, D), lambda e, *_: (e, 0, 0))
    pieces = []
    for n in range(parts):
        pieces += [(n, 0, 1), (n, 1, 2)] if n in cut_parts else [(n, 0, 3)]
    outs = pl.pallas_call(
        functools.partial(expert_grad_kernel, pieces=[(n, begin) for n, begin, _ in pieces]),
        name="expert_grads",
        grid_spec=pltpu.PrefetchScalarGridSpec(
            num_scalar_prefetch=1,
            grid=(experts,),
            in_specs=[stash, stash, pl.BlockSpec((1, 3, slots, H), lambda e, *_: (e, 0, 0, 0))],
            out_specs=[
                pl.BlockSpec((held, 1, part_rows, H), lambda e, *_: (0, e, 0, 0))
                for _, _, held in pieces
            ],
            scratch_shapes=[pltpu.VMEM((D, H), f32)],
        ),
        out_shape=[
            jax.ShapeDtypeStruct((held, experts, part_rows, H), bf16) for _, _, held in pieces
        ],
        compiler_params=pltpu.CompilerParams(
            dimension_semantics=("arbitrary",), vmem_limit_bytes=VMEM_LIMIT
        ),
    )(offsets, inputs, slot_grads, hidden)
    found = {}
    for (n, _, _), out in zip(pieces, outs):
        found.setdefault(n, []).append(out)
    return [found[n] for n in range(parts)]


def combine_kernel(ranks, rows_in, out, *, experts, turned):
    count = ranks.shape[1]
    slot = lax.broadcasted_iota(i32, (count, SLOTS), 1)
    pick = jnp.concatenate(
        [(ranks[0, :, e : e + 1] == slot).astype(bf16) for e in range(experts)], axis=1
    )
    total = dot(pick, rows_in[0])
    out[...] = (total.T if turned else total).astype(bf16)


def combine(ranks, slot_rows, g, turned):
    groups, rows, columns = ranks.shape
    experts = slot_rows.shape[1]
    block = min(512, rows)
    return pl.pallas_call(
        functools.partial(combine_kernel, experts=experts, turned=turned),
        name="combine",
        grid=(rows // block,),
        in_specs=[
            pl.BlockSpec((1, block, columns), lambda i: (g, i, 0)),
            pl.BlockSpec(
                (1, experts * SLOTS, D), lambda i: (g, 0, 0), pipeline_mode=pl.Buffered(1)
            ),
        ],
        out_specs=(
            pl.BlockSpec((D, block), lambda i: (0, i))
            if turned
            else pl.BlockSpec((block, D), lambda i: (i, 0))
        ),
        out_shape=jax.ShapeDtypeStruct((D, rows) if turned else (rows, D), bf16),
        compiler_params=pltpu.CompilerParams(vmem_limit_bytes=VMEM_LIMIT),
    )(ranks, slot_rows.reshape(groups, experts * SLOTS, D))


def project_kernel(mixed, x, gain, matrix, middle, normed, inverse):
    branch = dot_dims(mixed[...].astype(f32).T.astype(bf16), matrix[:, :D], 1, 1)
    total = x[...].astype(f32) + branch_scale * branch
    scale = lax.rsqrt(jnp.mean(total * total, axis=1, keepdims=True) + epsilon)
    middle[...] = total
    inverse[...] = scale
    normed[...] = (total * scale * gain[...]).astype(bf16)


def project_out(mixed, x, gain, matrix):
    rows = x.shape[0]
    block = min(512, rows)
    tall = pl.BlockSpec((block, D), lambda i: (i, 0))
    return pl.pallas_call(
        project_kernel,
        name="project_out",
        grid=(rows // block,),
        in_specs=[
            pl.BlockSpec((D, block), lambda i: (0, i)),
            tall,
            whole(gain.shape),
            whole(matrix.shape),
        ],
        out_specs=[tall, tall, pl.BlockSpec((block, 1), lambda i: (i, 0))],
        out_shape=[
            jax.ShapeDtypeStruct((rows, D), f32),
            jax.ShapeDtypeStruct((rows, D), bf16),
            jax.ShapeDtypeStruct((rows, 1), f32),
        ],
        compiler_params=pltpu.CompilerParams(
            dimension_semantics=("arbitrary",), vmem_limit_bytes=VMEM_LIMIT
        ),
    )(mixed, x, gain, matrix)


def rows_of(columns):
    return columns[...].astype(f32).T.astype(bf16)


def matrix_grad_kernel(
    offsets, h_one, project_grad, branch_grad, mixed, h_two, logit_grad, project, *rest
):
    outs, gain, total = rest[:-2], rest[-2], rest[-1]
    wide = project_grad.shape[0]
    end = wide + mixed.shape[0]
    late = dot_dims(h_one[...], rows_of(project_grad), 0, 0)
    gain[...] = jnp.sum(late * project[...].astype(f32), axis=1, keepdims=True)
    total[:, :wide] = late
    total[:, wide:end] = dot_dims(branch_grad[...], rows_of(mixed), 0, 0)
    total[:, end:] = dot_dims(h_two[...], rows_of(logit_grad), 0, 0)
    for k, out in enumerate(outs):
        count, rows, _ = out.shape
        for p in range(count):
            at = pl.ds(pl.multiple_of(offsets[k * count + p], rows), rows)
            out[p] = total[at, :].astype(bf16)


def matrix_grads_of(offsets, share, arrays):
    width = sum(a.shape[0] for a in (arrays[1], arrays[3], arrays[5]))
    count = offsets.shape[0] // share
    out = jax.ShapeDtypeStruct((count, D // (count * share), width), bf16)
    return pl.pallas_call(
        matrix_grad_kernel,
        name="matrix_grads",
        grid_spec=pltpu.PrefetchScalarGridSpec(
            num_scalar_prefetch=1,
            grid=(1,),
            in_specs=[whole(a.shape) for a in arrays],
            out_specs=[whole(out.shape)] * share + [whole((D, 1))],
            scratch_shapes=[pltpu.VMEM((D, width), f32)],
        ),
        out_shape=[out] * share + [jax.ShapeDtypeStruct((D, 1), f32)],
        compiler_params=pltpu.CompilerParams(vmem_limit_bytes=VMEM_LIMIT),
    )(offsets, *arrays)


def rotate(values, cosine, sine):
    first = values[..., : HD // 2, :]
    second = values[..., HD // 2 :, :]
    return jnp.concatenate([first * cosine - second * sine, second * cosine + first * sine], axis=-2)


def rotate_back(values, cosine, sine):
    first = values[..., : HD // 2, :]
    second = values[..., HD // 2 :, :]
    return jnp.concatenate([first * cosine + second * sine, second * cosine - first * sine], axis=-2)


def tree_tables(ancestry, own_all, token_starts, query_block, key_block):
    groups, rows, _ = ancestry.shape
    tokens = own_all.shape[0]
    segments = jnp.arange(SEGS, dtype=i32)
    index = jnp.arange(tokens, dtype=i32)
    member = own_all[None, :] == segments[:, None]
    begin = jnp.min(jnp.where(member, index[None, :], tokens), axis=1)
    length = jnp.sum(member.astype(i32), axis=1)
    on_path = jnp.any(ancestry[:, :, :, None] == segments, axis=2)
    at = token_starts[:, None] + jnp.arange(rows, dtype=i32)[None, :]
    before = jnp.clip(at[:, :, None] - begin, 0, length)
    position = jnp.sum(jnp.where(on_path, before, 0), axis=2)
    bits = jnp.sum(on_path.astype(i32) << segments, axis=2)
    blocked = on_path.reshape(groups * rows // query_block, query_block, SEGS)
    path_any = jnp.any(blocked, axis=1)
    path_all = jnp.all(blocked, axis=1)
    keys = jnp.any(member.reshape(SEGS, tokens // key_block, key_block), axis=2).T
    some = jnp.any(path_any[:, None, :] & keys[None, :, :], axis=2)
    every = jnp.all(path_all[:, None, :] | ~keys[None, :, :], axis=2)
    query_start = at.reshape(-1, query_block)[:, 0]
    key_start = jnp.arange(tokens // key_block, dtype=i32) * key_block
    some &= key_start[None, :] < query_start[:, None] + query_block
    every &= key_start[None, :] + key_block <= query_start[:, None] + 1
    codes = jnp.where(some, jnp.where(every, 2, 1), 0).astype(i32)
    return position, bits, query_start, codes.reshape(-1)


def body(
    layer_input,
    cotangent,
    gain_attention,
    gain_mixture,
    w_query,
    w_key,
    w_value,
    w_out,
    w_router,
    w_gate,
    w_up,
    w_down,
    routes,
    priority,
    ancestry,
):
    chips, share, columns = lax.axis_size("chip"), lax.axis_size("core"), lax.axis_size("col")
    chip, core, column = lax.axis_index("chip"), lax.axis_index("core"), lax.axis_index("col")
    row_axes = ("chip", "core")
    rows, width = layer_input.shape
    weight_rows = w_query.shape[0]
    query_heads = w_query.shape[1] // HD
    key_heads = w_key.shape[1] // HD
    group = query_heads // key_heads
    own_heads = key_heads // share
    experts = w_gate.shape[1] // share
    tokens_all = rows * chips * share
    query_block = min(QUERY_BLOCK, rows)
    key_block = min(KEY_BLOCK, tokens_all)
    token_block = rows // columns

    places = [(chip ^ j) * share + (core ^ h) for j in range(chips) for h in range(share)]
    token_offsets = jnp.stack([p * rows for p in places]).astype(i32)
    feature_offsets = jnp.stack([p * weight_rows for p in places]).astype(i32)

    def groups_of(values):
        return [values] + ([swap_core(values)] if share == 2 else [])

    x_full = lax.all_gather(layer_input, "col", axis=1, tiled=True)
    index_groups = groups_of(jnp.concatenate([routes, priority, ancestry], axis=1))
    index_arrays = jnp.stack(index_groups)

    own_all = lax.all_gather(ancestry[:, 0], row_axes, axis=0, tiled=True)
    project_part = jnp.concatenate([w_query, w_key, w_value], axis=1)
    levels_here = range(len(chip_bits(chips)))
    project_parts = shared_level([project_part], 0)
    own_all, project_parts = tie(own_all, project_parts)
    for level in levels_here[1:]:
        project_parts = shared_level(project_parts, level)

    stacked = jnp.stack([m.transpose(1, 0, 2) for m in (w_gate, w_up, w_down)])
    stacked = stacked.reshape(3, share, experts, weight_rows, H).transpose(1, 0, 2, 3, 4)
    own_weights, other_weights = own_and_other(stacked, core, share)
    starts = [own_weights] + ([swap_core(other_weights)] if share == 2 else [])
    project_parts, starts, index_arrays = tie(project_parts, starts, index_arrays)
    all_routes = index_arrays[:, :, :TOPK]
    all_priority = index_arrays[:, :, TOPK : 2 * TOPK]
    all_ancestry = index_arrays[:, :, 2 * TOPK :]
    project = shared_rows(project_parts)
    rounds = gather_rounds(chips, share)
    weights_held = run_gather({(h, 0): v for h, v in enumerate(starts)}, rounds[:1])
    gains = column_rows(jnp.concatenate([gain_attention, gain_mixture])[None, :])
    gains = gains.reshape(columns, 2, width).transpose(1, 0, 2).reshape(2, D)

    token_starts = jnp.stack([(chip * share + (core ^ g)) * rows for g in range(share)]).astype(i32)
    position, path_bits, query_starts, codes = tree_tables(
        all_ancestry, own_all, token_starts, query_block, key_block
    )
    frequency = rope_base ** (-(jnp.arange(HD // 2, dtype=f32) * 2.0) / HD)
    angle = position.astype(f32)[:, None, :] * frequency[None, :, None]
    by_rows = Layout(major_to_minor=(0, 1, 2))
    cosine = with_layout_constraint(jnp.cos(angle), by_rows)
    sine = with_layout_constraint(jnp.sin(angle), by_rows)
    first_expert = (column * (experts * share) + core * experts).astype(i32)
    ranks = slot_ranks(first_expert, all_routes, all_priority, experts)
    rank_columns = ranks.transpose(0, 2, 1)
    expert_ids = jnp.arange(EXPERTS, dtype=i32)
    chosen = jnp.any(all_routes[:, None, :, :] == expert_ids[None, :, None, None], axis=3)

    key_bits = (jnp.int32(1) << own_all)[None, :]
    early_tables = (ranks, rank_columns, codes, path_bits, chosen, cosine, sine, project)
    x_full, w_out_here, early_tables = tie(x_full, w_out, early_tables)
    ranks, rank_columns, codes, path_bits, chosen, cosine, sine, project = early_tables
    out_columns = jnp.zeros((weight_rows, D), bf16)
    for c, part in [(column, w_out_here)] + column_shifts(lambda _: w_out_here):
        out_columns = lax.dynamic_update_slice_in_dim(out_columns, part, c * part.shape[1], 1)
    cotangent_here, out_columns = tie(cotangent, out_columns)
    cotangent_full = lax.all_gather(cotangent_here, "col", axis=1, tiled=True)
    tables = (ranks, rank_columns, cosine, sine, path_bits, codes, chosen, key_bits, project, gains)
    out_parts = [jnp.concatenate([out_columns, w_router], axis=1)]
    x_full, weights_held, tables = tie(x_full, weights_held, tables)
    ranks, rank_columns, cosine, sine, path_bits, codes, chosen, key_bits, project, gains = tables
    x_wide = x_full.astype(f32)
    inverse_one = lax.rsqrt(jnp.mean(x_wide * x_wide, axis=1, keepdims=True) + epsilon)
    h_one = (x_wide * inverse_one * gains[0][None, :]).astype(bf16)
    projected = dot_dims(project, h_one, 0, 1)
    query_width, key_width = query_heads * HD, key_heads * HD
    query = rotate(
        projected[:query_width].reshape(share, own_heads, group, HD, rows), cosine[0], sine[0]
    )
    query = (query.astype(bf16).astype(f32) * score_scale).astype(bf16)
    keys = rotate(
        projected[query_width : query_width + key_width].reshape(share, own_heads, HD, rows),
        cosine[0],
        sine[0],
    ).astype(bf16)
    values = projected[query_width + key_width :].reshape(share, own_heads, HD, rows).astype(bf16)
    sent = jnp.concatenate([keys[:, :, None], values[:, :, None], query], axis=2)
    own_sent, other_sent = own_and_other(sent, core, share)
    received = [own_sent] + ([swap_core(other_sent)] if share == 2 else [])
    query_groups = jnp.stack([r[:, 2:] for r in received], axis=1)
    pairs = [r[:, :2].reshape(own_heads, 2 * HD, rows) for r in received]
    for level in levels_here:
        out_parts = shared_level(out_parts, level)
    pairs, weights_held, out_parts = tie(pairs, weights_held, out_parts)
    kv_parts = gather_parts(pairs, chips)
    kv_parts, weights_held = tie(kv_parts, weights_held)
    weights_held = run_gather(weights_held, rounds[1 : len(rounds) - 1])

    attend_outs = [
        attend_forward(
            token_offsets,
            query_starts,
            codes,
            query_groups[head],
            path_bits,
            key_bits,
            [p[head] for p in kv_parts],
        )
        for head in range(own_heads)
    ]
    mixed_b = jnp.stack([o[1] for o in attend_outs])
    mixed_b, weights_held, cotangent_full, out_parts = tie(
        mixed_b, weights_held, cotangent_full, out_parts
    )
    out_router = shared_rows(out_parts)
    weights_held = run_gather(weights_held, rounds[len(rounds) - 1 :])
    mixed_other = swap_core(mixed_b[:, 1]) if share == 2 else None
    mixed = in_core_order(mixed_b[:, 0], mixed_other, core).reshape(query_width, rows)
    mixed_full = lax.all_gather(mixed, "col", axis=0, tiled=True)
    mixed_full, weights_held, out_router = tie(mixed_full, weights_held, out_router)
    mix_grads = groups_of((branch_scale * cotangent_full.astype(f32)).astype(bf16))
    x_middle, h_two, inverse_two = project_out(
        mixed_full, x_full, gains[1:2], out_router
    )
    full_router = out_router[:, D:]
    h_two_groups = groups_of(h_two)

    def gates_of(tokens, picks):
        logits = dot_dims(full_router, tokens, 0, 1)
        shown = jnp.where(picks, logits, masked_score)
        raised = jnp.where(picks, jnp.exp(logits - jnp.max(shown, axis=0, keepdims=True)), 0.0)
        return raised / jnp.sum(raised, axis=0, keepdims=True)

    gates = [gates_of(h_two_groups[g], chosen[g]) for g in range(share)]
    weighted_out, slot_token_grads, inputs, slot_grads, hidden, pair_rows = run_experts(
        feature_offsets,
        first_expert,
        ranks,
        gates,
        h_two_groups,
        mix_grads,
        listed(weights_held, chips),
    )

    def combine_groups(slot_rows, turned):
        if share == 1:
            return combine(rank_columns, slot_rows, 0, turned)
        received = swap_core(combine(rank_columns, slot_rows, 1, turned))
        own = combine(rank_columns, slot_rows, 0, turned)
        return (own.astype(f32) + received.astype(f32)).astype(bf16)

    token_sum = combine_groups(slot_token_grads, False)
    token_grads = lax.psum_scatter(token_sum, "col", scatter_dimension=0, tiled=True)
    pair_other = swap_core(pair_rows[1, :experts]) if share == 2 else None
    pair_columns = in_core_order(pair_rows[0, :experts], pair_other, core)
    pair_columns = pair_columns.reshape(share * experts, rows)
    pair_grad = column_rows(pair_columns)
    picked_grad = gates[0] * (pair_grad - jnp.sum(gates[0] * pair_grad, axis=0, keepdims=True))
    logit_grad = picked_grad.astype(bf16)
    mix_sum = combine_groups(weighted_out, True)

    levels = reduce_levels(chips, share)
    first = [[m for m in moves if m[1]] for moves in levels[0]]
    last = [[m for m in moves if not m[1]] for moves in levels[0]]
    sent = {(h, j ^ bit) for moves in first for h, j, bit in moves}
    last_sent = {(h, j ^ bit) for moves in last for h, j, bit in moves}
    parts = expert_grads(
        feature_offsets,
        inputs,
        slot_grads,
        hidden,
        chips * share,
        {j * share + h for h, j in sent | last_sent},
        weight_rows,
    )
    sums_held = {(h, j): parts[j * share + h] for j in range(chips) for h in range(share)}

    def take_piece(rounds_here, held):
        taken = {}
        for moves in rounds_here:
            taken.update(take(held, moves))
        return taken

    first_taken = take_piece(first, {k: sums_held[k][0] for k in sent})
    staying = [sums_held[h, 0][0] for h in range(share)]
    token_grads, staying, mix_sum, logit_grad, first_taken = tie(
        token_grads, staying, mix_sum, logit_grad, first_taken
    )
    token_grads = token_grads.astype(f32)
    second_taken = take_piece(first, {k: sums_held[k][1] for k in sent})

    token_start = column * token_block

    def own_tokens(array):
        return lax.dynamic_slice_in_dim(array, token_start, token_block, 0)

    h_two_grad = token_grads + dot_dims(
        lax.dynamic_slice_in_dim(logit_grad, token_start, token_block, 1), full_router, 0, 1
    )
    x_part, inverse_part = own_tokens(x_middle), own_tokens(inverse_two)
    scaled_two = h_two_grad * gains[1][None, :]
    inner_two = jnp.sum(scaled_two * x_part, axis=1, keepdims=True)
    x_middle_grad = (
        own_tokens(cotangent_full).astype(f32)
        + inverse_part * scaled_two
        - x_part * inverse_part**3 * inner_two / D
    )
    gain_mixture_part = jnp.sum(h_two_grad * x_part * inverse_part, axis=0)
    branch_part = (branch_scale * x_middle_grad).astype(bf16)
    mixed_parts = dot(branch_part, out_router[:, :D]).astype(bf16)
    mixed_parts = mixed_parts.reshape(token_block, columns, query_width).transpose(1, 0, 2)
    mixed_grad = lax.all_to_all(mixed_parts, "col", split_axis=0, concat_axis=0, tiled=True)
    mixed_grad, branch_part, mix_sum, second_taken = tie(
        mixed_grad, branch_part, mix_sum, second_taken
    )
    branch_grad = lax.all_gather(branch_part, "col", axis=0, tiled=True)
    sums_here = {}
    for k, part in first_taken.items():
        taken = jnp.concatenate([part, second_taken[k]])
        sums_here[k] = (sums_held[k][0].astype(f32) + taken.astype(f32)).astype(bf16)

    mixed_grad = mixed_grad.reshape(rows, query_width).T
    mixed_grad, sums_here = tie(mixed_grad, sums_here)
    own_grad, other_grad = own_and_other(
        mixed_grad.reshape(share, own_heads, group, HD, rows), core, share
    )
    arrived = [[part] for part in staying]
    for rounds_here in levels[1:]:
        passed = {}
        for moves in rounds_here:
            passed.update(take(sums_here, moves))
        for h in range(share):
            if (h, 0) in passed:
                arrived[h].append(passed.pop((h, 0)))
        sums_here = add_taken(sums_here, passed)
    last_begin = {k: sums_held[k][0] for k in last_sent}
    last_rest = {k: sums_held[k][1] for k in last_sent}
    last_rest, own_grad = tie(last_rest, own_grad)
    last_rest = take_piece(last, last_rest)
    grad_groups = jnp.stack(
        [own_grad] + ([swap_core(other_grad)] if share == 2 else []), axis=1
    )
    backward_outs = [
        attend_backward(
            token_offsets,
            query_starts,
            codes,
            query_groups[head],
            grad_groups[head],
            attend_outs[head][0],
            attend_outs[head][2],
            path_bits,
            key_bits,
            [p[head] for p in kv_parts],
        )
        for head in range(own_heads)
    ]
    mix_slice = lax.psum_scatter(mix_sum, "col", scatter_dimension=0, tiled=True).astype(f32).T
    feature_start = column * width
    x_middle_slice = lax.dynamic_slice_in_dim(x_middle, feature_start, width, 1)
    result = (x_middle_slice + branch_scale * mix_slice).astype(bf16)
    backward_outs, arrived, branch_later, last_rest = tie(
        backward_outs, arrived, branch_grad, last_rest
    )
    query_grad = jnp.stack([o[0] for o in backward_outs])
    query_grad = rotate_back(query_grad, cosine[None, :, None], sine[None, :, None]).astype(bf16)
    query_other = swap_core(query_grad[:, 1]) if share == 2 else None
    query_pre_grad = in_core_order(query_grad[:, 0], query_other, core).reshape(query_width, rows)
    kv_sums = reduce_parts(
        [jnp.stack([o[1][n] for o in backward_outs]) for n in range(chips * share)], chips, share
    )
    kv_other = swap_core(kv_sums[1]) if share == 2 else None
    kv_grad = in_core_order(kv_sums[0], kv_other, core).astype(f32)
    kv_grad, last_begin = tie(kv_grad, last_begin)
    last_begin = take_piece(last, last_begin)
    for h in range(share):
        for k in last_rest:
            if k[0] == h:
                arrived[h].append(jnp.concatenate([last_begin[k], last_rest[k]]))
    kv_grad = kv_grad.transpose(0, 1, 3, 2).reshape(key_heads, 2 * HD, rows)
    key_pre_grad = (
        rotate_back(kv_grad[:, :HD], cosine[0], sine[0]).astype(bf16).reshape(key_width, rows)
    )
    value_pre_grad = kv_grad[:, HD:].astype(bf16).reshape(key_width, rows)
    project_grad = jnp.concatenate([query_pre_grad, key_pre_grad, value_pre_grad], axis=0)

    (project_grad,) = tie(project_grad)
    h_one_part = dot(project, project_grad).astype(bf16)
    h_one_part, project_grad = tie(h_one_part, project_grad)
    h_one_grad = lax.psum_scatter(h_one_part, "col", scatter_dimension=0, tiled=True)
    inner_one = column_sum(jnp.sum(project_grad.astype(f32) * projected, axis=0))[:, None]
    sums = [functools.reduce(jnp.add, [p.astype(f32) for p in own]).astype(bf16) for own in arrived]
    small_places = shared_places(chips, share, core)
    if share == 2:
        small_places = small_places + shared_places(chips, share, 1 - core)
    *small_parts, gain_column = matrix_grads_of(
        jnp.stack([p * weight_rows for p in small_places]).astype(i32),
        share,
        (h_one, project_grad, branch_later, mixed, h_two, logit_grad, project),
    )
    gain_attention_part = gain_column[:, 0] / gains[0]
    gain_parts = jnp.stack([gain_attention_part, gain_mixture_part])

    def own_features(array, c):
        return lax.dynamic_slice_in_dim(array, c * width, width, 1)

    gain_sums = own_features(gain_parts, column)
    for _, other in column_shifts(lambda c: own_features(gain_parts, c)):
        gain_sums = gain_sums + other
    small_parts, sums = tie(small_parts, sums)
    returned = swap_core(sums[1]) if share == 2 else None
    small_sum = shared_reduce(small_parts[0], small_parts[1] if share == 2 else None)
    gain_sums = row_sum(gain_sums)
    matrix_grads = [
        in_core_order(sums[0][m], None if returned is None else returned[m], core)
        .astype(f32)
        .reshape(share * experts, weight_rows, H)
        .transpose(1, 0, 2)
        for m in range(3)
    ]
    h_one_grad, matrix_grads, small_sum, gain_sums, inner_one = tie(
        h_one_grad, matrix_grads, small_sum, gain_sums, inner_one
    )
    x_slice = layer_input.astype(f32)
    middle_slice = lax.dynamic_slice_in_dim(branch_grad, feature_start, width, 1).astype(f32)
    input_grad = (
        middle_slice * (1.0 / branch_scale)
        + inverse_one * h_one_grad.astype(f32).T * gain_attention[None, :]
        - x_slice * inverse_one**2 * inner_one / D
    )
    kv_width = query_width + 2 * key_width
    return (
        result,
        input_grad,
        gain_sums[0],
        gain_sums[1],
        small_sum[:, :query_width],
        small_sum[:, query_width : query_width + key_width],
        small_sum[:, query_width + key_width : kv_width],
        small_sum[:, kv_width : kv_width + query_width],
        small_sum[:, kv_width + query_width :],
        *matrix_grads,
    )


def solution(mesh):
    rows, columns = mesh.shape["row"], mesh.shape["col"]
    halves = rows % 2 == 0 and EXPERTS // columns % 2 == 0 and KVH // columns % 2 == 0
    share = 2 if halves else 1
    split = Mesh(mesh.devices.reshape(rows // share, share, columns), ("chip", "core", "col"))
    row = ("chip", "core")
    return jax.shard_map(
        body,
        mesh=split,
        in_specs=(
            P(row, "col"),
            P(row, "col"),
            P("col"),
            P("col"),
            P(row, "col"),
            P(row, "col"),
            P(row, "col"),
            P(row, "col"),
            P(row, None),
            P(row, "col", None),
            P(row, "col", None),
            P(row, "col", None),
            P(row, None),
            P(row, None),
            P(row, None),
        ),
        out_specs=(
            P(row, "col"),
            P(row, "col"),
            P("col"),
            P("col"),
            P(row, "col"),
            P(row, "col"),
            P(row, "col"),
            P(row, "col"),
            P(row, None),
            P(row, "col", None),
            P(row, "col", None),
            P(row, "col", None),
        ),
        check_vma=False,
    )
```
